32 devices in a mesh: dp: 8 (over z, x), tensor: 4 (over y, core).
Axes of the slice: x: 2, y: 2, z: 4, core: 2. Of those that a mesh axis runs over, the one named last changes fastest.
Arguments:
- block_input: float32 [4096, 1024], P(('dp', 'tensor')), may hold values from -6 to 6
- seq_begin: int32 [4096], P('dp'), may hold values from 0 to 511, as said below
- group_fill: int32 [8], P('dp'), may hold values from 256 to 512, as said below
- attention_norm_gain: float32 [1024], P(('dp', 'tensor')), may hold values from 0.1 to 1.9
- attention_norm_bias: float32 [1024], P(('dp', 'tensor')), may hold values from -3 to 3
- qkv_weight: bfloat16 [1024, 3072], P('dp', 'tensor'), may hold values from -0.1875 to 0.1875
- qv_bias: bfloat16 [2048], P(('tensor', 'dp')), may hold values from -3 to 3
- dense_weight: bfloat16 [1024, 1024], P(('tensor', 'dp')), may hold values from -0.5 to 0.5
- dense_bias: float32 [1024], P(('dp', 'tensor')), may hold values from -3 to 3
- feedforward_norm_gain: float32 [1024], P(('dp', 'tensor')), may hold values from 0.1 to 1.9
- feedforward_norm_bias: float32 [1024], P(('dp', 'tensor')), may hold values from -3 to 3
- up_weight: bfloat16 [1024, 4096], P('dp', 'tensor'), may hold values from -0.1875 to 0.1875
- up_bias: bfloat16 [4096], P(('tensor', 'dp')), may hold values from -3 to 3
- down_weight: bfloat16 [4096, 1024], P(('tensor', 'dp')), may hold values from -0.09375 to 0.09375
- down_bias: float32 [1024], P(('dp', 'tensor')), may hold values from -3 to 3
- out_grad: float32 [4096, 1024], P(('dp', 'tensor')), may hold values from -6 to 6
Outputs:
- block_out: float32 [4096, 1024], P(('dp', 'tensor'))
- block_input_gradient: float32 [4096, 1024], P(('dp', 'tensor'))
- attention_gain_gradient: float32 [1024], P(('dp', 'tensor'))
- attn_bias_grad: float32 [1024], P(('dp', 'tensor'))
- qkv_weight_grad: float32 [1024, 3072], P('dp', 'tensor')
- qv_bias_grad: float32 [2048], P(('tensor', 'dp'))
- dense_weight_grad: float32 [1024, 1024], P(('tensor', 'dp'))
- dense_bias_grad: float32 [1024], P(('dp', 'tensor'))
- feedforward_gain_gradient: float32 [1024], P(('dp', 'tensor'))
- mlp_bias_grad: float32 [1024], P(('dp', 'tensor'))
- up_weight_grad: float32 [1024, 4096], P('dp', 'tensor')
- up_bias_grad: float32 [4096], P(('tensor', 'dp'))
- down_weight_grad: float32 [4096, 1024], P(('tensor', 'dp'))
- down_bias_grad: float32 [1024], P(('dp', 'tensor'))
The draws below stay inside these ranges and needn't reach their ends.
Inputs may be any that keep to these rules, and one draw needn't show every extreme that they name: For row i of a group, seq_begin is the row of the same group where the sequence of row i starts, at most i; rows at or beyond the group's fill have seq_begin equal to their own row. One group in each draw holds a single sequence of 512 rows. `group_fill`: one group in each draw is full.
All inputs are finite; a program needn't handle non-finite values.
Results may differ from the reference program's by a relative error of at most 0.018.
Values may be sent and summed in bfloat16 or wider, within the bound.
A program may use at most 128 MiB of HBM per device.

```python
import math
import jax
import jax.numpy as jnp
from jax import lax

D = 1024
HEADS = 16
FF = 4096
TOK_GRP = 512
TOKENS = 4096


def layout_tables(key):
    group_count = TOKENS // TOK_GRP
    fill_key = jax.random.fold_in(key, 11)
    full_key = jax.random.fold_in(key, 12)
    cut_key = jax.random.fold_in(key, 13)
    groups_idx = jnp.arange(group_count, dtype=jnp.int32)
    fills = jax.random.randint(fill_key, (group_count,), TOK_GRP // 2, TOK_GRP, dtype=jnp.int32)
    full_group = jax.random.randint(full_key, (), 0, group_count, dtype=jnp.int32)
    fills = jnp.where(groups_idx == full_group, TOK_GRP, fills).astype(jnp.int32)
    row_idx = jnp.arange(TOK_GRP, dtype=jnp.int32)[None, :]
    cuts = jax.random.randint(cut_key, (group_count, TOK_GRP), 0, TOK_GRP, dtype=jnp.int32) < 3
    cuts = cuts & (groups_idx[:, None] != full_group)
    marks = jnp.where(cuts | (row_idx == 0), row_idx, 0)
    begins = lax.cummax(marks, axis=1)
    begins = jnp.where(row_idx < fills[:, None], begins, row_idx)
    return (begins.reshape(-1).astype(jnp.int32), fills)


def draw_seq_begin(key, part):
    return layout_tables(key)[0]


def draw_group_fill(key, part):
    return layout_tables(key)[1]


def block_scale(own_key, extent, split, smallest, largest):
    loudness = 1.0
    for dim, shards_of in split:
        draws = jax.random.uniform(jax.random.fold_in(jax.random.fold_in(own_key, 6), dim), (shards_of,), jnp.float32, smallest / len(split), largest / len(split))
        loudness = loudness * jnp.repeat(jnp.exp(draws), extent[dim] // shards_of).reshape((-1,) + (1,) * (len(extent) - 1 - dim))
    return loudness


def scatter_about(own_key, shape, width, bound, shards=(), held_as=jnp.bfloat16):
    array = jax.random.normal(own_key, shape, jnp.float32) * width
    if len(shards) > 0:
        array = block_scale(own_key, shape, shards, -0.22, 0.18) * array
    return jnp.clip(array, min=-bound, max=bound).astype(held_as)


def setup_inputs(seed: int = 0) -> dict:
    splits = jax.random.split(jax.random.key(seed), 17)
    return {
        "block_input": scatter_about(splits[0], (TOKENS, D), 1.0, 6.0, ((0, 32),), jnp.float32),
        "seq_begin": draw_seq_begin(jax.random.fold_in(splits[16], 71), 0),
        "group_fill": draw_group_fill(jax.random.fold_in(splits[16], 71), 0),
        "attention_norm_gain": jnp.clip(1.0 + 0.18 * jax.random.normal(splits[3], (D,), jnp.float32), 0.1, 1.9),
        "attention_norm_bias": scatter_about(splits[4], (D,), 0.5, 3.0, ((0, 32),), jnp.float32),
        "qkv_weight": scatter_about(splits[5], (D, 3 * D), D ** -0.5, 0.1875, ((0, 8), (1, 4))),
        "qv_bias": scatter_about(splits[6], (2 * D,), 0.5, 3.0, ((0, 32),)),
        "dense_weight": scatter_about(splits[7], (D, D), (D // 8) ** -0.5, 0.5, ((0, 32),)),
        "dense_bias": scatter_about(splits[8], (D,), 0.5, 3.0, ((0, 32),), jnp.float32),
        "feedforward_norm_gain": jnp.clip(1.0 + 0.18 * jax.random.normal(splits[9], (D,), jnp.float32), 0.1, 1.9),
        "feedforward_norm_bias": scatter_about(splits[10], (D,), 0.5, 3.0, ((0, 32),), jnp.float32),
        "up_weight": scatter_about(splits[11], (D, FF), D ** -0.5, 0.1875, ((0, 8), (1, 4))),
        "up_bias": scatter_about(splits[12], (FF,), 0.5, 3.0, ((0, 32),)),
        "down_weight": scatter_about(splits[13], (FF, D), FF ** -0.5, 0.09375, ((0, 32),)),
        "down_bias": scatter_about(splits[14], (D,), 0.5, 3.0, ((0, 32),), jnp.float32),
        "out_grad": scatter_about(splits[15], (TOKENS, D), 1.0, 6.0, ((0, 32),), jnp.float32),
    }


EPSILON = 1e-05
MASKED_SCORE = -1e+30

def layer_normalize(hidden_row_count, norm_gain, norm_shift):
    row_mean = lax.optimization_barrier(jnp.mean(hidden_row_count, axis=-1, keepdims=True))
    centred = hidden_row_count - row_mean
    inv_std = lax.rsqrt(lax.optimization_barrier(jnp.mean(centred * centred, axis=-1, keepdims=True)) + EPSILON)
    normed = centred * inv_std
    return (normed * norm_gain + norm_shift, normed, inv_std)

def norm_backward_step(upstream, norm_gain, normed, inv_std):
    scaled = upstream * norm_gain
    return inv_std * (scaled - lax.optimization_barrier(jnp.mean(scaled, axis=-1, keepdims=True)) - normed * lax.optimization_barrier(jnp.mean(scaled * normed, axis=-1, keepdims=True)))

def gelu_tanh(values_in):
    return jax.nn.gelu(values_in, approximate=True)

def head_slopes(first_head, head_count):
    heads_idx = first_head + jnp.arange(head_count).astype(jnp.float32)
    return jnp.exp2(-8.0 * (heads_idx + 1.0) / HEADS)

def masked_scores(query_blk, key_all, slopes, row_start, begin_blk):
    row_count = query_blk.shape[0]
    key_count = key_all.shape[0]
    query_pos = row_start + jnp.arange(row_count, dtype=jnp.int32)
    key_pos = jnp.arange(key_count, dtype=jnp.int32)
    score_scale = 1.0 / math.sqrt(query_blk.shape[-1])
    logits = jnp.einsum('qhd,khd->hqk', query_blk.astype(jnp.float32), key_all.astype(jnp.float32)) * score_scale
    offset = (key_pos[None, :] - query_pos[:, None]).astype(jnp.float32)
    logits = logits + slopes[:, None, None] * offset[None, :, :]
    allowed = (key_pos[None, :] >= begin_blk[:, None]) & (key_pos[None, :] <= query_pos[:, None])
    return jnp.where(allowed[None, :, :], logits, MASKED_SCORE)

def attention_forward(queries, key_all, values, slopes, begins):
    total_rows = queries.shape[0]
    block_rows = min(512, total_rows)
    pieces = []
    totals = []
    for first_row in range(0, total_rows, block_rows):
        last_row = first_row + block_rows
        scores = masked_scores(queries[first_row:last_row], key_all, slopes, first_row, begins[first_row:last_row])
        row_top = lax.optimization_barrier(jnp.max(scores, axis=-1))
        log_total = row_top + jnp.log(lax.optimization_barrier(jnp.sum(jnp.exp(scores - row_top[..., None]), axis=-1)))
        attn_probs = jnp.exp(scores - log_total[..., None]).astype(jnp.bfloat16)
        pieces.append(jnp.einsum('hqk,khd->qhd', attn_probs.astype(jnp.float32), values.astype(jnp.float32)).astype(jnp.bfloat16))
        totals.append(log_total)
    return (jnp.concatenate(pieces, axis=0), jnp.concatenate(totals, axis=1))

def attention_backward(queries, key_all, values, slopes, begins, log_total, context, context_grad):
    total_rows = queries.shape[0]
    block_rows = min(512, total_rows)
    score_scale = 1.0 / math.sqrt(queries.shape[-1])
    key_grad = jnp.zeros(key_all.shape, jnp.float32)
    value_grad = jnp.zeros(values.shape, jnp.float32)
    query_parts = []
    for first_row in range(0, total_rows, block_rows):
        last_row = first_row + block_rows
        query_blk = queries[first_row:last_row]
        grad_blk = context_grad[first_row:last_row].astype(jnp.float32)
        scores = masked_scores(query_blk, key_all, slopes, first_row, begins[first_row:last_row])
        attn_probs = jnp.exp(scores - log_total[:, first_row:last_row, None])
        row_delta = lax.optimization_barrier(jnp.sum(grad_blk * context[first_row:last_row].astype(jnp.float32), axis=-1))
        probs_low = attn_probs.astype(jnp.bfloat16).astype(jnp.float32)
        value_grad = value_grad + jnp.einsum('hqk,qhd->khd', probs_low, grad_blk)
        prob_grad = jnp.einsum('qhd,khd->hqk', grad_blk, values.astype(jnp.float32))
        score_grad = (attn_probs * (prob_grad - jnp.transpose(row_delta)[:, :, None])).astype(jnp.bfloat16).astype(jnp.float32)
        query_parts.append(jnp.einsum('hqk,khd->qhd', score_grad, key_all.astype(jnp.float32)) * score_scale)
        key_grad = key_grad + jnp.einsum('hqk,qhd->khd', score_grad, query_blk.astype(jnp.float32)) * score_scale
    query_grad = jnp.concatenate(query_parts, axis=0)
    return jnp.stack([query_grad, key_grad, value_grad], axis=2).astype(jnp.bfloat16)

def group_pass(weights, slopes, hidden_row_count, grad_rows, begins, fill_value):
    attention_norm_gain, attention_norm_bias, qkv_weight, qv_bias, dense_weight, dense_bias, feedforward_norm_gain, feedforward_norm_bias, up_weight, up_bias, down_weight, down_bias = weights
    head_dim = D // HEADS
    group_rows = hidden_row_count.shape[0]
    normalized_input, first_standardized, first_inverse_deviation = layer_normalize(hidden_row_count, attention_norm_gain, attention_norm_bias)
    attn_in = normalized_input.astype(jnp.bfloat16)
    projected = jnp.dot(attn_in, qkv_weight, preferred_element_type=jnp.float32).reshape(group_rows, HEADS, 3, head_dim)
    bias_pair = qv_bias.astype(jnp.float32).reshape(HEADS, 2, head_dim)
    bias_full = jnp.stack([bias_pair[:, 0], jnp.zeros_like(bias_pair[:, 0]), bias_pair[:, 1]], axis=1)
    qkv_low = (projected + bias_full).astype(jnp.bfloat16)
    queries = qkv_low[:, :, 0]
    key_all = qkv_low[:, :, 1]
    values = qkv_low[:, :, 2]
    context, log_total = attention_forward(queries, key_all, values, slopes, begins)
    context_flat = context.reshape(group_rows, D)
    residual_middle = hidden_row_count + jnp.dot(context_flat, dense_weight, preferred_element_type=jnp.float32) + dense_bias
    normalized_middle, second_standardized, second_inverse_deviation = layer_normalize(residual_middle, feedforward_norm_gain, feedforward_norm_bias)
    mlp_in = normalized_middle.astype(jnp.bfloat16)
    pre_act = jnp.dot(mlp_in, up_weight, preferred_element_type=jnp.float32) + up_bias.astype(jnp.float32)
    act_value, act_back = jax.vjp(gelu_tanh, pre_act)
    activated = act_value.astype(jnp.bfloat16)
    block_out = residual_middle + jnp.dot(activated, down_weight, preferred_element_type=jnp.float32) + down_bias
    live_rows = (jnp.arange(group_rows) < fill_value).astype(jnp.float32)[:, None]
    running_gradient = grad_rows * live_rows
    down_bias_grad = lax.optimization_barrier(jnp.sum(running_gradient, axis=0))
    out_low = running_gradient.astype(jnp.bfloat16)
    down_weight_grad = jnp.dot(activated.T, out_low, preferred_element_type=jnp.float32)
    act_grad = jnp.dot(out_low, down_weight.T, preferred_element_type=jnp.float32)
    pre_grad = act_back(act_grad)[0].astype(jnp.bfloat16)
    up_weight_grad = jnp.dot(mlp_in.T, pre_grad, preferred_element_type=jnp.float32)
    up_bias_grad = lax.optimization_barrier(jnp.sum(pre_grad.astype(jnp.float32), axis=0))
    feedforward_input_gradient = jnp.dot(pre_grad, up_weight.T, preferred_element_type=jnp.float32)
    feedforward_gain_gradient = lax.optimization_barrier(jnp.sum(feedforward_input_gradient * second_standardized, axis=0))
    mlp_bias_grad = lax.optimization_barrier(jnp.sum(feedforward_input_gradient, axis=0))
    residual_middle_gradient = running_gradient + norm_backward_step(feedforward_input_gradient, feedforward_norm_gain, second_standardized, second_inverse_deviation)
    dense_bias_grad = lax.optimization_barrier(jnp.sum(residual_middle_gradient, axis=0))
    middle_low = residual_middle_gradient.astype(jnp.bfloat16)
    dense_weight_grad = jnp.dot(context_flat.T, middle_low, preferred_element_type=jnp.float32)
    context_grad = jnp.dot(middle_low, dense_weight.T, preferred_element_type=jnp.float32).astype(jnp.bfloat16).reshape(group_rows, HEADS, head_dim)
    qkv_grad = attention_backward(queries, key_all, values, slopes, begins, log_total, context, context_grad)
    qkv_grad_flat = qkv_grad.reshape(group_rows, 3 * D)
    qkv_weight_grad = jnp.dot(attn_in.T, qkv_grad_flat, preferred_element_type=jnp.float32)
    summed = lax.optimization_barrier(jnp.sum(qkv_grad.astype(jnp.float32), axis=0))
    qv_bias_grad = jnp.stack([summed[:, 0], summed[:, 2]], axis=1).reshape(2 * D)
    attention_input_gradient = jnp.dot(qkv_grad_flat, qkv_weight.T, preferred_element_type=jnp.float32)
    attention_gain_gradient = lax.optimization_barrier(jnp.sum(attention_input_gradient * first_standardized, axis=0))
    attn_bias_grad = lax.optimization_barrier(jnp.sum(attention_input_gradient, axis=0))
    block_input_gradient = residual_middle_gradient + norm_backward_step(attention_input_gradient, attention_norm_gain, first_standardized, first_inverse_deviation)
    grads = (attention_gain_gradient, attn_bias_grad, qkv_weight_grad, qv_bias_grad, dense_weight_grad, dense_bias_grad, feedforward_gain_gradient, mlp_bias_grad, up_weight_grad, up_bias_grad, down_weight_grad, down_bias_grad)
    return ((block_out, block_input_gradient), grads)

def reference(block_input, seq_begin, group_fill, attention_norm_gain, attention_norm_bias, qkv_weight, qv_bias, dense_weight, dense_bias, feedforward_norm_gain, feedforward_norm_bias, up_weight, up_bias, down_weight, down_bias, out_grad):
    group_count = TOKENS // TOK_GRP
    slopes = head_slopes(0.0, HEADS)
    weights = (attention_norm_gain, attention_norm_bias, qkv_weight, qv_bias, dense_weight, dense_bias, feedforward_norm_gain, feedforward_norm_bias, up_weight, up_bias, down_weight, down_bias)
    initial = tuple((jnp.zeros(weight_arr.shape, jnp.float32) for weight_arr in weights))

    def one_group(carry, inputs):
        hidden_row_count, grad_rows, begins, fill_value = inputs
        outputs, grads = group_pass(weights, slopes, hidden_row_count, grad_rows, begins, fill_value)
        return (tuple((total_val + new_val for total_val, new_val in zip(carry, grads))), outputs)
    inputs = (block_input.reshape(group_count, TOK_GRP, D), out_grad.reshape(group_count, TOK_GRP, D), seq_begin.reshape(group_count, TOK_GRP), group_fill)
    totals, outputs = lax.scan(one_group, initial, inputs)
    block_out = outputs[0].reshape(TOKENS, D)
    block_input_gradient = outputs[1].reshape(TOKENS, D)
    return (block_out, block_input_gradient, totals[0], totals[1], totals[2], totals[3], totals[4], totals[5], totals[6], totals[7], totals[8], totals[9], totals[10], totals[11])
```

```python
import functools
import math

import jax
import jax.numpy as jnp
from jax import lax
from jax.experimental import pallas as pl
from jax.experimental.pallas import tpu as pltpu
from jax.sharding import PartitionSpec as P

D = 1024
HEADS = 16
HEAD = D // HEADS
TENSOR = 4
EPSILON = 1e-05
MASKED_SCORE = -1e30
MESH = pl.DeviceIdType.MESH
VECTOR_ROWS = 8
LANES = 128
BF16 = jnp.bfloat16
F32 = jnp.float32
DMA = pltpu.SemaphoreType.DMA


def dot_nn(a, b):
    return lax.dot_general(a, b, (((1,), (0,)), ((), ())), preferred_element_type=F32)


def dot_nt(a, b):
    return lax.dot_general(a, b, (((1,), (1,)), ((), ())), preferred_element_type=F32)


def dot_tn(a, b):
    return lax.dot_general(a, b, (((0,), (0,)), ((), ())), preferred_element_type=F32)


def normalize(hidden):
    centred = hidden - jnp.mean(hidden, axis=-1, keepdims=True)
    inverse = lax.rsqrt(jnp.mean(centred * centred, axis=-1, keepdims=True) + EPSILON)
    return centred * inverse, inverse


def norm_backward(upstream, gain, normed, inverse):
    scaled = upstream * gain
    return inverse * (
        scaled
        - jnp.mean(scaled, axis=-1, keepdims=True)
        - normed * jnp.mean(scaled * normed, axis=-1, keepdims=True)
    )


def column_sum(value):
    return jnp.sum(value, axis=0, keepdims=True)


def put_rows(base, values):
    row = lax.broadcasted_iota(jnp.int32, base.shape, 0)
    for index, value in values:
        base = jnp.where(row == index, value, base)
    return base


def place():
    return lax.axis_index("dp"), lax.axis_index("tensor")


def tensor_peers(t):
    h, c = t // 2, t % 2
    core = h * 2 + (1 - c)
    across = (1 - h) * 2 + c
    diagonal = (1 - h) * 2 + (1 - c)
    return core, across, diagonal


def block(start, rows):
    return pl.ds(pl.multiple_of(start * rows, rows), rows)


def enter(dp_count):
    d, t = place()
    barrier = pltpu.get_barrier_semaphore()
    for j in range(1, 4):
        pl.semaphore_signal(
            barrier, inc=1, device_id=(d, lax.rem(t + j, 4)), device_id_type=MESH
        )

    def greet(j, carry):
        pl.semaphore_signal(
            barrier, inc=1, device_id=(lax.rem(d + j, dp_count), t), device_id_type=MESH
        )
        return carry

    lax.fori_loop(1, dp_count, greet, 0)
    pl.semaphore_wait(barrier, 3 + dp_count - 1)


def remote(src, dst, send, recv, d, t):
    return pltpu.make_async_remote_copy(
        src_ref=src, dst_ref=dst, send_sem=send, recv_sem=recv, device_id=(d, t), device_id_type=MESH
    )


class VectorSum:
    def __init__(self, dp_count, dbuf, tbuf, dsend, drecv, tsend, trecv):
        self.dp_count = dp_count
        self.dbuf, self.tbuf = dbuf, tbuf
        self.dsend, self.drecv, self.tsend, self.trecv = dsend, drecv, tsend, trecv

    @staticmethod
    def scratch(dp_count):
        return [
            pltpu.VMEM((dp_count, VECTOR_ROWS, D), F32),
            pltpu.VMEM((4, VECTOR_ROWS, D), F32),
            DMA((dp_count,)),
            DMA((dp_count,)),
            DMA((4,)),
            DMA((4,)),
        ]

    def dcopy(self, j):
        d, t = place()
        return remote(
            self.dbuf.at[0], self.dbuf.at[j], self.dsend.at[j], self.drecv.at[j],
            lax.rem(d + j, self.dp_count), t,
        )

    def tcopy(self, j):
        d, t = place()
        return remote(
            self.tbuf.at[0], self.tbuf.at[j], self.tsend.at[j], self.trecv.at[j],
            d, lax.rem(t + j, 4),
        )

    def start(self, value):
        self.dbuf[0] = value

        def go(j, carry):
            self.dcopy(j).start()
            return carry

        lax.fori_loop(1, self.dp_count, go, 0)

    def middle(self):
        def wait(j, carry):
            self.dcopy(j).wait()
            return carry

        lax.fori_loop(1, self.dp_count, wait, 0)
        self.tbuf[0] = jnp.sum(self.dbuf[...], axis=0)
        for j in range(1, 4):
            self.tcopy(j).start()

    def finish(self):
        for j in range(1, 4):
            self.tcopy(j).wait()
        own = self.tbuf[0]
        total = own + self.tbuf[1] + self.tbuf[2] + self.tbuf[3]
        row = lax.broadcasted_iota(jnp.int32, own.shape, 0)
        return jnp.where(row < 6, total, own)


class TensorGather:
    def __init__(self, buf, send, recv):
        self.buf, self.rows = buf, buf.shape[0] // 4
        d, t = place()
        core, across, _ = tensor_peers(t)
        half = self.rows // 2
        at = lambda s, k: buf.at[block(s * 2 + k, half)]
        self.to_across = [
            remote(at(t, k), at(t, k), send.at[k], recv.at[k], d, across) for k in range(2)
        ]
        self.to_core = [
            remote(at(t, k), at(t, k), send.at[2 + k], recv.at[2 + k], d, core) for k in range(2)
        ]
        self.relay = [
            remote(at(across, k), at(across, k), send.at[4 + k], recv.at[4 + k], d, core)
            for k in range(2)
        ]

    @staticmethod
    def scratch(rows):
        return [pltpu.VMEM((4 * rows, D), BF16), DMA((6,)), DMA((6,))]

    def start(self, value):
        _, t = place()
        self.buf[block(t, self.rows)] = value
        for c in self.to_across + self.to_core:
            c.start()

    def forward(self):
        for k in range(2):
            self.to_across[k].wait_recv()
            self.relay[k].start()

    def finish(self):
        for c in self.to_across:
            c.wait_send()
        for c in self.to_core + self.relay:
            c.wait()


class TensorScatter:
    def __init__(self, part, near, far, out, send, recv):
        self.part, self.near, self.far, self.out = part, near, far, out
        d, t = place()
        core, across, diagonal = tensor_peers(t)
        self.count = far.shape[0]
        half = self.count // 2
        self.half = half
        p = lambda s, k: part.at[block(s * 2 + k, half)]
        n = lambda s, k: near.at[pl.ds((s * 2 + k) * half, half)]
        r = [pl.ds(k * half, half) for k in range(2)]
        self.rows = r
        self.first = [
            remote(p(diagonal, k), n(1, k), send.at[k], recv.at[k], d, core) for k in range(2)
        ]
        self.own = [
            remote(p(core, k), n(0, k), send.at[2 + k], recv.at[2 + k], d, core) for k in range(2)
        ]
        self.second = [
            remote(out.at[r[k]], far.at[r[k]], send.at[4 + k], recv.at[4 + k], d, across)
            for k in range(2)
        ]

    @staticmethod
    def scratch(rows):
        return [
            pltpu.VMEM((4 * rows, D), BF16),
            pltpu.VMEM((2 * rows, D), BF16),
            pltpu.VMEM((rows, D), BF16),
            pltpu.VMEM((rows, D), BF16),
            DMA((6,)),
            DMA((6,)),
        ]

    def start(self):
        for c in self.first + self.own:
            c.start()

    def middle(self):
        _, t = place()
        _, across, _ = tensor_peers(t)
        for k in range(2):
            self.first[k].wait_recv()
            self.out[self.rows[k]] = (
                self.part[block(across * 2 + k, self.half)].astype(F32)
                + self.near[pl.ds((2 + k) * self.half, self.half)].astype(F32)
            ).astype(BF16)
            self.second[k].start()

    def finish(self):
        _, t = place()
        for c in self.first:
            c.wait_send()
        for c in self.own + self.second:
            c.wait()
        return (
            self.part[block(t, self.count)].astype(F32)
            + self.near[pl.ds(0, self.count)].astype(F32)
            + self.far[...].astype(F32)
        )


def pair_peers():
    d, t = place()
    b, h, c = d % 2, t // 2, t % 2
    dx = d + 1 - 2 * b
    slot = lambda bb, hh, cc: bb * 4 + hh * 2 + cc
    return d, t, b, h, c, dx, slot


class PairGather:
    def __init__(self, buf, send, recv):
        self.buf, self.rows = buf, buf.shape[0] // 8
        d, t, b, h, c, dx, slot = pair_peers()
        half = self.rows // 2
        core, across = h * 2 + 1 - c, (1 - h) * 2 + c
        own, sx = slot(b, h, c), slot(1 - b, h, c)
        sy, sd = slot(b, 1 - h, c), slot(1 - b, 1 - h, c)

        def copy(i, s, k, dd, tt):
            ref = buf.at[block(s * 2 + k, half)]
            return remote(ref, ref, send.at[i], recv.at[i], dd, tt)

        self.own = own
        self.to_x = [copy(k, own, k, dx, t) for k in range(2)]
        self.to_y = [copy(2 + k, own, k, d, across) for k in range(2)]
        self.to_core = [copy(4 + k, own, k, d, core) for k in range(2)]
        self.x_to_y = copy(6, sx, 0, d, across)
        self.y_to_x = copy(7, sy, 1, dx, t)
        self.x_core = [copy(8 + k, sx, k, d, core) for k in range(2)]
        self.y_core = [copy(10 + k, sy, k, d, core) for k in range(2)]
        self.d_core = [copy(12 + k, sd, k, d, core) for k in range(2)]

    @staticmethod
    def scratch(rows):
        return [pltpu.VMEM((8 * rows, D), BF16), DMA((14,)), DMA((14,))]

    def start(self, value):
        self.buf[block(self.own, self.rows)] = value
        for c in (self.to_x[0], self.to_y[1], self.to_x[1], self.to_y[0]):
            c.start()
        for c in self.to_core:
            c.start()

    def forward(self):
        self.to_x[0].wait_recv()
        self.x_to_y.start()
        self.to_y[1].wait_recv()
        self.y_to_x.start()
        self.x_core[0].start()
        self.y_core[1].start()

    def relay(self):
        self.to_x[1].wait_recv()
        self.x_core[1].start()
        self.to_y[0].wait_recv()
        self.y_core[0].start()
        self.x_to_y.wait_recv()
        self.d_core[0].start()
        self.y_to_x.wait_recv()
        self.d_core[1].start()

    def finish(self):
        for c in self.to_x + self.to_y + [self.x_to_y, self.y_to_x]:
            c.wait_send()
        for c in self.to_core + self.x_core + self.y_core + self.d_core:
            c.wait()


class PairScatter:
    def __init__(self, part, near, diag, out, far, send, recv):
        self.part, self.near, self.diag, self.out, self.far = part, near, diag, out, far
        d, t, b, h, c, dx, slot = pair_peers()
        rows = part.shape[0] // 8
        half = rows // 2
        self.rows, self.half = rows, half
        core, across = h * 2 + 1 - c, (1 - h) * 2 + c
        where = [(1 - b, 1 - h), (1 - b, h), (b, 1 - h), (b, h)]
        self.mine = [slot(bb, hh, c) for bb, hh in where]
        theirs = [slot(bb, hh, 1 - c) for bb, hh in where]
        self.first = [
            remote(
                part.at[block(theirs[i], rows)], near.at[pl.ds(i * rows, rows)],
                send.at[i], recv.at[i], d, core,
            )
            for i in range(4)
        ]

        def at(ref, i, k):
            return ref.at[pl.ds((i * 2 + k) * half, half)]

        self.diag_x = remote(at(out, 0, 0), at(diag, 0, 0), send.at[4], recv.at[4], dx, t)
        self.diag_y = remote(at(out, 0, 1), at(diag, 0, 1), send.at[5], recv.at[5], d, across)
        self.to_x = [
            remote(at(out, 1, k), at(far, 0, k), send.at[6 + k], recv.at[6 + k], dx, t)
            for k in range(2)
        ]
        self.to_y = [
            remote(at(out, 2, k), at(far, 1, k), send.at[8 + k], recv.at[8 + k], d, across)
            for k in range(2)
        ]

    @staticmethod
    def scratch(rows):
        return [
            pltpu.VMEM((8 * rows, D), BF16),
            pltpu.VMEM((4 * rows, D), BF16),
            pltpu.VMEM((rows, D), BF16),
            pltpu.VMEM((3 * rows, D), BF16),
            pltpu.VMEM((2 * rows, D), BF16),
            DMA((10,)),
            DMA((10,)),
        ]

    def start(self):
        for c in self.first:
            c.start()

    def pair(self, i, k):
        return (
            self.part[block(self.mine[i] * 2 + k, self.half)].astype(F32)
            + self.near[pl.ds((i * 2 + k) * self.half, self.half)].astype(F32)
        )

    def put(self, i, k, value):
        self.out[pl.ds((i * 2 + k) * self.half, self.half)] = value.astype(BF16)

    def middle(self):
        self.first[0].wait_recv()
        self.put(0, 0, self.pair(0, 0))
        self.diag_x.start()
        self.put(0, 1, self.pair(0, 1))
        self.diag_y.start()
        self.first[1].wait_recv()
        self.put(1, 0, self.pair(1, 0))
        self.to_x[0].start()
        self.first[2].wait_recv()
        self.put(2, 1, self.pair(2, 1))
        self.to_y[1].start()

    def second(self):
        half = self.half
        self.diag_x.wait_recv()
        self.put(2, 0, self.pair(2, 0) + self.diag[pl.ds(0, half)].astype(F32))
        self.to_y[0].start()
        self.diag_y.wait_recv()
        self.put(1, 1, self.pair(1, 1) + self.diag[pl.ds(half, half)].astype(F32))
        self.to_x[1].start()

    def finish(self):
        for c in self.first + [self.diag_x, self.diag_y]:
            c.wait_send()
        self.first[3].wait_recv()
        for c in self.to_x + self.to_y:
            c.wait()
        rows = self.rows
        return (
            self.part[block(self.mine[3], rows)].astype(F32)
            + self.near[pl.ds(3 * rows, rows)].astype(F32)
            + self.far[pl.ds(0, rows)].astype(F32)
            + self.far[pl.ds(rows, rows)].astype(F32)
        )


class LineGather:
    def __init__(self, dp_count, buf, with_x, zsend, zrecv, xsend, xrecv):
        self.buf, self.with_x, self.line_count = buf, with_x, dp_count // 2
        self.rows = buf.shape[0] // (dp_count if with_x else dp_count // 2)
        self.zsend, self.zrecv, self.xsend, self.xrecv = zsend, zrecv, xsend, xrecv
        self.d, self.t = place()
        self.line, self.b = self.d // 2, self.d % 2

    @staticmethod
    def scratch(dp_count, shape):
        n = dp_count // 2
        return [pltpu.VMEM(shape, BF16), DMA((2, n)), DMA((n,)), DMA((n,)), DMA((n,))]

    def at(self, blk, b):
        slot = blk * 2 + b if self.with_x else blk
        return self.buf.at[block(slot, self.rows)]

    def zcopy(self, way, step, blk):
        ref = self.at(blk, self.b)
        return remote(
            ref, ref, self.zsend.at[way, step], self.zrecv.at[blk],
            (self.line + (1 if way == 0 else -1)) * 2 + self.b, self.t,
        )

    def xcopy(self, blk, b):
        ref = self.at(blk, b)
        return remote(
            ref, ref, self.xsend.at[blk], self.xrecv.at[blk],
            self.line * 2 + (1 - self.b), self.t,
        )

    def more(self, way):
        return (self.line + 1 < self.line_count) if way == 0 else (self.line > 0)

    def place(self, own):
        slot = self.d if self.with_x else self.line
        self.buf[block(slot, self.rows)] = own[...]

    def start(self):
        for way in range(2):

            @pl.when(self.more(way))
            def _():
                self.zcopy(way, 0, self.line).start()

        if self.with_x:
            self.xcopy(self.line, self.b).start()

    def hop(self, step, act, sending=False):
        for way in range(2):
            blk = self.line - step if way == 0 else self.line + step
            valid = (blk >= 0) if way == 0 else (blk < self.line_count)
            if sending:
                valid = valid & self.more(way)

            @pl.when(valid)
            def _():
                act(way, step, blk)

    def relay(self, step):
        def act(way, step, blk):
            self.zcopy(way, step, blk).wait_recv()

            @pl.when(self.more(way))
            def _():
                self.zcopy(way, step, blk).start()

            if self.with_x:
                self.xcopy(blk, self.b).start()

        self.hop(step, act)

    def finish(self):
        if self.with_x:

            def pair(blk, carry):
                self.xcopy(blk, 1 - self.b).wait_recv()
                return carry

            lax.fori_loop(0, self.line_count, pair, 0)

    def drain(self):
        def act(way, step, blk):
            self.zcopy(way, step, blk).wait_send()

        def step(i, carry):
            self.hop(i, act, sending=True)
            if self.with_x:
                self.xcopy(i, self.b).wait_send()
            return carry

        lax.fori_loop(0, self.line_count, step, 0)


def relay_range(items, first, last):
    def body(step, carry):
        for item in items:
            item.relay(step)
        return carry

    if first < last:
        lax.fori_loop(first, last, body, 0)


class LineReduce:
    def __init__(self, dp_count, with_x, grad, below, above, held, xsend, xrecv, zsend, zrecv):
        self.grad, self.below, self.above, self.with_x = grad, below, above, with_x
        self.held = held if with_x else grad
        self.xsend, self.xrecv, self.zsend, self.zrecv = xsend, xrecv, zsend, zrecv
        self.line_count = dp_count // 2
        self.rows = grad.shape[0] // (dp_count if with_x else self.line_count)
        self.d, self.t = place()
        self.line, self.b = self.d // 2, self.d % 2

    @staticmethod
    def scratch(dp_count, with_x, shape):
        n = dp_count // 2
        half = (shape[0] // 2, shape[1]) if with_x else shape
        held = half if with_x else (16, LANES)
        return [
            pltpu.VMEM(shape, BF16), pltpu.VMEM(half, BF16), pltpu.VMEM(half, BF16),
            pltpu.VMEM(held, BF16), DMA((n,)), DMA((n,)), DMA((n,)), DMA((2, n)),
        ]

    def xcopy(self, target):
        return remote(
            self.grad.at[block(target * 2 + (1 - self.b), self.rows)],
            self.held.at[block(target, self.rows)],
            self.xsend.at[target], self.xrecv.at[target],
            self.line * 2 + (1 - self.b), self.t,
        )

    def zcopy(self, way, target):
        dst = self.below if way == 0 else self.above
        return remote(
            self.held.at[block(target, self.rows)], dst.at[block(target, self.rows)],
            self.zsend.at[target], self.zrecv.at[way, target],
            (self.line + (1 if way == 0 else -1)) * 2 + self.b, self.t,
        )

    def each_target(self, act, first=0, stop=None):
        last = self.line_count - 1
        stop = last if stop is None else min(stop, last)

        def step(i, carry):
            @pl.when(last - i > self.line)
            def _():
                act(0, last - i)

            @pl.when(i < self.line)
            def _():
                act(1, i)

            return carry

        if first < stop:
            lax.fori_loop(first, stop, step, 0)

    def start(self):
        if self.with_x:

            def send(way, target):
                self.xcopy(target).start()

            self.each_target(send)
            send(0, self.line)

    def has(self, way):
        return (self.line > 0) if way == 0 else (self.line + 1 < self.line_count)

    def run(self, first=0, stop=None):
        def reduce(way, target):
            at = block(target, self.rows)
            dst = self.below if way == 0 else self.above
            if self.with_x:
                self.xcopy(target).wait_recv()
                mine = self.grad[block(target * 2 + self.b, self.rows)].astype(F32)

            @pl.when(self.has(way))
            def _():
                self.zcopy(way, target).wait_recv()
                total = self.held[at].astype(F32) + dst[at].astype(F32)
                if self.with_x:
                    total = total + mine
                self.held[at] = total.astype(BF16)

            if self.with_x:

                @pl.when(jnp.logical_not(self.has(way)))
                def _():
                    self.held[at] = (mine + self.held[at].astype(F32)).astype(BF16)

            self.zcopy(way, target).start()

        self.each_target(reduce, first, stop)

    def finish(self, put, add):
        at = block(self.line, self.rows)
        if self.with_x:
            self.xcopy(self.line).wait_recv()
            own = self.grad[block(self.d, self.rows)].astype(F32)
            put(own + self.held[at].astype(F32))
        else:
            put(self.grad[at].astype(F32))
        for way in range(2):

            @pl.when(self.has(way))
            def _():
                self.zcopy(way, self.line).wait_recv()
                add((self.below if way == 0 else self.above)[at].astype(F32))

    def drain(self):
        def act(way, target):
            self.zcopy(way, target).wait_send()
            if self.with_x:
                self.xcopy(target).wait_send()

        self.each_target(act)
        if self.with_x:
            self.xcopy(self.line).wait_send()


class Refs:
    def __init__(self):
        self.shapes, self.refs, self.at = [], None, 0

    def bind(self, refs):
        self.refs, self.at = refs, 0

    def take(self, shapes):
        if self.refs is None:
            self.shapes += shapes
            return [None] * len(shapes)
        got = self.refs[self.at : self.at + len(shapes)]
        self.at += len(shapes)
        return got


class Sizes:
    def __init__(self, dp_count, rows, group, qkv, dense, up, down):
        self.dp, self.lines, self.rows, self.group = dp_count, dp_count // 2, rows, group
        self.qkv_cols, self.heads = qkv[1], qkv[1] // (3 * HEAD)
        self.width = self.heads * HEAD
        self.hidden = up[2]
        self.qkv_rows, self.dense_rows, self.up_rows, self.down_rows = qkv[0], dense[0], up[1], down[0]
        self.dense_whole = dense[0] == self.width
        self.piece = D // (dp_count * TENSOR)
        self.up_piece = 2 * self.hidden // dp_count
        self.qv_piece = 2 * self.width // dp_count


def scratch_of(s, pool):
    take = pool.take
    out = {}
    out["vsum"] = take(VectorSum.scratch(s.dp))
    out["vsum_out"] = take(VectorSum.scratch(s.dp))
    out["gather_x"] = take(TensorGather.scratch(s.rows))
    out["gather_low"] = take(TensorGather.scratch(s.rows))
    out["scatter_attn"] = take(TensorScatter.scratch(s.rows))
    out["scatter_in"] = take(TensorScatter.scratch(s.rows))
    out["gather_mlp"] = take(PairGather.scratch(s.rows))
    out["gather_og"] = take(PairGather.scratch(s.rows))
    out["scatter_mlp"] = take(PairScatter.scratch(s.rows))
    out["scatter_out"] = take(PairScatter.scratch(s.rows))
    out["w_qkv"] = take(LineGather.scratch(s.dp, (D, s.qkv_cols)))
    out["w_dense"] = take(LineGather.scratch(s.dp, (s.width, D)))
    out["w_up"] = take(LineGather.scratch(s.dp, (D, s.hidden)))
    out["w_down"] = take(LineGather.scratch(s.dp, (s.hidden, D)))
    out["up_swap"] = take([DMA, DMA])
    out["g_qkv"] = take(LineReduce.scratch(s.dp, True, (D, s.qkv_cols)))
    out["g_dense"] = take(LineReduce.scratch(s.dp, True, (s.width, D)))
    out["g_up"] = take(LineReduce.scratch(s.dp, False, (D, s.hidden)))
    out["g_down"] = take(LineReduce.scratch(s.dp, False, (s.hidden, D)))
    out["g_swap"] = take(
        [
            pltpu.VMEM((2 * s.up_rows, s.hidden), F32),
            pltpu.VMEM((s.up_rows, s.hidden), BF16),
            pltpu.VMEM((s.up_rows, s.hidden), BF16),
            DMA,
            DMA,
        ]
    )
    out["data"] = take(
        [
            pltpu.VMEM((D, s.group), BF16),
            pltpu.VMEM((s.qkv_cols, s.group), BF16),
            pltpu.VMEM((s.heads, s.group, s.group), F32),
            pltpu.VMEM((s.width, s.group), BF16),
            pltpu.VMEM((s.width, s.group), BF16),
            pltpu.VMEM((s.qkv_cols, s.group), BF16),
            pltpu.VMEM((s.group, s.qkv_cols), BF16),
            pltpu.VMEM((2 * s.group, s.hidden), BF16),
            pltpu.VMEM((2 * s.group, s.hidden), F32),
            pltpu.VMEM((2 * s.group, s.hidden), BF16),
            pltpu.VMEM((s.rows, D), F32),
            pltpu.VMEM((s.rows, D), F32),
            pltpu.VMEM((s.rows, D), F32),
        ]
    )
    return out


def loop(count, body):
    def step(i, carry):
        body(i)
        return carry

    lax.fori_loop(0, count, step, 0)


def block_kernel(s, refs_in):
    pool = Refs()
    scratch_of(s, pool)
    names_in, names_out = 9, 7
    (vec_ref, fill_ref, begin_ref, x_ref, og_ref, wq_ref, wd_ref, wu_ref, wn_ref) = refs_in[:names_in]
    (block_out, input_grad, qkv_out, dense_out, up_out, down_out, vec_out) = refs_in[
        names_in : names_in + names_out
    ]
    pool.bind(refs_in[names_in + names_out :])
    got = scratch_of(s, pool)
    d, t = place()
    b = d % 2
    rows, group, hidden = s.rows, s.group, s.hidden
    (attn_in_t, qkv_t, probs_t, context_t, context_grad_t, qkv_grad_t, qkv_grad,
     active, slope, pre_grad, live_grad, middle, middle_grad) = got["data"]

    vsum, vsum_out = VectorSum(s.dp, *got["vsum"]), VectorSum(s.dp, *got["vsum_out"])
    attn_in, gx_send, gx_recv = got["gather_x"]
    gather_x = TensorGather(attn_in, gx_send, gx_recv)
    middle_low, gl_send, gl_recv = got["gather_low"]
    gather_low = TensorGather(middle_low, gl_send, gl_recv)
    scatter_attn = TensorScatter(*got["scatter_attn"])
    scatter_in = TensorScatter(*got["scatter_in"])
    mlp_in, gm_send, gm_recv = got["gather_mlp"]
    gather_mlp = PairGather(mlp_in, gm_send, gm_recv)
    out_low, go_send, go_recv = got["gather_og"]
    gather_og = PairGather(out_low, go_send, go_recv)
    scatter_mlp = PairScatter(*got["scatter_mlp"])
    scatter_out = PairScatter(*got["scatter_out"])
    w_qkv = LineGather(s.dp, got["w_qkv"][0], True, *got["w_qkv"][1:])
    w_dense = LineGather(s.dp, got["w_dense"][0], True, *got["w_dense"][1:])
    w_up = LineGather(s.dp, got["w_up"][0], False, *got["w_up"][1:])
    w_down = LineGather(s.dp, got["w_down"][0], False, *got["w_down"][1:])
    g_qkv = LineReduce(s.dp, True, *got["g_qkv"])
    g_dense = LineReduce(s.dp, True, *got["g_dense"])
    g_up = LineReduce(s.dp, False, *got["g_up"])
    g_down = LineReduce(s.dp, False, *got["g_down"])
    attn_weights = [w_qkv] if s.dense_whole else [w_qkv, w_dense]
    mlp_weights = [w_up, w_down]
    up_swap = remote(
        wu_ref.at[1 - b], w_up.buf.at[block(d, s.up_rows)], got["up_swap"][0], got["up_swap"][1],
        d + 1 - 2 * b, t,
    )

    enter(s.dp)
    shard = d * TENSOR + t
    vec_in = jnp.concatenate(
        [vec_ref[...], jnp.zeros((VECTOR_ROWS, D - LANES), F32)], axis=1
    )
    up_place = b * hidden + (d // 2) * s.up_piece
    row = lax.broadcasted_iota(jnp.int32, (VECTOR_ROWS, D), 0)

    def turn(value, first, second, third):
        return jnp.where(
            row < 6,
            pltpu.roll(value, first, 1),
            jnp.where(row == 6, pltpu.roll(value, second, 1), pltpu.roll(value, third, 1)),
        )

    vsum.start(turn(vec_in, shard * s.piece, up_place, d * s.qv_piece))
    w_qkv.place(wq_ref)
    if not s.dense_whole:
        w_dense.place(wd_ref)
    for w in attn_weights:
        w.start()
    up_swap.start()
    own_row = t * rows + lax.broadcasted_iota(jnp.int32, (rows, D), 0)
    live = og_ref[...] * (own_row < fill_ref[0]).astype(F32)
    live_grad[...] = live
    w_up.buf[block(d, s.up_rows)] = wu_ref[b]
    w_down.place(wn_ref)
    vsum.middle()
    x_normed, x_inverse = normalize(x_ref[...])
    relay_range(attn_weights, 1, 2)
    vec = vsum.finish()
    gather_x.start((x_normed * vec[0:1] + vec[1:2]).astype(BF16))
    up_swap.wait()
    for w in mlp_weights:
        w.start()
    gather_og.start(live.astype(BF16))
    relay_range(attn_weights, 2, s.lines)
    gather_x.forward()
    gather_og.forward()
    gather_x.finish()
    attn_in_t[...] = attn_in[...].T
    for w in attn_weights:
        w.finish()

    wq, wd = w_qkv.buf, (wd_ref if s.dense_whole else w_dense.buf)
    zero_bias = jnp.zeros((1, HEAD), F32)
    pieces = []
    for h in range(s.heads):
        at = 2 * h * HEAD
        pieces += [vec[7:8, at : at + HEAD], zero_bias, vec[7:8, at + HEAD : at + 2 * HEAD]]
    qkv_bias = jnp.concatenate(pieces, axis=1)

    def project(i):
        tile = block(i, 256)
        value = dot_nn(attn_in[tile], wq[...]) + qkv_bias
        qkv_t[:, tile] = value.astype(BF16).T

    loop(group // 256, project)
    gather_og.relay()

    def part_of(ref, h, which):
        return ref.at[block(3 * h + which, HEAD)]

    def attend(h):
        query = part_of(qkv_t, h, 0)
        key = part_of(qkv_t, h, 1)[...].T
        value = part_of(qkv_t, h, 2)
        head = (t * s.heads + h + 1).astype(F32)
        m = jnp.exp2(jnp.full((1, 256), -8.0 / HEADS, F32) * head)
        for i in range(group // 256):
            n = (i + 1) * 256
            cols = pl.ds(i * 256, 256)
            score = dot_nn(key[:n], query[:, cols]) * (1.0 / math.sqrt(HEAD))
            at_key = lax.broadcasted_iota(jnp.int32, (n, 256), 0)
            at_query = lax.broadcasted_iota(jnp.int32, (n, 256), 1) + i * 256
            score = score + m * (at_key - at_query).astype(F32)
            seen = (at_key >= begin_ref[:, cols]) & (at_key <= at_query)
            score = jnp.where(seen, score, MASKED_SCORE)
            weight = jnp.exp(score - jnp.max(score, axis=0, keepdims=True))
            weight = weight * (1.0 / jnp.sum(weight, axis=0, keepdims=True))
            probs_t[h, 0:n, cols] = weight
            context = dot_nn(value[:, 0:n], weight.astype(BF16))
            context_t[block(h, HEAD), cols] = context.astype(BF16)

    relay_range(mlp_weights, 1, 2)
    loop(s.heads, attend)

    part_attn = scatter_attn.part

    def project_out(i):
        tile = block(i, 256)
        part_attn[tile] = dot_tn(context_t[:, tile], wd[...]).astype(BF16)

    loop(group // 256, project_out)
    scatter_attn.start()
    scatter_attn.middle()
    relay_range(mlp_weights, 2, 3)
    mid = x_ref[...] + vec[2:3] + scatter_attn.finish()
    middle[...] = mid
    mid_normed, mid_inverse = normalize(mid)
    gather_mlp.start((mid_normed * vec[3:4] + vec[4:5]).astype(BF16))
    gather_mlp.forward()
    gather_og.finish()
    gather_mlp.relay()
    gather_mlp.finish()
    relay_range(mlp_weights, 3, s.lines)

    up, down = w_up.buf, w_down.buf
    up_bias = jnp.where(b == 0, vec[6:7, 0:hidden], vec[6:7, hidden : 2 * hidden])
    cubic, scale = 0.044715, math.sqrt(2.0 / math.pi)

    def forward(i):
        tile = block(i, 256)
        u = dot_nn(mlp_in[tile], up[...]) + up_bias
        square = u * u
        bend = jnp.tanh(scale * (u + cubic * (square * u)))
        active[tile] = (0.5 * u * (1.0 + bend)).astype(BF16)
        slope[tile] = 0.5 * (1.0 + bend) + (0.5 * scale) * u * (1.0 - bend * bend) * (
            1.0 + (3.0 * cubic) * square
        )

    loop(2 * group // 256, forward)

    def backward(i):
        tile = block(i, 256)
        grad = dot_nt(out_low[tile], down[...]) * slope[tile]
        low = grad.astype(BF16)
        pre_grad[tile] = low
        scatter_mlp.part[tile] = dot_nt(low, up[...]).astype(BF16)

    loop(2 * group // 256, backward)
    scatter_mlp.start()

    def down_gradient(i):
        cols = block(i, LANES)
        g_down.grad[cols] = dot_tn(active[:, cols], out_low[...]).astype(BF16)

    loop(hidden // LANES, down_gradient)
    scatter_mlp.middle()
    g_down.run(0, 1)

    def up_gradient(i):
        cols = block(i, 256)
        g_up.grad[cols] = dot_tn(mlp_in[:, cols], pre_grad[...]).astype(BF16)

    loop(D // 256, up_gradient)
    scatter_mlp.second()
    g_up.run(0, 1)

    def forward_out(i):
        tile = block(i, 256)
        scatter_out.part[tile] = dot_nn(active[tile], down[...]).astype(BF16)

    loop(2 * group // 256, forward_out)
    up_bias_grad = column_sum(pre_grad[...].astype(F32))
    live = live_grad[...]
    upstream = scatter_mlp.finish()
    mid_normed, mid_inverse = normalize(middle[...])
    mid_grad = live + norm_backward(upstream, vec[3:4], mid_normed, mid_inverse)
    middle_grad[...] = mid_grad
    gather_low.start(mid_grad.astype(BF16))
    sums = put_rows(
        jnp.zeros((VECTOR_ROWS, D), F32),
        [
            (2, column_sum(mid_grad)),
            (3, column_sum(upstream * mid_normed)),
            (4, column_sum(upstream)),
            (5, column_sum(live)),
        ],
    )
    g_down.run(1, 2)
    gather_low.forward()
    g_up.run(1, 2)
    gather_low.finish()

    def dense_back(i):
        tile = block(i, 256)
        context_grad_t[:, tile] = dot_nt(wd[...], middle_low[tile]).astype(BF16)

    loop(group // 256, dense_back)
    dense_grad = dot_nn(context_t[...], middle_low[...])
    if s.dense_whole:
        dense_out[...] = dense_grad
    else:
        g_dense.grad[...] = dense_grad.astype(BF16)
        g_dense.start()
    root = 1.0 / math.sqrt(HEAD)

    def attend_back(h):
        at = block(h, HEAD)
        grad_t = context_grad_t[at]
        delta = column_sum(grad_t.astype(F32) * context_t[at].astype(F32))
        query, key = part_of(qkv_t, h, 0)[...], part_of(qkv_t, h, 1)[...]
        value = part_of(qkv_t, h, 2)[...].T
        query_grad, key_grad, value_grad = [], None, None
        for i in range(group // 256):
            n = (i + 1) * 256
            cols = slice(i * 256, n)
            probs = probs_t[h, 0:n, cols]
            score = (probs * (dot_nn(value[:n], grad_t[:, cols]) - delta[:, cols])).astype(BF16)
            query_grad.append(dot_nn(key[:, :n], score))
            key_part = dot_nt(query[:, cols], score)
            value_part = dot_nt(grad_t[:, cols], probs.astype(BF16))
            if i == 0:
                key_grad, value_grad = key_part, value_part
            else:
                wide = lambda v: jnp.concatenate(
                    [v, jnp.zeros((HEAD, n - v.shape[1]), F32)], axis=1
                )
                key_grad, value_grad = wide(key_grad) + key_part, wide(value_grad) + value_part
        part_of(qkv_grad_t, h, 0)[...] = (jnp.concatenate(query_grad, axis=1) * root).astype(BF16)
        part_of(qkv_grad_t, h, 1)[...] = (key_grad * root).astype(BF16)
        part_of(qkv_grad_t, h, 2)[...] = value_grad.astype(BF16)

    loop(s.heads, attend_back)
    qkv_grad[...] = qkv_grad_t[...].T

    def input_part(i):
        tile = block(i, 256)
        scatter_in.part[tile] = dot_nt(qkv_grad[tile], wq[...]).astype(BF16)

    loop(group // 256, input_part)
    scatter_in.start()

    def qkv_gradient(i):
        tile = block(i, 256)
        g_qkv.grad[tile] = dot_nn(attn_in_t[tile], qkv_grad[...]).astype(BF16)

    loop(D // 256, qkv_gradient)
    g_qkv.start()
    scatter_in.middle()
    g_down.run(2)
    g_up.run(2)
    if not s.dense_whole:
        g_dense.run()
    g_qkv.run(0, 1)
    scatter_out.start()
    scatter_out.middle()
    qkv_sum = column_sum(qkv_grad[...].astype(F32))
    qv_parts = []
    for h in range(s.heads):
        at = 3 * h * HEAD
        qv_parts += [qkv_sum[:, at : at + HEAD], qkv_sum[:, at + 2 * HEAD : at + 3 * HEAD]]
    qv_parts.append(jnp.zeros((1, D - 2 * s.width), F32))
    qv_grad = jnp.concatenate(qv_parts, axis=1)
    up_grad_row = jnp.concatenate(
        [jnp.where(b == 0, up_bias_grad, 0.0), jnp.where(b == 1, up_bias_grad, 0.0)], axis=1
    )
    x_normed, x_inverse = normalize(x_ref[...])
    upstream = scatter_in.finish()
    vsum_out.start(
        put_rows(
            sums,
            [
                (0, column_sum(upstream * x_normed)),
                (1, column_sum(upstream)),
                (6, up_grad_row),
                (7, qv_grad),
            ],
        )
    )
    input_grad[...] = middle_grad[...] + norm_backward(upstream, vec[0:1], x_normed, x_inverse)
    scatter_out.second()
    g_qkv.run(1, 2)
    vsum_out.middle()
    g_qkv.run(2)

    def keep(ref):
        def put(value):
            ref[...] = value

        def add(value):
            ref[...] += value

        return put, add

    swap_sum, swap_send, swap_recv, ssem, rsem = got["g_swap"]
    g_down.finish(*keep(down_out))
    g_up.finish(*keep(swap_sum))
    swap_send[...] = swap_sum[block(1 - b, s.up_rows)].astype(BF16)
    swap = remote(swap_send, swap_recv, ssem, rsem, d + 1 - 2 * b, t)
    swap.start()
    up_out[b] = swap_sum[block(b, s.up_rows)]
    block_out[...] = middle[...] + scatter_out.finish() + vec[5:6]
    if not s.dense_whole:
        g_dense.finish(*keep(dense_out))
    g_qkv.finish(*keep(qkv_out))
    swap.wait()
    up_out[1 - b] = swap_recv[...].astype(F32)
    total = vsum_out.finish()
    back = lambda at: lax.rem(D - at, D)
    total = turn(total, back(shard * s.piece), back(up_place), back(d * s.qv_piece))
    vec_out[...] = total[:, :LANES]
    for w in attn_weights + mlp_weights:
        w.drain()
    g_down.drain()
    g_up.drain()
    if not s.dense_whole:
        g_dense.drain()
    g_qkv.drain()


def block_call(s, *args):
    shape = jax.ShapeDtypeStruct
    pool = Refs()
    scratch_of(s, pool)
    vmem = pl.BlockSpec(memory_space=pltpu.VMEM)
    smem = pl.BlockSpec(memory_space=pltpu.SMEM)
    dense = (s.width if s.dense_whole else s.dense_rows, D)
    return pl.pallas_call(
        lambda *refs: block_kernel(s, refs),
        out_shape=[
            shape((s.rows, D), F32),
            shape((s.rows, D), F32),
            shape((s.qkv_rows, s.qkv_cols), F32),
            shape(dense, F32),
            shape((2, s.up_rows, s.hidden), F32),
            shape((s.down_rows, D), F32),
            shape((VECTOR_ROWS, LANES), F32),
        ],
        in_specs=[vmem, smem] + [vmem] * 7,
        out_specs=[vmem] * 7,
        scratch_shapes=pool.shapes,
        compiler_params=pltpu.CompilerParams(
            collective_id=1, has_side_effects=True, vmem_limit_bytes=62 * 1024 * 1024
        ),
        name="block_both_ways",
    )(*args)


def per_device(
    dp_count,
    block_input,
    seq_begin,
    group_fill,
    attention_norm_gain,
    attention_norm_bias,
    qkv_weight,
    qv_bias,
    dense_weight,
    dense_bias,
    feedforward_norm_gain,
    feedforward_norm_bias,
    up_weight,
    up_bias,
    down_weight,
    down_bias,
    out_grad,
):
    vectors = [
        attention_norm_gain,
        attention_norm_bias,
        dense_bias,
        feedforward_norm_gain,
        feedforward_norm_bias,
        down_bias,
        up_bias.astype(F32),
        qv_bias.astype(F32),
    ]
    vec = jnp.stack([jnp.pad(v, (0, LANES - v.shape[0])) for v in vectors])
    up_rows, up_cols = up_weight.shape
    lines, piece = dp_count // 2, up_bias.shape[0]
    up_split = up_weight.reshape(up_rows, lines, 2, piece).transpose(2, 0, 1, 3)
    up_split = up_split.reshape(2, up_rows, up_cols // 2)
    whole = dense_weight.shape[0] % 16 != 0
    dense = lax.all_gather(dense_weight, "dp", axis=0, tiled=True) if whole else dense_weight
    s = Sizes(
        dp_count, block_input.shape[0], seq_begin.shape[0], qkv_weight.shape, dense.shape,
        up_split.shape, down_weight.shape,
    )
    block_out, input_grad, qkv_out, dense_out, up_out, down_out, vec_out = block_call(
        s, vec, group_fill, seq_begin[None], block_input, out_grad, qkv_weight, dense, up_split,
        down_weight,
    )
    if whole:
        dense_out = lax.psum_scatter(dense_out, "dp", scatter_dimension=0, tiled=True)
    up_out = up_out.reshape(2, up_rows, lines, piece).transpose(1, 2, 0, 3)
    up_out = up_out.reshape(up_rows, up_cols)
    own = lambda i, v: vec_out[i, : v.shape[0]]
    return (
        block_out,
        input_grad,
        own(0, attention_norm_gain),
        own(1, attention_norm_bias),
        qkv_out,
        own(7, qv_bias),
        dense_out,
        own(2, dense_bias),
        own(3, feedforward_norm_gain),
        own(4, feedforward_norm_bias),
        up_out,
        own(6, up_bias),
        down_out,
        own(5, down_bias),
    )


def solution(mesh):
    rows, line = P(("dp", "tensor"), None), P(("dp", "tensor"))
    inner, columns = P(("tensor", "dp")), P("dp", "tensor")
    inner_rows = P(("tensor", "dp"), None)
    return jax.shard_map(
        functools.partial(per_device, mesh.shape["dp"]),
        mesh=mesh,
        in_specs=(
            rows, P("dp"), P("dp"), line, line, columns, inner, inner_rows, line, line, line,
            columns, inner, inner_rows, line, rows,
        ),
        out_specs=(
            rows, rows, line, line, columns, inner, inner_rows, line, line, line, columns, inner,
            inner_rows, line,
        ),
        check_vma=False,
    )
```

```python
import functools
import math

import jax
import jax.numpy as jnp
from jax import lax
from jax.experimental import pallas as pl
from jax.experimental.pallas import tpu as pltpu
from jax.sharding import PartitionSpec as P

D = 1024
HEADS = 16
HEAD = D // HEADS
TENSOR = 4
EPSILON = 1e-05
MASKED_SCORE = -1e30
MESH = pl.DeviceIdType.MESH
VECTOR_ROWS = 8
LANES = 128
BF16 = jnp.bfloat16
F32 = jnp.float32
DMA = pltpu.SemaphoreType.DMA


def dot_nn(a, b):
    return lax.dot_general(a, b, (((1,), (0,)), ((), ())), preferred_element_type=F32)


def dot_nt(a, b):
    return lax.dot_general(a, b, (((1,), (1,)), ((), ())), preferred_element_type=F32)


def dot_tn(a, b):
    return lax.dot_general(a, b, (((0,), (0,)), ((), ())), preferred_element_type=F32)


def normalize(hidden):
    centred = hidden - jnp.mean(hidden, axis=-1, keepdims=True)
    inverse = lax.rsqrt(jnp.mean(centred * centred, axis=-1, keepdims=True) + EPSILON)
    return centred * inverse, inverse


def norm_backward(upstream, gain, normed, inverse):
    scaled = upstream * gain
    return inverse * (
        scaled
        - jnp.mean(scaled, axis=-1, keepdims=True)
        - normed * jnp.mean(scaled * normed, axis=-1, keepdims=True)
    )


def column_sum(value):
    return jnp.sum(value, axis=0, keepdims=True)


def put_rows(base, values):
    row = lax.broadcasted_iota(jnp.int32, base.shape, 0)
    for index, value in values:
        base = jnp.where(row == index, value, base)
    return base


def place():
    return lax.axis_index("dp"), lax.axis_index("tensor")


def tensor_peers(t):
    h, c = t // 2, t % 2
    core = h * 2 + (1 - c)
    across = (1 - h) * 2 + c
    diagonal = (1 - h) * 2 + (1 - c)
    return core, across, diagonal


def block(start, rows):
    return pl.ds(pl.multiple_of(start * rows, rows), rows)


def enter(dp_count):
    d, t = place()
    barrier = pltpu.get_barrier_semaphore()
    for j in range(1, 4):
        pl.semaphore_signal(
            barrier, inc=1, device_id=(d, lax.rem(t + j, 4)), device_id_type=MESH
        )

    def greet(j, carry):
        pl.semaphore_signal(
            barrier, inc=1, device_id=(lax.rem(d + j, dp_count), t), device_id_type=MESH
        )
        return carry

    lax.fori_loop(1, dp_count, greet, 0)


def entered(dp_count):
    pl.semaphore_wait(pltpu.get_barrier_semaphore(), 3 + dp_count - 1)


def remote(src, dst, send, recv, d, t):
    return pltpu.make_async_remote_copy(
        src_ref=src, dst_ref=dst, send_sem=send, recv_sem=recv, device_id=(d, t), device_id_type=MESH
    )


class VectorExchange:
    def __init__(self, dp_count, dout, din, tbuf, dsend, drecv, tsend, trecv):
        self.dp_count = dp_count
        self.dout, self.din, self.tbuf = dout, din, tbuf
        self.dsend, self.drecv, self.tsend, self.trecv = dsend, drecv, tsend, trecv

    @staticmethod
    def scratch(dp_count, outgoing, width):
        return [
            pltpu.VMEM((outgoing, VECTOR_ROWS, LANES), F32),
            pltpu.VMEM((dp_count, VECTOR_ROWS, LANES), F32),
            pltpu.VMEM((4, VECTOR_ROWS, width), F32),
            DMA((dp_count,)),
            DMA((dp_count,)),
            DMA((4,)),
            DMA((4,)),
        ]

    def peer(self, j):
        return lax.rem(place()[0] + j, self.dp_count)

    def source(self, j):
        return lax.rem(place()[0] + self.dp_count - j, self.dp_count)

    def dcopy(self, j):
        out = self.dout.at[j] if self.dout.shape[0] > 1 else self.dout.at[0]
        return remote(
            out, self.din.at[j], self.dsend.at[j], self.drecv.at[j], self.peer(j), place()[1]
        )

    def tcopy(self, j):
        d, t = place()
        return remote(
            self.tbuf.at[0], self.tbuf.at[j], self.tsend.at[j], self.trecv.at[j],
            d, lax.rem(t + j, 4),
        )

    def start(self, block_for):
        def go(j, carry):
            value = block_for(self.peer(j))
            if self.dout.shape[0] > 1:
                self.dout[j] = value
            self.dcopy(j).start()
            return carry

        self.din[0] = block_for(place()[0])
        if self.dout.shape[0] == 1:
            self.dout[0] = block_for(place()[0])
        lax.fori_loop(1, self.dp_count, go, 0)

    def middle(self, spread):
        def wait(j, carry):
            self.dcopy(j).wait()
            return carry

        lax.fori_loop(1, self.dp_count, wait, 0)

        def add(j, total):
            return total + spread(self.din[j], self.source(j))

        self.tbuf[0] = lax.fori_loop(0, self.dp_count, add, jnp.zeros(self.tbuf.shape[1:], F32))
        for j in range(1, 4):
            self.tcopy(j).start()

    def finish(self):
        for j in range(1, 4):
            self.tcopy(j).wait()
        own = self.tbuf[0]
        total = own + self.tbuf[1] + self.tbuf[2] + self.tbuf[3]
        row = lax.broadcasted_iota(jnp.int32, own.shape, 0)
        return jnp.where(row < 6, total, own)


class TensorGather:
    def __init__(self, buf, send, recv):
        self.buf, self.rows = buf, buf.shape[0] // 4
        d, t = place()
        core, across, _ = tensor_peers(t)
        half = self.rows // 2
        at = lambda s, k: buf.at[block(s * 2 + k, half)]
        self.to_across = [
            remote(at(t, k), at(t, k), send.at[k], recv.at[k], d, across) for k in range(2)
        ]
        self.to_core = [
            remote(at(t, k), at(t, k), send.at[2 + k], recv.at[2 + k], d, core) for k in range(2)
        ]
        self.relay = [
            remote(at(across, k), at(across, k), send.at[4 + k], recv.at[4 + k], d, core)
            for k in range(2)
        ]

    @staticmethod
    def scratch(rows):
        return [pltpu.VMEM((4 * rows, D), BF16), DMA((6,)), DMA((6,))]

    def start_half(self, k, value):
        _, t = place()
        self.buf[block(t * 2 + k, self.rows // 2)] = value
        self.to_across[k].start()
        self.to_core[k].start()

    def start(self, value):
        half = self.rows // 2
        for k in range(2):
            self.start_half(k, value[k * half : (k + 1) * half])

    def forward(self):
        for k in range(2):
            self.to_across[k].wait_recv()
            self.relay[k].start()

    def finish(self):
        for c in self.to_across:
            c.wait_send()
        for c in self.to_core + self.relay:
            c.wait()


class TensorScatter:
    def __init__(self, part, near, far, out, send, recv):
        self.part, self.near, self.far, self.out = part, near, far, out
        d, t = place()
        core, across, diagonal = tensor_peers(t)
        self.count = far.shape[0]
        half = self.count // 2
        self.half = half
        p = lambda s, k: part.at[block(s * 2 + k, half)]
        n = lambda s, k: near.at[pl.ds((s * 2 + k) * half, half)]
        r = [pl.ds(k * half, half) for k in range(2)]
        self.rows = r
        self.first = [
            remote(p(diagonal, k), n(1, k), send.at[k], recv.at[k], d, core) for k in range(2)
        ]
        self.own = [
            remote(p(core, k), n(0, k), send.at[2 + k], recv.at[2 + k], d, core) for k in range(2)
        ]
        self.second = [
            remote(out.at[r[k]], far.at[r[k]], send.at[4 + k], recv.at[4 + k], d, across)
            for k in range(2)
        ]

    @staticmethod
    def scratch(rows):
        return [
            pltpu.VMEM((4 * rows, D), BF16),
            pltpu.VMEM((2 * rows, D), BF16),
            pltpu.VMEM((rows, D), BF16),
            pltpu.VMEM((rows, D), BF16),
            DMA((6,)),
            DMA((6,)),
        ]

    def start(self):
        for c in self.first + self.own:
            c.start()

    def middle(self):
        _, t = place()
        _, across, _ = tensor_peers(t)
        for k in range(2):
            self.first[k].wait_recv()
            self.out[self.rows[k]] = (
                self.part[block(across * 2 + k, self.half)].astype(F32)
                + self.near[pl.ds((2 + k) * self.half, self.half)].astype(F32)
            ).astype(BF16)
            self.second[k].start()

    def finish_half(self, k):
        _, t = place()
        self.own[k].wait_recv()
        self.second[k].wait_recv()
        return (
            self.part[block(t * 2 + k, self.half)].astype(F32)
            + self.near[pl.ds(k * self.half, self.half)].astype(F32)
            + self.far[self.rows[k]].astype(F32)
        )

    def drain(self):
        for c in self.first + self.own + self.second:
            c.wait_send()

    def finish(self):
        value = jnp.concatenate([self.finish_half(k) for k in range(2)], axis=0)
        self.drain()
        return value


def pair_peers():
    d, t = place()
    b, h, c = d % 2, t // 2, t % 2
    dx = d + 1 - 2 * b
    slot = lambda bb, hh, cc: bb * 4 + hh * 2 + cc
    return d, t, b, h, c, dx, slot


class PairGather:
    def __init__(self, buf, send, recv):
        self.buf, self.rows = buf, buf.shape[0] // 8
        d, t, b, h, c, dx, slot = pair_peers()
        half = self.rows // 2
        core, across = h * 2 + 1 - c, (1 - h) * 2 + c
        own, sx = slot(b, h, c), slot(1 - b, h, c)
        sy, sd = slot(b, 1 - h, c), slot(1 - b, 1 - h, c)

        def copy(i, s, k, dd, tt):
            ref = buf.at[block(s * 2 + k, half)]
            return remote(ref, ref, send.at[i], recv.at[i], dd, tt)

        self.own = own
        self.to_x = [copy(k, own, k, dx, t) for k in range(2)]
        self.to_y = [copy(2 + k, own, k, d, across) for k in range(2)]
        self.to_core = [copy(4 + k, own, k, d, core) for k in range(2)]
        self.x_to_y = copy(6, sx, 0, d, across)
        self.y_to_x = copy(7, sy, 1, dx, t)
        self.x_core = [copy(8 + k, sx, k, d, core) for k in range(2)]
        self.y_core = [copy(10 + k, sy, k, d, core) for k in range(2)]
        self.d_core = [copy(12 + k, sd, k, d, core) for k in range(2)]

    @staticmethod
    def scratch(rows):
        return [pltpu.VMEM((8 * rows, D), BF16), DMA((14,)), DMA((14,))]

    def start_half(self, k, value):
        self.buf[block(self.own * 2 + k, self.rows // 2)] = value
        order = [self.to_x[k], self.to_y[k]]
        for c in (order if k == 0 else order[::-1]) + [self.to_core[k]]:
            c.start()

    def start(self, value):
        half = self.rows // 2
        for k in range(2):
            self.start_half(k, value[k * half : (k + 1) * half])

    def forward(self):
        self.to_x[0].wait_recv()
        self.x_to_y.start()
        self.to_y[1].wait_recv()
        self.y_to_x.start()
        self.x_core[0].start()
        self.y_core[1].start()

    def relay(self):
        self.to_x[1].wait_recv()
        self.x_core[1].start()
        self.to_y[0].wait_recv()
        self.y_core[0].start()
        self.x_to_y.wait_recv()
        self.d_core[0].start()
        self.y_to_x.wait_recv()
        self.d_core[1].start()

    def ready(self, which):
        for c in {"own": self.to_core, "x": self.x_core, "y": self.y_core, "d": self.d_core}[which]:
            c.wait_recv()

    def drain(self):
        for c in self.to_x + self.to_y + [self.x_to_y, self.y_to_x]:
            c.wait_send()
        for c in self.to_core + self.x_core + self.y_core + self.d_core:
            c.wait_send()

    def finish(self):
        for which in ("own", "x", "y", "d"):
            self.ready(which)
        self.drain()


class PairScatter:
    def __init__(self, part, near, diag, out, far, send, recv):
        self.part, self.near, self.diag, self.out, self.far = part, near, diag, out, far
        d, t, b, h, c, dx, slot = pair_peers()
        rows = part.shape[0] // 8
        half = rows // 2
        self.rows, self.half = rows, half
        core, across = h * 2 + 1 - c, (1 - h) * 2 + c
        where = [(1 - b, 1 - h), (1 - b, h), (b, 1 - h), (b, h)]
        self.mine = [slot(bb, hh, c) for bb, hh in where]
        theirs = [slot(bb, hh, 1 - c) for bb, hh in where]
        self.first = [
            remote(
                part.at[block(theirs[i], rows)], near.at[pl.ds(i * rows, rows)],
                send.at[i], recv.at[i], d, core,
            )
            for i in range(4)
        ]

        def at(ref, i, k):
            return ref.at[pl.ds((i * 2 + k) * half, half)]

        self.diag_x = remote(at(out, 0, 0), at(diag, 0, 0), send.at[4], recv.at[4], dx, t)
        self.diag_y = remote(at(out, 0, 1), at(diag, 0, 1), send.at[5], recv.at[5], d, across)
        self.to_x = [
            remote(at(out, 1, k), at(far, 0, k), send.at[6 + k], recv.at[6 + k], dx, t)
            for k in range(2)
        ]
        self.to_y = [
            remote(at(out, 2, k), at(far, 1, k), send.at[8 + k], recv.at[8 + k], d, across)
            for k in range(2)
        ]

    @staticmethod
    def scratch(rows):
        return [
            pltpu.VMEM((8 * rows, D), BF16),
            pltpu.VMEM((4 * rows, D), BF16),
            pltpu.VMEM((rows, D), BF16),
            pltpu.VMEM((3 * rows, D), BF16),
            pltpu.VMEM((2 * rows, D), BF16),
            DMA((10,)),
            DMA((10,)),
        ]

    def start(self):
        for c in self.first:
            c.start()

    def pair(self, i, k):
        return (
            self.part[block(self.mine[i] * 2 + k, self.half)].astype(F32)
            + self.near[pl.ds((i * 2 + k) * self.half, self.half)].astype(F32)
        )

    def put(self, i, k, value):
        self.out[pl.ds((i * 2 + k) * self.half, self.half)] = value.astype(BF16)

    def send_diagonal(self):
        self.first[0].wait_recv()
        self.put(0, 0, self.pair(0, 0))
        self.diag_x.start()
        self.put(0, 1, self.pair(0, 1))
        self.diag_y.start()

    def send_x(self):
        self.first[1].wait_recv()
        self.put(1, 0, self.pair(1, 0))
        self.to_x[0].start()

    def send_y(self):
        self.first[2].wait_recv()
        self.put(2, 1, self.pair(2, 1))
        self.to_y[1].start()

    def middle(self):
        self.send_diagonal()
        self.send_x()
        self.send_y()

    def second(self):
        half = self.half
        self.diag_x.wait_recv()
        self.put(2, 0, self.pair(2, 0) + self.diag[pl.ds(0, half)].astype(F32))
        self.to_y[0].start()
        self.diag_y.wait_recv()
        self.put(1, 1, self.pair(1, 1) + self.diag[pl.ds(half, half)].astype(F32))
        self.to_x[1].start()

    def finish_half(self, k):
        self.to_x[k].wait_recv()
        self.to_y[k].wait_recv()
        if k == 0:
            self.first[3].wait_recv()
        half = self.half
        return (
            self.pair(3, k)
            + self.far[pl.ds(k * half, half)].astype(F32)
            + self.far[pl.ds((2 + k) * half, half)].astype(F32)
        )

    def drain(self):
        for c in self.first + [self.diag_x, self.diag_y] + self.to_x + self.to_y:
            c.wait_send()

    def finish(self):
        value = jnp.concatenate([self.finish_half(k) for k in range(2)], axis=0)
        self.drain()
        return value


class LineGather:
    def __init__(self, dp_count, buf, with_x, zsend, zrecv, xsend, xrecv, part=0, parts=1):
        self.buf, self.with_x, self.line_count = buf, with_x, dp_count // 2
        self.rows = buf.shape[0] // (dp_count if with_x else dp_count // 2)
        self.part, self.parts = part, parts
        self.zsend, self.zrecv, self.xsend, self.xrecv = zsend, zrecv, xsend, xrecv
        self.d, self.t = place()
        self.line, self.b = self.d // 2, self.d % 2

    @staticmethod
    def semaphores(dp_count):
        n = dp_count // 2
        return [DMA((2, n)), DMA((n,)), DMA((n,)), DMA((n,))]

    @staticmethod
    def scratch(dp_count, shape):
        return [pltpu.VMEM(shape, BF16)] + LineGather.semaphores(dp_count)

    def at(self, blk, b):
        slot = blk * 2 + b if self.with_x else blk
        return self.buf.at[block(slot * self.parts + self.part, self.rows // self.parts)]

    def zcopy(self, way, step, blk):
        ref = self.at(blk, self.b)
        return remote(
            ref, ref, self.zsend.at[way, step], self.zrecv.at[blk],
            (self.line + (1 if way == 0 else -1)) * 2 + self.b, self.t,
        )

    def xcopy(self, blk, b):
        ref = self.at(blk, b)
        return remote(
            ref, ref, self.xsend.at[blk], self.xrecv.at[blk],
            self.line * 2 + (1 - self.b), self.t,
        )

    def more(self, way):
        return (self.line + 1 < self.line_count) if way == 0 else (self.line > 0)

    def place(self, own):
        slot = self.d if self.with_x else self.line
        self.buf[block(slot, self.rows)] = own[...]

    def start(self):
        for way in range(2):

            @pl.when(self.more(way))
            def _():
                self.zcopy(way, 0, self.line).start()

        if self.with_x:
            self.xcopy(self.line, self.b).start()

    def hop(self, step, act, sending=False):
        for way in range(2):
            blk = self.line - step if way == 0 else self.line + step
            valid = (blk >= 0) if way == 0 else (blk < self.line_count)
            if sending:
                valid = valid & self.more(way)

            @pl.when(valid)
            def _():
                act(way, step, blk)

    def relay(self, step):
        def act(way, step, blk):
            self.zcopy(way, step, blk).wait_recv()

            @pl.when(self.more(way))
            def _():
                self.zcopy(way, step, blk).start()

            if self.with_x:
                self.xcopy(blk, self.b).start()

        self.hop(step, act)

    def finish(self):
        if self.with_x:

            def pair(blk, carry):
                self.xcopy(blk, 1 - self.b).wait_recv()
                return carry

            lax.fori_loop(0, self.line_count, pair, 0)

    def drain(self):
        def act(way, step, blk):
            self.zcopy(way, step, blk).wait_send()

        def step(i, carry):
            self.hop(i, act, sending=True)
            if self.with_x:
                self.xcopy(i, self.b).wait_send()
            return carry

        lax.fori_loop(0, self.line_count, step, 0)


def relay_range(items, first, last):
    def body(step, carry):
        for item in items:
            item.relay(step)
        return carry

    if first < last:
        lax.fori_loop(first, last, body, 0)


class LineReduce:
    def __init__(self, dp_count, with_x, grad, below, above, held, xsend, xrecv, zsend, zrecv):
        self.grad, self.below, self.above, self.with_x = grad, below, above, with_x
        self.held = held if with_x else grad
        self.xsend, self.xrecv, self.zsend, self.zrecv = xsend, xrecv, zsend, zrecv
        self.line_count = dp_count // 2
        self.rows = grad.shape[0] // (dp_count if with_x else self.line_count)
        self.d, self.t = place()
        self.line, self.b = self.d // 2, self.d % 2

    @staticmethod
    def scratch(dp_count, with_x, shape):
        n = dp_count // 2
        half = (shape[0] // 2, shape[1]) if with_x else shape
        held = half if with_x else (16, LANES)
        return [
            pltpu.VMEM(shape, BF16), pltpu.VMEM(half, BF16), pltpu.VMEM(half, BF16),
            pltpu.VMEM(held, BF16), DMA((n,)), DMA((n,)), DMA((n,)), DMA((2, n)),
        ]

    def xcopy(self, target):
        return remote(
            self.grad.at[block(target * 2 + (1 - self.b), self.rows)],
            self.held.at[block(target, self.rows)],
            self.xsend.at[target], self.xrecv.at[target],
            self.line * 2 + (1 - self.b), self.t,
        )

    def zcopy(self, way, target):
        dst = self.below if way == 0 else self.above
        return remote(
            self.held.at[block(target, self.rows)], dst.at[block(target, self.rows)],
            self.zsend.at[target], self.zrecv.at[way, target],
            (self.line + (1 if way == 0 else -1)) * 2 + self.b, self.t,
        )

    def each_target(self, act, first=0, stop=None):
        last = self.line_count - 1
        stop = last if stop is None else min(stop, last)

        def step(i, carry):
            @pl.when(last - i > self.line)
            def _():
                act(0, last - i)

            @pl.when(i < self.line)
            def _():
                act(1, i)

            return carry

        if first < stop:
            lax.fori_loop(first, stop, step, 0)

    def start(self):
        if self.with_x:

            def send(way, target):
                self.xcopy(target).start()

            self.each_target(send)
            send(0, self.line)

    def has(self, way):
        return (self.line > 0) if way == 0 else (self.line + 1 < self.line_count)

    def free(self):
        def send(way, target):
            @pl.when(jnp.logical_not(self.has(way)))
            def _():
                self.zcopy(way, target).start()

        self.each_target(send)

    def run(self, first=0, stop=None):
        def reduce(way, target):
            at = block(target, self.rows)
            dst = self.below if way == 0 else self.above
            if self.with_x:
                self.xcopy(target).wait_recv()
                mine = self.grad[block(target * 2 + self.b, self.rows)].astype(F32)

            @pl.when(self.has(way))
            def _():
                self.zcopy(way, target).wait_recv()
                total = self.held[at].astype(F32) + dst[at].astype(F32)
                if self.with_x:
                    total = total + mine
                self.held[at] = total.astype(BF16)
                if not self.with_x:
                    self.zcopy(way, target).start()

            if self.with_x:

                @pl.when(jnp.logical_not(self.has(way)))
                def _():
                    self.held[at] = (mine + self.held[at].astype(F32)).astype(BF16)

                self.zcopy(way, target).start()

        self.each_target(reduce, first, stop)

    def finish(self, put, add):
        at = block(self.line, self.rows)
        if self.with_x:
            self.xcopy(self.line).wait_recv()
            own = self.grad[block(self.d, self.rows)].astype(F32)
            put(own + self.held[at].astype(F32))
        else:
            put(self.grad[at].astype(F32))
        for way in range(2):

            @pl.when(self.has(way))
            def _():
                self.zcopy(way, self.line).wait_recv()
                add((self.below if way == 0 else self.above)[at].astype(F32))

    def drain(self):
        def act(way, target):
            self.zcopy(way, target).wait_send()
            if self.with_x:
                self.xcopy(target).wait_send()

        self.each_target(act)
        if self.with_x:
            self.xcopy(self.line).wait_send()


class Refs:
    def __init__(self):
        self.shapes, self.refs, self.at = [], None, 0

    def bind(self, refs):
        self.refs, self.at = refs, 0

    def take(self, shapes):
        if self.refs is None:
            self.shapes += shapes
            return [None] * len(shapes)
        got = self.refs[self.at : self.at + len(shapes)]
        self.at += len(shapes)
        return got


class Sizes:
    def __init__(self, dp_count, rows, group, qkv, dense, up, down):
        self.dp, self.lines, self.rows, self.group = dp_count, dp_count // 2, rows, group
        self.qkv_cols, self.heads = qkv[1], qkv[1] // (3 * HEAD)
        self.width = self.heads * HEAD
        self.split_up = len(up) == 2
        self.hidden = up[-1] // 2 if self.split_up else up[-1]
        self.qkv_rows, self.dense_rows, self.up_rows, self.down_rows = qkv[0], dense[0], up[-2], down[0]
        self.qkv_parts = 2 if qkv[0] % 32 == 0 else 1
        self.dense_whole = dense[0] == self.width
        self.piece = D // (dp_count * TENSOR)
        self.up_piece = 2 * self.hidden // dp_count
        self.qv_piece = 2 * self.width // dp_count


def scratch_of(s, pool):
    take = pool.take
    out = {}
    out["vsum"] = take(VectorExchange.scratch(s.dp, 1, D))
    out["vsum_out"] = take(VectorExchange.scratch(s.dp, s.dp, LANES))
    out["gather_x"] = take(TensorGather.scratch(s.rows))
    out["gather_low"] = take(TensorGather.scratch(s.rows))
    out["scatter_attn"] = take(TensorScatter.scratch(s.rows))
    out["scatter_in"] = take(TensorScatter.scratch(s.rows))
    out["gather_mlp"] = take(PairGather.scratch(s.rows))
    out["gather_og"] = take(PairGather.scratch(s.rows))
    out["scatter_mlp"] = take(PairScatter.scratch(s.rows))
    out["scatter_out"] = take(PairScatter.scratch(s.rows))
    out["w_qkv"] = take(LineGather.scratch(s.dp, (D, s.qkv_cols)))
    out["w_qkv_more"] = take(LineGather.semaphores(s.dp))
    out["w_dense"] = take(LineGather.scratch(s.dp, (s.width, D)))
    out["w_up"] = take(LineGather.scratch(s.dp, (D, s.hidden)))
    out["w_down"] = take(LineGather.scratch(s.dp, (s.hidden, D)))
    out["up_swap"] = take([DMA, DMA])
    out["g_qkv"] = take(LineReduce.scratch(s.dp, True, (D, s.qkv_cols)))
    out["g_dense"] = take(LineReduce.scratch(s.dp, True, (s.width, D)))
    out["g_up"] = take(LineReduce.scratch(s.dp, False, (D, s.hidden)))
    out["g_down"] = take(LineReduce.scratch(s.dp, False, (s.hidden, D)))
    out["g_swap"] = take(
        [
            pltpu.VMEM((2 * s.up_rows, s.hidden), F32),
            pltpu.VMEM((s.up_rows, s.hidden), BF16),
            pltpu.VMEM((s.up_rows, s.hidden), BF16),
            DMA,
            DMA,
        ]
    )
    out["data"] = take(
        [
            pltpu.VMEM((D, s.group), BF16),
            pltpu.VMEM((s.qkv_cols, s.group), BF16),
            pltpu.VMEM((s.heads, s.group, s.group), F32),
            pltpu.VMEM((s.width, s.group), BF16),
            pltpu.VMEM((s.width, s.group), BF16),
            pltpu.VMEM((s.qkv_cols, s.group), BF16),
            pltpu.VMEM((s.group, s.qkv_cols), BF16),
            pltpu.VMEM((2 * s.group, s.hidden), BF16),
            pltpu.VMEM((2 * s.group, s.hidden), F32),
            pltpu.VMEM((2 * s.group, s.hidden), BF16),
            pltpu.VMEM((s.rows, D), F32),
            pltpu.VMEM((s.rows, D), F32),
            pltpu.VMEM((s.rows, D), F32),
            pltpu.VMEM((VECTOR_ROWS, LANES), F32),
            pltpu.VMEM((2, s.up_rows, s.hidden), BF16),
            pltpu.VMEM((s.rows, D), F32),
            pltpu.VMEM((s.rows, D), F32),
        ]
    )
    return out


def loop(count, body):
    def step(i, carry):
        body(i)
        return carry

    lax.fori_loop(0, count, step, 0)


def block_kernel(s, refs_in):
    pool = Refs()
    scratch_of(s, pool)
    names_in, names_out = 8 + VECTOR_ROWS, 7
    (fill_ref, begin_ref, x_ref, og_ref, wq_ref, wd_ref, wu_ref, wn_ref) = refs_in[:8]
    vec_refs = refs_in[8:names_in]
    (block_out, input_grad, qkv_out, dense_out, up_out, down_out, vec_out) = refs_in[
        names_in : names_in + names_out
    ]
    pool.bind(refs_in[names_in + names_out :])
    got = scratch_of(s, pool)
    d, t = place()
    b = d % 2
    rows, group, hidden = s.rows, s.group, s.hidden
    (attn_in_t, qkv_t, probs_t, context_t, context_grad_t, qkv_grad_t, qkv_grad,
     active, slope, pre_grad, live_grad, middle, middle_grad, vec_in, up_halves, mid_normed, mid_up) = got["data"]

    vsum = VectorExchange(s.dp, *got["vsum"])
    vsum_out = VectorExchange(s.dp, *got["vsum_out"])
    attn_in, gx_send, gx_recv = got["gather_x"]
    gather_x = TensorGather(attn_in, gx_send, gx_recv)
    middle_low, gl_send, gl_recv = got["gather_low"]
    gather_low = TensorGather(middle_low, gl_send, gl_recv)
    scatter_attn = TensorScatter(*got["scatter_attn"])
    scatter_in = TensorScatter(*got["scatter_in"])
    mlp_in, gm_send, gm_recv = got["gather_mlp"]
    gather_mlp = PairGather(mlp_in, gm_send, gm_recv)
    out_low, go_send, go_recv = got["gather_og"]
    gather_og = PairGather(out_low, go_send, go_recv)
    scatter_mlp = PairScatter(*got["scatter_mlp"])
    scatter_out = PairScatter(*got["scatter_out"])
    qkv_sems = [got["w_qkv"][1:], got["w_qkv_more"]][: s.qkv_parts]
    w_qkv = [
        LineGather(s.dp, got["w_qkv"][0], True, *sems, part, s.qkv_parts)
        for part, sems in enumerate(qkv_sems)
    ]
    w_dense = LineGather(s.dp, got["w_dense"][0], True, *got["w_dense"][1:])
    w_up = LineGather(s.dp, got["w_up"][0], False, *got["w_up"][1:])
    w_down = LineGather(s.dp, got["w_down"][0], False, *got["w_down"][1:])
    g_qkv = LineReduce(s.dp, True, *got["g_qkv"])
    g_dense = LineReduce(s.dp, True, *got["g_dense"])
    g_up = LineReduce(s.dp, False, *got["g_up"])
    g_down = LineReduce(s.dp, False, *got["g_down"])
    w_dense = [] if s.dense_whole else [w_dense]
    w_up, w_down = [w_up], [w_down]
    halves = up_halves if s.split_up else wu_ref
    up_swap = remote(
        halves.at[1 - b], w_up[0].buf.at[block(d, s.up_rows)], got["up_swap"][0],
        got["up_swap"][1], d + 1 - 2 * b, t,
    )

    enter(s.dp)
    w_qkv[0].place(wq_ref)
    for w in w_dense:
        w.place(wd_ref)
    w_down[0].place(wn_ref)
    if s.split_up:
        for k in range(2 * hidden // LANES):
            up_halves[k % 2, :, (k // 2) * LANES : (k // 2 + 1) * LANES] = wu_ref[
                :, k * LANES : (k + 1) * LANES
            ]
    vec_in[...] = jnp.zeros(vec_in.shape, F32)
    for i, ref in enumerate(vec_refs):
        vec_in[i : i + 1, 0 : ref.shape[1]] = ref[...].astype(F32)
    row = lax.broadcasted_iota(jnp.int32, (VECTOR_ROWS, D), 0)

    def turn(value, first, second, third):
        return jnp.where(
            row < 6,
            pltpu.roll(value, first, 1),
            jnp.where(row == 6, pltpu.roll(value, second, 1), pltpu.roll(value, third, 1)),
        )

    def up_place(device):
        return (device % 2) * hidden + (device // 2) * s.up_piece

    def spread(value, device):
        wide = jnp.concatenate([value, jnp.zeros((VECTOR_ROWS, D - LANES), F32)], axis=1)
        return turn(
            wide, (device * TENSOR + t) * s.piece, up_place(device), device * s.qv_piece
        )

    def back(at):
        return lax.rem(D - at, D)

    entered(s.dp)
    vsum.start(lambda device: vec_in[...])
    for w in w_qkv + w_dense:
        w.start()
    up_swap.start()
    own_row = t * rows + lax.broadcasted_iota(jnp.int32, (rows, D), 0)
    live = og_ref[...] * (own_row < fill_ref[0]).astype(F32)
    live_grad[...] = live
    w_up[0].buf[block(d, s.up_rows)] = halves[b]
    x_normed, x_inverse = normalize(x_ref[...])
    vsum.middle(spread)
    relay_range(w_qkv, 1, 2)
    vec = vsum.finish()
    gather_x.start((x_normed * vec[0:1] + vec[1:2]).astype(BF16))
    relay_range(w_qkv, 2, 3)
    up_swap.wait()
    for w in w_up:
        w.start()
    relay_range(w_dense, 1, 2)
    gather_x.forward()
    relay_range(w_qkv, 3, s.lines)
    gather_og.start(live_grad[...].astype(BF16))
    relay_range(w_dense, 2, 3)
    for w in w_down:
        w.start()
    gather_x.finish()
    attn_in_t[...] = attn_in[...].T
    for w in w_qkv:
        w.finish()

    wq, wd = w_qkv[0].buf, (wd_ref if s.dense_whole else w_dense[0].buf)
    zero_bias = jnp.zeros((1, HEAD), F32)
    pieces = []
    for h in range(s.heads):
        at = 2 * h * HEAD
        pieces += [vec[7:8, at : at + HEAD], zero_bias, vec[7:8, at + HEAD : at + 2 * HEAD]]
    qkv_bias = jnp.concatenate(pieces, axis=1)

    def project(i):
        tile = block(i, 256)
        value = dot_nn(attn_in[tile], wq[...]) + qkv_bias
        qkv_t[:, tile] = value.astype(BF16).T

    loop(group // 256, project)
    relay_range(w_dense, 3, s.lines)

    def part_of(ref, h, which):
        return ref.at[block(3 * h + which, HEAD)]

    def attend(h):
        query = part_of(qkv_t, h, 0)
        key = part_of(qkv_t, h, 1)[...].T
        value = part_of(qkv_t, h, 2)
        head = (t * s.heads + h + 1).astype(F32)
        m = jnp.exp2(jnp.full((1, 256), -8.0 / HEADS, F32) * head)
        for i in range(group // 256):
            n = (i + 1) * 256
            cols = pl.ds(i * 256, 256)
            score = dot_nn(key[:n], query[:, cols]) * (1.0 / math.sqrt(HEAD))
            at_key = lax.broadcasted_iota(jnp.int32, (n, 256), 0)
            at_query = lax.broadcasted_iota(jnp.int32, (n, 256), 1) + i * 256
            score = score + m * (at_key - at_query).astype(F32)
            seen = (at_key >= begin_ref[:, cols]) & (at_key <= at_query)
            score = jnp.where(seen, score, MASKED_SCORE)
            weight = jnp.exp(score - jnp.max(score, axis=0, keepdims=True))
            weight = weight * (1.0 / jnp.sum(weight, axis=0, keepdims=True))
            probs_t[h, 0:n, cols] = weight
            context = dot_nn(value[:, 0:n], weight.astype(BF16))
            context_t[block(h, HEAD), cols] = context.astype(BF16)

    relay_range(w_up, 1, 2)
    loop(s.heads, attend)
    gather_og.forward()
    for w in w_dense:
        w.finish()

    part_attn = scatter_attn.part

    def project_out(i):
        tile = block(i, 256)
        part_attn[tile] = dot_tn(context_t[:, tile], wd[...]).astype(BF16)

    own_half = t // 2
    project_out(1 - own_half)
    for c in scatter_attn.first:
        c.start()
    project_out(own_half)
    for c in scatter_attn.own:
        c.start()
    gather_og.relay()
    relay_range(w_up, 2, 3)
    scatter_attn.middle()
    relay_range(w_down, 1, 2)
    half = rows // 2
    for k in range(2):
        at = pl.ds(k * half, half)
        mid = x_ref[at] + vec[2:3] + scatter_attn.finish_half(k)
        middle[at] = mid
        normed = normalize(mid)[0]
        gather_mlp.start_half(k, (normed * vec[3:4] + vec[4:5]).astype(BF16))
    gather_og.finish()
    gather_mlp.forward()
    relay_range(w_up, 3, s.lines)

    up, down = w_up[0].buf, w_down[0].buf
    up_bias = jnp.where(b == 0, vec[6:7, 0:hidden], vec[6:7, hidden : 2 * hidden])
    cubic, scale = 0.044715, math.sqrt(2.0 / math.pi)

    def forward(i):
        tile = block(i, 256)
        u = dot_nn(mlp_in[tile], up[...]) + up_bias
        square = u * u
        bend = jnp.tanh(scale * (u + cubic * (square * u)))
        active[tile] = (0.5 * u * (1.0 + bend)).astype(BF16)
        slope[tile] = 0.5 * (1.0 + bend) + (0.5 * scale) * u * (1.0 - bend * bend) * (
            1.0 + (3.0 * cubic) * square
        )

    chip = {
        "own": b * 2 + own_half, "x": (1 - b) * 2 + own_half,
        "y": b * 2 + 1 - own_half, "d": (1 - b) * 2 + 1 - own_half,
    }
    gather_mlp.ready("own")
    forward(chip["own"])
    gather_mlp.relay()
    for which in ("x", "y", "d"):
        gather_mlp.ready(which)
        forward(chip[which])
    relay_range(w_down, 2, 3)

    def down_gradient(i):
        cols = block(i, LANES)
        g_down.grad[cols] = dot_tn(active[:, cols], out_low[...]).astype(BF16)

    relay_range(w_down, 3, s.lines)

    def backward(i):
        tile = block(i, 256)
        grad = dot_nt(out_low[tile], down[...]) * slope[tile]
        low = grad.astype(BF16)
        pre_grad[tile] = low
        scatter_mlp.part[tile] = dot_nt(low, up[...]).astype(BF16)

    backward(chip["d"])
    scatter_mlp.first[0].start()
    backward(chip["x"])
    scatter_mlp.first[1].start()
    scatter_mlp.send_diagonal()
    backward(chip["y"])
    scatter_mlp.first[2].start()
    scatter_mlp.send_x()
    backward(chip["own"])
    scatter_mlp.first[3].start()
    scatter_mlp.send_y()
    loop(hidden // LANES, down_gradient)
    g_down.free()

    def up_gradient(i):
        cols = block(i, 256)
        g_up.grad[cols] = dot_tn(mlp_in[:, cols], pre_grad[...]).astype(BF16)

    scatter_mlp.second()
    loop(D // 256, up_gradient)
    g_up.free()

    def forward_out(i):
        tile = block(i, 256)
        scatter_out.part[tile] = dot_nn(active[tile], down[...]).astype(BF16)

    mid_normed[...], mid_inverse = normalize(middle[...])
    for k in range(2):
        at = pl.ds(k * half, half)
        upstream = scatter_mlp.finish_half(k)
        mid_up[at] = upstream
        grad = live_grad[at] + norm_backward(
            upstream, vec[3:4], mid_normed[at], mid_inverse[k * half : (k + 1) * half]
        )
        middle_grad[at] = grad
        gather_low.start_half(k, grad.astype(BF16))
    loop(2 * group // 256, forward_out)
    scatter_out.start()
    gather_low.forward()
    up_bias_grad = column_sum(pre_grad[...].astype(F32))
    sums = put_rows(
        jnp.zeros((VECTOR_ROWS, D), F32),
        [
            (2, column_sum(middle_grad[...])),
            (3, column_sum(mid_up[...] * mid_normed[...])),
            (4, column_sum(mid_up[...])),
            (5, column_sum(live_grad[...])),
        ],
    )
    scatter_out.middle()
    g_down.run()
    gather_low.finish()

    def dense_back(i):
        tile = block(i, 256)
        context_grad_t[:, tile] = dot_nt(wd[...], middle_low[tile]).astype(BF16)

    loop(group // 256, dense_back)
    dense_grad = dot_nn(context_t[...], middle_low[...])
    if s.dense_whole:
        dense_out[...] = dense_grad
    else:
        g_dense.grad[...] = dense_grad.astype(BF16)
        g_dense.start()
    root = 1.0 / math.sqrt(HEAD)

    def attend_back(h):
        at = block(h, HEAD)
        grad_t = context_grad_t[at]
        delta = column_sum(grad_t.astype(F32) * context_t[at].astype(F32))
        query, key = part_of(qkv_t, h, 0)[...], part_of(qkv_t, h, 1)[...]
        value = part_of(qkv_t, h, 2)[...].T
        query_grad, key_grad, value_grad = [], None, None
        for i in range(group // 256):
            n = (i + 1) * 256
            cols = slice(i * 256, n)
            probs = probs_t[h, 0:n, cols]
            score = (probs * (dot_nn(value[:n], grad_t[:, cols]) - delta[:, cols])).astype(BF16)
            query_grad.append(dot_nn(key[:, :n], score))
            key_part = dot_nt(query[:, cols], score)
            value_part = dot_nt(grad_t[:, cols], probs.astype(BF16))
            if i == 0:
                key_grad, value_grad = key_part, value_part
            else:
                wide = lambda v: jnp.concatenate(
                    [v, jnp.zeros((HEAD, n - v.shape[1]), F32)], axis=1
                )
                key_grad, value_grad = wide(key_grad) + key_part, wide(value_grad) + value_part
        part_of(qkv_grad_t, h, 0)[...] = (jnp.concatenate(query_grad, axis=1) * root).astype(BF16)
        part_of(qkv_grad_t, h, 1)[...] = (key_grad * root).astype(BF16)
        part_of(qkv_grad_t, h, 2)[...] = value_grad.astype(BF16)

    loop(s.heads, attend_back)
    scatter_out.second()
    qkv_grad[...] = qkv_grad_t[...].T

    def input_part(i):
        tile = block(i, 256)
        scatter_in.part[tile] = dot_nt(qkv_grad[tile], wq[...]).astype(BF16)

    pair_rows = 2 * s.qkv_rows

    def qkv_gradient(i):
        near = lax.rem(g_qkv.line + s.lines - 1 - i, s.lines)
        far = lax.rem(g_qkv.line + 1 + i, s.lines)
        target = jnp.where(2 * g_qkv.line < s.lines, near, far)
        tile = block(target, pair_rows)
        g_qkv.grad[tile] = dot_nn(attn_in_t[tile], qkv_grad[...]).astype(BF16)
        g_qkv.xcopy(target).start()

    loop(s.lines, qkv_gradient)
    input_part(1 - own_half)
    for c in scatter_in.first:
        c.start()
    input_part(own_half)
    for c in scatter_in.own:
        c.start()
    g_up.run()
    scatter_in.middle()
    if not s.dense_whole:
        g_dense.run()
    qkv_sum = column_sum(qkv_grad[...].astype(F32))
    qv_parts = []
    for h in range(s.heads):
        at = 3 * h * HEAD
        qv_parts += [qkv_sum[:, at : at + HEAD], qkv_sum[:, at + 2 * HEAD : at + 3 * HEAD]]
    qv_parts.append(jnp.zeros((1, D - 2 * s.width), F32))
    qv_grad = jnp.concatenate(qv_parts, axis=1)
    up_grad_row = jnp.concatenate(
        [jnp.where(b == 0, up_bias_grad, 0.0), jnp.where(b == 1, up_bias_grad, 0.0)], axis=1
    )
    x_normed, x_inverse = normalize(x_ref[...])
    upstream = scatter_in.finish()
    sums = put_rows(
        sums,
        [
            (0, column_sum(upstream * x_normed)),
            (1, column_sum(upstream)),
            (6, up_grad_row),
            (7, qv_grad),
        ],
    )
    vsum_out.start(
        lambda device: turn(
            sums, back(device * TENSOR * s.piece), back(up_place(device)),
            back(device * s.qv_piece),
        )[:, :LANES]
    )
    g_qkv.run(0, 1)
    input_grad[...] = middle_grad[...] + norm_backward(upstream, vec[0:1], x_normed, x_inverse)
    g_qkv.run(1, 2)
    vsum_out.middle(lambda value, device: value)
    g_qkv.run(2)

    def keep(ref):
        def put(value):
            ref[...] = value

        def add(value):
            ref[...] += value

        return put, add

    swap_sum, swap_send, swap_recv, ssem, rsem = got["g_swap"]
    g_down.finish(*keep(down_out))
    g_up.finish(*keep(swap_sum))
    swap_send[...] = swap_sum[block(1 - b, s.up_rows)].astype(BF16)
    swap = remote(swap_send, swap_recv, ssem, rsem, d + 1 - 2 * b, t)
    swap.start()

    def put_up(parity, value):
        if s.split_up:
            for k in range(hidden // LANES):
                at = pl.multiple_of((2 * k + parity) * LANES, LANES)
                up_out[:, pl.ds(at, LANES)] = value[:, k * LANES : (k + 1) * LANES]
        else:
            up_out[parity] = value

    put_up(b, swap_sum[block(b, s.up_rows)])
    block_out[...] = middle[...] + scatter_out.finish() + vec[5:6]
    if not s.dense_whole:
        g_dense.finish(*keep(dense_out))
    g_qkv.finish(*keep(qkv_out))
    swap.wait()
    put_up(1 - b, swap_recv[...].astype(F32))
    total = vsum_out.finish()
    turned = pltpu.roll(total, lax.rem(LANES - t * s.piece, LANES), 1)
    vec_out[...] = jnp.where(row[:, :LANES] < 6, turned, total)
    for c in (gather_mlp, scatter_mlp, scatter_attn):
        c.drain()
    for w in w_qkv + w_dense + w_up + w_down:
        w.drain()
    g_down.drain()
    g_up.drain()
    if not s.dense_whole:
        g_dense.drain()
    g_qkv.drain()


def block_call(s, *args):
    shape = jax.ShapeDtypeStruct
    pool = Refs()
    scratch_of(s, pool)
    vmem = pl.BlockSpec(memory_space=pltpu.VMEM)
    smem = pl.BlockSpec(memory_space=pltpu.SMEM)
    dense = (s.width if s.dense_whole else s.dense_rows, D)
    up = (s.up_rows, 2 * s.hidden) if s.split_up else (2, s.up_rows, s.hidden)
    return pl.pallas_call(
        lambda *refs: block_kernel(s, refs),
        out_shape=[
            shape((s.rows, D), F32),
            shape((s.rows, D), F32),
            shape((s.qkv_rows, s.qkv_cols), F32),
            shape(dense, F32),
            shape(up, F32),
            shape((s.down_rows, D), F32),
            shape((VECTOR_ROWS, LANES), F32),
        ],
        in_specs=[smem] + [vmem] * (len(args) - 1),
        out_specs=[vmem] * 7,
        scratch_shapes=pool.shapes,
        compiler_params=pltpu.CompilerParams(
            collective_id=1, has_side_effects=True, vmem_limit_bytes=62 * 1024 * 1024
        ),
        name="block_both_ways",
    )(*args)


def hand_out(arrays, table, pieces):
    n, m = len(arrays), len(pieces)

    def kernel(*refs):
        sources, table_ref = refs[:n], refs[n]
        targets, small = refs[n + 1 : 2 * n + 1], refs[2 * n + 1 : 2 * n + 1 + m]
        for i in range(m):
            small[i][...] = table_ref[i : i + 1, 0 : pieces[i]]
        held, sem_in, sem_out = refs[2 * n + 1 + m : -2], refs[-2], refs[-1]
        arrive = [
            pltpu.make_async_copy(a, h, sem_in.at[i]) for i, (a, h) in enumerate(zip(sources, held))
        ]
        leave = [
            pltpu.make_async_copy(h, o, sem_out.at[i]) for i, (h, o) in enumerate(zip(held, targets))
        ]
        for c in arrive:
            c.start()
        for c, e in zip(arrive, leave):
            c.wait()
            e.start()
        for e in leave:
            e.wait()

    shape = jax.ShapeDtypeStruct
    anywhere = pl.BlockSpec(memory_space=pl.ANY)
    vmem = pl.BlockSpec(memory_space=pltpu.VMEM)
    outs = pl.pallas_call(
        kernel,
        out_shape=[shape(a.shape, F32) for a in arrays] + [shape((1, p), F32) for p in pieces],
        in_specs=[anywhere] * n + [vmem],
        out_specs=[anywhere] * n + [vmem] * m,
        scratch_shapes=[pltpu.VMEM(a.shape, F32) for a in arrays] + [DMA((n,)), DMA((n,))],
        name="hand_out",
    )(*arrays, table)
    return outs[:n], [o.reshape(-1) for o in outs[n:]]


def per_device(
    dp_count,
    block_input,
    seq_begin,
    group_fill,
    attention_norm_gain,
    attention_norm_bias,
    qkv_weight,
    qv_bias,
    dense_weight,
    dense_bias,
    feedforward_norm_gain,
    feedforward_norm_bias,
    up_weight,
    up_bias,
    down_weight,
    down_bias,
    out_grad,
):
    vectors = [
        attention_norm_gain,
        attention_norm_bias,
        dense_bias,
        feedforward_norm_gain,
        feedforward_norm_bias,
        down_bias,
        up_bias,
        qv_bias,
    ]
    up_rows, up_cols = up_weight.shape
    lines, piece = dp_count // 2, up_bias.shape[0]
    in_place = piece % LANES == 0
    up_split = up_weight
    if not in_place:
        up_split = up_weight.reshape(up_rows, lines, 2, piece).transpose(2, 0, 1, 3)
        up_split = up_split.reshape(2, up_rows, up_cols // 2)
    whole = dense_weight.shape[0] % 16 != 0
    dense = lax.all_gather(dense_weight, "dp", axis=0, tiled=True) if whole else dense_weight
    s = Sizes(
        dp_count, block_input.shape[0], seq_begin.shape[0], qkv_weight.shape, dense.shape,
        up_split.shape, down_weight.shape,
    )
    *arrays, table = block_call(
        s, group_fill, seq_begin[None], block_input, out_grad, qkv_weight, dense, up_split,
        down_weight, *[v[None] for v in vectors],
    )
    arrays, small = hand_out(arrays, table, [v.shape[0] for v in vectors])
    block_out, input_grad, qkv_out, dense_out, up_out, down_out = arrays
    if whole:
        dense_out = lax.psum_scatter(dense_out, "dp", scatter_dimension=0, tiled=True)
    if not in_place:
        up_out = up_out.reshape(2, up_rows, lines, piece).transpose(1, 2, 0, 3)
        up_out = up_out.reshape(up_rows, up_cols)
    return (
        block_out,
        input_grad,
        small[0],
        small[1],
        qkv_out,
        small[7],
        dense_out,
        small[2],
        small[3],
        small[4],
        up_out,
        small[6],
        down_out,
        small[5],
    )


def solution(mesh):
    rows, line = P(("dp", "tensor"), None), P(("dp", "tensor"))
    inner, columns = P(("tensor", "dp")), P("dp", "tensor")
    inner_rows = P(("tensor", "dp"), None)
    return jax.shard_map(
        functools.partial(per_device, mesh.shape["dp"]),
        mesh=mesh,
        in_specs=(
            rows, P("dp"), P("dp"), line, line, columns, inner, inner_rows, line, line, line,
            columns, inner, inner_rows, line, rows,
        ),
        out_specs=(
            rows, rows, line, line, columns, inner, inner_rows, line, line, line, columns, inner,
            inner_rows, line,
        ),
        check_vma=False,
    )
```

```python
import functools
import math

import jax
import jax.numpy as jnp
from jax import lax
from jax.experimental import pallas as pl
from jax.experimental.pallas import tpu as pltpu
from jax.sharding import PartitionSpec as P

D = 1024
HEADS = 16
HEAD = D // HEADS
TENSOR = 4
EPSILON = 1e-05
MASKED_SCORE = -1e30
MESH = pl.DeviceIdType.MESH
VECTOR_ROWS = 8
LANES = 128
BF16 = jnp.bfloat16
F32 = jnp.float32
DMA = pltpu.SemaphoreType.DMA


def dot_nn(a, b):
    return lax.dot_general(a, b, (((1,), (0,)), ((), ())), preferred_element_type=F32)


def dot_nt(a, b):
    return lax.dot_general(a, b, (((1,), (1,)), ((), ())), preferred_element_type=F32)


def dot_tn(a, b):
    return lax.dot_general(a, b, (((0,), (0,)), ((), ())), preferred_element_type=F32)


def normalize(hidden):
    centred = hidden - jnp.mean(hidden, axis=-1, keepdims=True)
    inverse = lax.rsqrt(jnp.mean(centred * centred, axis=-1, keepdims=True) + EPSILON)
    return centred * inverse, inverse


def norm_backward(upstream, gain, normed, inverse):
    scaled = upstream * gain
    return inverse * (
        scaled
        - jnp.mean(scaled, axis=-1, keepdims=True)
        - normed * jnp.mean(scaled * normed, axis=-1, keepdims=True)
    )


def column_sum(value):
    return jnp.sum(value, axis=0, keepdims=True)


def put_rows(base, values):
    row = lax.broadcasted_iota(jnp.int32, base.shape, 0)
    for index, value in values:
        base = jnp.where(row == index, value, base)
    return base


def place():
    return lax.axis_index("dp"), lax.axis_index("tensor")


def tensor_peers(t):
    h, c = t // 2, t % 2
    core = h * 2 + (1 - c)
    across = (1 - h) * 2 + c
    diagonal = (1 - h) * 2 + (1 - c)
    return core, across, diagonal


def block(start, rows):
    return pl.ds(pl.multiple_of(start * rows, rows), rows)


def enter(dp_count):
    d, t = place()
    barrier = pltpu.get_barrier_semaphore()
    for j in range(1, 4):
        pl.semaphore_signal(
            barrier, inc=1, device_id=(d, lax.rem(t + j, 4)), device_id_type=MESH
        )

    def greet(j, carry):
        pl.semaphore_signal(
            barrier, inc=1, device_id=(lax.rem(d + j, dp_count), t), device_id_type=MESH
        )
        return carry

    lax.fori_loop(1, dp_count, greet, 0)


def entered(dp_count):
    pl.semaphore_wait(pltpu.get_barrier_semaphore(), 3 + dp_count - 1)


def remote(src, dst, send, recv, d, t):
    return pltpu.make_async_remote_copy(
        src_ref=src, dst_ref=dst, send_sem=send, recv_sem=recv, device_id=(d, t), device_id_type=MESH
    )


class VectorExchange:
    def __init__(self, dp_count, dout, din, tbuf, dsend, drecv, tsend, trecv):
        self.dp_count = dp_count
        self.dout, self.din, self.tbuf = dout, din, tbuf
        self.dsend, self.drecv, self.tsend, self.trecv = dsend, drecv, tsend, trecv

    @staticmethod
    def scratch(dp_count, outgoing, width):
        return [
            pltpu.VMEM((outgoing, VECTOR_ROWS, LANES), F32),
            pltpu.VMEM((dp_count, VECTOR_ROWS, LANES), F32),
            pltpu.VMEM((4, VECTOR_ROWS, width), F32),
            DMA((dp_count,)),
            DMA((dp_count,)),
            DMA((4,)),
            DMA((4,)),
        ]

    def peer(self, j):
        return lax.rem(place()[0] + j, self.dp_count)

    def source(self, j):
        return lax.rem(place()[0] + self.dp_count - j, self.dp_count)

    def dcopy(self, j):
        out = self.dout.at[j] if self.dout.shape[0] > 1 else self.dout.at[0]
        return remote(
            out, self.din.at[j], self.dsend.at[j], self.drecv.at[j], self.peer(j), place()[1]
        )

    def tcopy(self, j):
        d, t = place()
        return remote(
            self.tbuf.at[0], self.tbuf.at[j], self.tsend.at[j], self.trecv.at[j],
            d, lax.rem(t + j, 4),
        )

    def start(self, block_for):
        def go(j, carry):
            value = block_for(self.peer(j))
            if self.dout.shape[0] > 1:
                self.dout[j] = value
            self.dcopy(j).start()
            return carry

        self.din[0] = block_for(place()[0])
        if self.dout.shape[0] == 1:
            self.dout[0] = block_for(place()[0])
        lax.fori_loop(1, self.dp_count, go, 0)

    def middle(self, spread):
        def wait(j, carry):
            self.dcopy(j).wait()
            return carry

        lax.fori_loop(1, self.dp_count, wait, 0)

        def add(j, total):
            return total + spread(self.din[j], self.source(j))

        self.tbuf[0] = lax.fori_loop(0, self.dp_count, add, jnp.zeros(self.tbuf.shape[1:], F32))
        for j in range(1, 4):
            self.tcopy(j).start()

    def finish(self):
        for j in range(1, 4):
            self.tcopy(j).wait()
        own = self.tbuf[0]
        total = own + self.tbuf[1] + self.tbuf[2] + self.tbuf[3]
        row = lax.broadcasted_iota(jnp.int32, own.shape, 0)
        return jnp.where(row < 6, total, own)


class TensorGather:
    def __init__(self, buf, send, recv):
        self.buf, self.rows = buf, buf.shape[0] // 4
        d, t = place()
        core, across, _ = tensor_peers(t)
        half = self.rows // 2
        at = lambda s, k: buf.at[block(s * 2 + k, half)]
        self.to_across = [
            remote(at(t, k), at(t, k), send.at[k], recv.at[k], d, across) for k in range(2)
        ]
        self.to_core = [
            remote(at(t, k), at(t, k), send.at[2 + k], recv.at[2 + k], d, core) for k in range(2)
        ]
        self.relay = [
            remote(at(across, k), at(across, k), send.at[4 + k], recv.at[4 + k], d, core)
            for k in range(2)
        ]

    @staticmethod
    def scratch(rows):
        return [pltpu.VMEM((4 * rows, D), BF16), DMA((6,)), DMA((6,))]

    def start_half(self, k, value):
        _, t = place()
        self.buf[block(t * 2 + k, self.rows // 2)] = value
        self.to_across[k].start()
        self.to_core[k].start()

    def start(self, value):
        half = self.rows // 2
        for k in range(2):
            self.start_half(k, value[k * half : (k + 1) * half])

    def forward(self):
        for k in range(2):
            self.to_across[k].wait_recv()
            self.relay[k].start()

    def finish(self):
        for c in self.to_across:
            c.wait_send()
        for c in self.to_core + self.relay:
            c.wait()


class TensorScatter:
    def __init__(self, part, near, far, out, send, recv):
        self.part, self.near, self.far, self.out = part, near, far, out
        d, t = place()
        core, across, diagonal = tensor_peers(t)
        self.count = far.shape[0]
        half = self.count // 2
        self.half = half
        p = lambda s, k: part.at[block(s * 2 + k, half)]
        n = lambda s, k: near.at[pl.ds((s * 2 + k) * half, half)]
        r = [pl.ds(k * half, half) for k in range(2)]
        self.rows = r
        self.first = [
            remote(p(diagonal, k), n(1, k), send.at[k], recv.at[k], d, core) for k in range(2)
        ]
        self.own = [
            remote(p(core, k), n(0, k), send.at[2 + k], recv.at[2 + k], d, core) for k in range(2)
        ]
        self.second = [
            remote(out.at[r[k]], far.at[r[k]], send.at[4 + k], recv.at[4 + k], d, across)
            for k in range(2)
        ]

    @staticmethod
    def scratch(rows):
        return [
            pltpu.VMEM((4 * rows, D), BF16),
            pltpu.VMEM((2 * rows, D), BF16),
            pltpu.VMEM((rows, D), BF16),
            pltpu.VMEM((rows, D), BF16),
            DMA((6,)),
            DMA((6,)),
        ]

    def start(self):
        for c in self.first + self.own:
            c.start()

    def middle(self):
        _, t = place()
        _, across, _ = tensor_peers(t)
        for k in range(2):
            self.first[k].wait_recv()
            self.out[self.rows[k]] = (
                self.part[block(across * 2 + k, self.half)].astype(F32)
                + self.near[pl.ds((2 + k) * self.half, self.half)].astype(F32)
            ).astype(BF16)
            self.second[k].start()

    def finish_half(self, k):
        _, t = place()
        self.own[k].wait_recv()
        self.second[k].wait_recv()
        return (
            self.part[block(t * 2 + k, self.half)].astype(F32)
            + self.near[pl.ds(k * self.half, self.half)].astype(F32)
            + self.far[self.rows[k]].astype(F32)
        )

    def drain(self):
        for c in self.first + self.own + self.second:
            c.wait_send()

    def finish(self):
        value = jnp.concatenate([self.finish_half(k) for k in range(2)], axis=0)
        self.drain()
        return value


def pair_peers():
    d, t = place()
    b, h, c = d % 2, t // 2, t % 2
    dx = d + 1 - 2 * b
    slot = lambda bb, hh, cc: bb * 4 + hh * 2 + cc
    return d, t, b, h, c, dx, slot


class PairGather:
    def __init__(self, buf, send, recv):
        self.buf, self.rows = buf, buf.shape[0] // 8
        d, t, b, h, c, dx, slot = pair_peers()
        half = self.rows // 2
        core, across = h * 2 + 1 - c, (1 - h) * 2 + c
        own, sx = slot(b, h, c), slot(1 - b, h, c)
        sy, sd = slot(b, 1 - h, c), slot(1 - b, 1 - h, c)

        def copy(i, s, k, dd, tt):
            ref = buf.at[block(s * 2 + k, half)]
            return remote(ref, ref, send.at[i], recv.at[i], dd, tt)

        self.own = own
        self.to_x = [copy(k, own, k, dx, t) for k in range(2)]
        self.to_y = [copy(2 + k, own, k, d, across) for k in range(2)]
        self.to_core = [copy(4 + k, own, k, d, core) for k in range(2)]
        self.x_to_y = copy(6, sx, 0, d, across)
        self.y_to_x = copy(7, sy, 1, dx, t)
        self.x_core = [copy(8 + k, sx, k, d, core) for k in range(2)]
        self.y_core = [copy(10 + k, sy, k, d, core) for k in range(2)]
        self.d_core = [copy(12 + k, sd, k, d, core) for k in range(2)]

    @staticmethod
    def scratch(rows):
        return [pltpu.VMEM((8 * rows, D), BF16), DMA((14,)), DMA((14,))]

    def start_half(self, k, value):
        self.buf[block(self.own * 2 + k, self.rows // 2)] = value
        order = [self.to_x[k], self.to_y[k]]
        for c in (order if k == 0 else order[::-1]) + [self.to_core[k]]:
            c.start()

    def start(self, value):
        half = self.rows // 2
        for k in range(2):
            self.start_half(k, value[k * half : (k + 1) * half])

    def forward(self):
        self.to_x[0].wait_recv()
        self.x_to_y.start()
        self.to_y[1].wait_recv()
        self.y_to_x.start()
        self.x_core[0].start()
        self.y_core[1].start()

    def relay(self):
        self.to_x[1].wait_recv()
        self.x_core[1].start()
        self.to_y[0].wait_recv()
        self.y_core[0].start()
        self.x_to_y.wait_recv()
        self.d_core[0].start()
        self.y_to_x.wait_recv()
        self.d_core[1].start()

    def ready(self, which):
        for c in {"own": self.to_core, "x": self.x_core, "y": self.y_core, "d": self.d_core}[which]:
            c.wait_recv()

    def drain(self):
        for c in self.to_x + self.to_y + [self.x_to_y, self.y_to_x]:
            c.wait_send()
        for c in self.to_core + self.x_core + self.y_core + self.d_core:
            c.wait_send()

    def finish(self):
        for which in ("own", "x", "y", "d"):
            self.ready(which)
        self.drain()


class PairScatter:
    def __init__(self, part, near, diag, out, far, send, recv):
        self.part, self.near, self.diag, self.out, self.far = part, near, diag, out, far
        d, t, b, h, c, dx, slot = pair_peers()
        rows = part.shape[0] // 8
        half = rows // 2
        self.rows, self.half = rows, half
        core, across = h * 2 + 1 - c, (1 - h) * 2 + c
        where = [(1 - b, 1 - h), (1 - b, h), (b, 1 - h), (b, h)]
        self.mine = [slot(bb, hh, c) for bb, hh in where]
        theirs = [slot(bb, hh, 1 - c) for bb, hh in where]
        self.first = [
            remote(
                part.at[block(theirs[i], rows)], near.at[pl.ds(i * rows, rows)],
                send.at[i], recv.at[i], d, core,
            )
            for i in range(4)
        ]

        def at(ref, i, k):
            return ref.at[pl.ds((i * 2 + k) * half, half)]

        self.diag_x = remote(at(out, 0, 0), at(diag, 0, 0), send.at[4], recv.at[4], dx, t)
        self.diag_y = remote(at(out, 0, 1), at(diag, 0, 1), send.at[5], recv.at[5], d, across)
        self.to_x = [
            remote(at(out, 1, k), at(far, 0, k), send.at[6 + k], recv.at[6 + k], dx, t)
            for k in range(2)
        ]
        self.to_y = [
            remote(at(out, 2, k), at(far, 1, k), send.at[8 + k], recv.at[8 + k], d, across)
            for k in range(2)
        ]

    @staticmethod
    def scratch(rows):
        return [
            pltpu.VMEM((8 * rows, D), BF16),
            pltpu.VMEM((4 * rows, D), BF16),
            pltpu.VMEM((rows, D), BF16),
            pltpu.VMEM((3 * rows, D), BF16),
            pltpu.VMEM((2 * rows, D), BF16),
            DMA((10,)),
            DMA((10,)),
        ]

    def start(self):
        for c in self.first:
            c.start()

    def pair(self, i, k):
        return (
            self.part[block(self.mine[i] * 2 + k, self.half)].astype(F32)
            + self.near[pl.ds((i * 2 + k) * self.half, self.half)].astype(F32)
        )

    def put(self, i, k, value):
        self.out[pl.ds((i * 2 + k) * self.half, self.half)] = value.astype(BF16)

    def send_diagonal(self):
        self.first[0].wait_recv()
        self.put(0, 0, self.pair(0, 0))
        self.diag_x.start()
        self.put(0, 1, self.pair(0, 1))
        self.diag_y.start()

    def send_x(self):
        self.first[1].wait_recv()
        self.put(1, 0, self.pair(1, 0))
        self.to_x[0].start()

    def send_y(self):
        self.first[2].wait_recv()
        self.put(2, 1, self.pair(2, 1))
        self.to_y[1].start()

    def middle(self):
        self.send_diagonal()
        self.send_x()
        self.send_y()

    def second(self):
        half = self.half
        self.diag_x.wait_recv()
        self.put(2, 0, self.pair(2, 0) + self.diag[pl.ds(0, half)].astype(F32))
        self.to_y[0].start()
        self.diag_y.wait_recv()
        self.put(1, 1, self.pair(1, 1) + self.diag[pl.ds(half, half)].astype(F32))
        self.to_x[1].start()

    def finish_half(self, k):
        self.to_x[k].wait_recv()
        self.to_y[k].wait_recv()
        if k == 0:
            self.first[3].wait_recv()
        half = self.half
        return (
            self.pair(3, k)
            + self.far[pl.ds(k * half, half)].astype(F32)
            + self.far[pl.ds((2 + k) * half, half)].astype(F32)
        )

    def drain(self):
        for c in self.first + [self.diag_x, self.diag_y] + self.to_x + self.to_y:
            c.wait_send()

    def finish(self):
        value = jnp.concatenate([self.finish_half(k) for k in range(2)], axis=0)
        self.drain()
        return value


class LineGather:
    def __init__(self, dp_count, buf, with_x, zsend, zrecv, xsend, xrecv, part=0, parts=1):
        self.buf, self.with_x, self.line_count = buf, with_x, dp_count // 2
        self.rows = buf.shape[0] // (dp_count if with_x else dp_count // 2)
        self.part, self.parts = part, parts
        self.zsend, self.zrecv, self.xsend, self.xrecv = zsend, zrecv, xsend, xrecv
        self.d, self.t = place()
        self.line, self.b = self.d // 2, self.d % 2

    @staticmethod
    def semaphores(dp_count):
        n = dp_count // 2
        return [DMA((2, n)), DMA((n,)), DMA((n,)), DMA((n,))]

    @staticmethod
    def scratch(dp_count, shape):
        return [pltpu.VMEM(shape, BF16)] + LineGather.semaphores(dp_count)

    def at(self, blk, b):
        slot = blk * 2 + b if self.with_x else blk
        return self.buf.at[block(slot * self.parts + self.part, self.rows // self.parts)]

    def zcopy(self, way, step, blk):
        ref = self.at(blk, self.b)
        return remote(
            ref, ref, self.zsend.at[way, step], self.zrecv.at[blk],
            (self.line + (1 if way == 0 else -1)) * 2 + self.b, self.t,
        )

    def xcopy(self, blk, b):
        ref = self.at(blk, b)
        return remote(
            ref, ref, self.xsend.at[blk], self.xrecv.at[blk],
            self.line * 2 + (1 - self.b), self.t,
        )

    def more(self, way):
        return (self.line + 1 < self.line_count) if way == 0 else (self.line > 0)

    def place(self, own):
        slot = self.d if self.with_x else self.line
        self.buf[block(slot, self.rows)] = own[...]

    def start(self):
        for way in range(2):

            @pl.when(self.more(way))
            def _():
                self.zcopy(way, 0, self.line).start()

        if self.with_x:
            self.xcopy(self.line, self.b).start()

    def hop(self, step, act, sending=False):
        for way in range(2):
            blk = self.line - step if way == 0 else self.line + step
            valid = (blk >= 0) if way == 0 else (blk < self.line_count)
            if sending:
                valid = valid & self.more(way)

            @pl.when(valid)
            def _():
                act(way, step, blk)

    def relay(self, step):
        def act(way, step, blk):
            self.zcopy(way, step, blk).wait_recv()

            @pl.when(self.more(way))
            def _():
                self.zcopy(way, step, blk).start()

            if self.with_x:
                self.xcopy(blk, self.b).start()

        self.hop(step, act)

    def finish(self):
        if self.with_x:

            def pair(blk, carry):
                self.xcopy(blk, 1 - self.b).wait_recv()
                return carry

            lax.fori_loop(0, self.line_count, pair, 0)

    def drain(self):
        def act(way, step, blk):
            self.zcopy(way, step, blk).wait_send()

        def step(i, carry):
            self.hop(i, act, sending=True)
            if self.with_x:
                self.xcopy(i, self.b).wait_send()
            return carry

        lax.fori_loop(0, self.line_count, step, 0)


def relay_range(items, first, last):
    def body(step, carry):
        for item in items:
            item.relay(step)
        return carry

    if first < last:
        lax.fori_loop(first, last, body, 0)


class LineReduce:
    def __init__(self, dp_count, with_x, grad, below, above, held, xsend, xrecv, zsend, zrecv):
        self.grad, self.below, self.above, self.with_x = grad, below, above, with_x
        self.held = held if with_x else grad
        self.xsend, self.xrecv, self.zsend, self.zrecv = xsend, xrecv, zsend, zrecv
        self.line_count = dp_count // 2
        self.rows = grad.shape[0] // (dp_count if with_x else self.line_count)
        self.d, self.t = place()
        self.line, self.b = self.d // 2, self.d % 2

    @staticmethod
    def scratch(dp_count, with_x, shape):
        n = dp_count // 2
        half = (shape[0] // 2, shape[1]) if with_x else shape
        held = half if with_x else (16, LANES)
        return [
            pltpu.VMEM(shape, BF16), pltpu.VMEM(half, BF16), pltpu.VMEM(half, BF16),
            pltpu.VMEM(held, BF16), DMA((n,)), DMA((n,)), DMA((n,)), DMA((2, n)),
        ]

    def xcopy(self, target):
        return remote(
            self.grad.at[block(target * 2 + (1 - self.b), self.rows)],
            self.held.at[block(target, self.rows)],
            self.xsend.at[target], self.xrecv.at[target],
            self.line * 2 + (1 - self.b), self.t,
        )

    def zcopy(self, way, target):
        dst = self.below if way == 0 else self.above
        return remote(
            self.held.at[block(target, self.rows)], dst.at[block(target, self.rows)],
            self.zsend.at[target], self.zrecv.at[way, target],
            (self.line + (1 if way == 0 else -1)) * 2 + self.b, self.t,
        )

    def each_target(self, act, first=0, stop=None):
        last = self.line_count - 1
        stop = last if stop is None else min(stop, last)

        def step(i, carry):
            @pl.when(last - i > self.line)
            def _():
                act(0, last - i)

            @pl.when(i < self.line)
            def _():
                act(1, i)

            return carry

        if first < stop:
            lax.fori_loop(first, stop, step, 0)

    def start(self):
        if self.with_x:

            def send(way, target):
                self.xcopy(target).start()

            self.each_target(send)
            send(0, self.line)

    def has(self, way):
        return (self.line > 0) if way == 0 else (self.line + 1 < self.line_count)

    def free(self):
        def send(way, target):
            @pl.when(jnp.logical_not(self.has(way)))
            def _():
                self.zcopy(way, target).start()

        self.each_target(send)

    def run(self, first=0, stop=None):
        def reduce(way, target):
            at = block(target, self.rows)
            dst = self.below if way == 0 else self.above
            if self.with_x:
                self.xcopy(target).wait_recv()
                mine = self.grad[block(target * 2 + self.b, self.rows)].astype(F32)

            @pl.when(self.has(way))
            def _():
                self.zcopy(way, target).wait_recv()
                total = self.held[at].astype(F32) + dst[at].astype(F32)
                if self.with_x:
                    total = total + mine
                self.held[at] = total.astype(BF16)
                if not self.with_x:
                    self.zcopy(way, target).start()

            if self.with_x:

                @pl.when(jnp.logical_not(self.has(way)))
                def _():
                    self.held[at] = (mine + self.held[at].astype(F32)).astype(BF16)

                self.zcopy(way, target).start()

        self.each_target(reduce, first, stop)

    def finish(self, put, add):
        at = block(self.line, self.rows)
        if self.with_x:
            self.xcopy(self.line).wait_recv()
            own = self.grad[block(self.d, self.rows)].astype(F32)
            put(own + self.held[at].astype(F32))
        else:
            put(self.grad[at].astype(F32))
        for way in range(2):

            @pl.when(self.has(way))
            def _():
                self.zcopy(way, self.line).wait_recv()
                add((self.below if way == 0 else self.above)[at].astype(F32))

    def drain(self):
        def act(way, target):
            self.zcopy(way, target).wait_send()
            if self.with_x:
                self.xcopy(target).wait_send()

        self.each_target(act)
        if self.with_x:
            self.xcopy(self.line).wait_send()


class Refs:
    def __init__(self):
        self.shapes, self.refs, self.at = [], None, 0

    def bind(self, refs):
        self.refs, self.at = refs, 0

    def take(self, shapes):
        if self.refs is None:
            self.shapes += shapes
            return [None] * len(shapes)
        got = self.refs[self.at : self.at + len(shapes)]
        self.at += len(shapes)
        return got


class Sizes:
    def __init__(self, dp_count, rows, group, qkv, dense, up, down):
        self.dp, self.lines, self.rows, self.group = dp_count, dp_count // 2, rows, group
        self.qkv_cols, self.heads = qkv[1], qkv[1] // (3 * HEAD)
        self.width = self.heads * HEAD
        self.split_up = len(up) == 2
        self.hidden = up[-1] // 2 if self.split_up else up[-1]
        self.qkv_rows, self.dense_rows, self.up_rows, self.down_rows = qkv[0], dense[0], up[-2], down[0]
        self.qkv_parts = 2 if qkv[0] % 32 == 0 else 1
        self.dense_whole = dense[0] == self.width
        self.piece = D // (dp_count * TENSOR)
        self.up_piece = 2 * self.hidden // dp_count
        self.qv_piece = 2 * self.width // dp_count


def scratch_of(s, pool):
    take = pool.take
    out = {}
    out["vsum"] = take(VectorExchange.scratch(s.dp, 1, D))
    out["vsum_out"] = take(VectorExchange.scratch(s.dp, s.dp, LANES))
    out["gather_x"] = take(TensorGather.scratch(s.rows))
    out["gather_low"] = take(TensorGather.scratch(s.rows))
    out["scatter_attn"] = take(TensorScatter.scratch(s.rows))
    out["scatter_in"] = take(TensorScatter.scratch(s.rows))
    out["gather_mlp"] = take(PairGather.scratch(s.rows))
    out["gather_og"] = take(PairGather.scratch(s.rows))
    out["scatter_mlp"] = take(PairScatter.scratch(s.rows))
    out["scatter_out"] = take(PairScatter.scratch(s.rows))
    out["w_qkv"] = take(LineGather.scratch(s.dp, (D, s.qkv_cols)))
    out["w_qkv_more"] = take(LineGather.semaphores(s.dp))
    out["w_dense"] = take(LineGather.scratch(s.dp, (s.width, D)))
    out["w_up"] = take(LineGather.scratch(s.dp, (D, s.hidden)))
    out["w_down"] = take(LineGather.scratch(s.dp, (s.hidden, D)))
    out["up_swap"] = take([DMA, DMA])
    out["g_qkv"] = take(LineReduce.scratch(s.dp, True, (D, s.qkv_cols)))
    out["g_dense"] = take(LineReduce.scratch(s.dp, True, (s.width, D)))
    out["g_up"] = take(LineReduce.scratch(s.dp, False, (D, s.hidden)))
    out["g_down"] = take(LineReduce.scratch(s.dp, False, (s.hidden, D)))
    out["g_swap"] = take(
        [
            pltpu.VMEM((2 * s.up_rows, s.hidden), F32),
            pltpu.VMEM((s.up_rows, s.hidden), BF16),
            pltpu.VMEM((s.up_rows, s.hidden), BF16),
            DMA,
            DMA,
        ]
    )
    out["data"] = take(
        [
            pltpu.VMEM((D, s.group), BF16),
            pltpu.VMEM((s.qkv_cols, s.group), BF16),
            pltpu.VMEM((s.heads, s.group, s.group), F32),
            pltpu.VMEM((s.width, s.group), BF16),
            pltpu.VMEM((s.width, s.group), BF16),
            pltpu.VMEM((s.qkv_cols, s.group), BF16),
            pltpu.VMEM((s.group, s.qkv_cols), BF16),
            pltpu.VMEM((2 * s.group, s.hidden), BF16),
            pltpu.VMEM((2 * s.group, s.hidden), F32),
            pltpu.VMEM((2 * s.group, s.hidden), BF16),
            pltpu.VMEM((s.rows, D), F32),
            pltpu.VMEM((s.rows, D), F32),
            pltpu.VMEM((s.rows, D), F32),
            pltpu.VMEM((VECTOR_ROWS, LANES), F32),
            pltpu.VMEM((2, s.up_rows, s.hidden), BF16),
            pltpu.VMEM((s.rows, D), F32),
            pltpu.VMEM((s.rows, D), F32),
        ]
    )
    return out


def loop(count, body):
    def step(i, carry):
        body(i)
        return carry

    lax.fori_loop(0, count, step, 0)


def block_kernel(s, refs_in):
    pool = Refs()
    scratch_of(s, pool)
    names_in, names_out = 8 + VECTOR_ROWS, 7
    (fill_ref, begin_ref, x_ref, og_ref, wq_ref, wd_ref, wu_ref, wn_ref) = refs_in[:8]
    vec_refs = refs_in[8:names_in]
    (block_out, input_grad, qkv_out, dense_out, up_out, down_out, vec_out) = refs_in[
        names_in : names_in + names_out
    ]
    pool.bind(refs_in[names_in + names_out :])
    got = scratch_of(s, pool)
    d, t = place()
    b = d % 2
    rows, group, hidden = s.rows, s.group, s.hidden
    (attn_in_t, qkv_t, probs_t, context_t, context_grad_t, qkv_grad_t, qkv_grad,
     active, slope, pre_grad, live_grad, middle, middle_grad, vec_in, up_halves, mid_normed, mid_up) = got["data"]

    vsum = VectorExchange(s.dp, *got["vsum"])
    vsum_out = VectorExchange(s.dp, *got["vsum_out"])
    attn_in, gx_send, gx_recv = got["gather_x"]
    gather_x = TensorGather(attn_in, gx_send, gx_recv)
    middle_low, gl_send, gl_recv = got["gather_low"]
    gather_low = TensorGather(middle_low, gl_send, gl_recv)
    scatter_attn = TensorScatter(*got["scatter_attn"])
    scatter_in = TensorScatter(*got["scatter_in"])
    mlp_in, gm_send, gm_recv = got["gather_mlp"]
    gather_mlp = PairGather(mlp_in, gm_send, gm_recv)
    out_low, go_send, go_recv = got["gather_og"]
    gather_og = PairGather(out_low, go_send, go_recv)
    scatter_mlp = PairScatter(*got["scatter_mlp"])
    scatter_out = PairScatter(*got["scatter_out"])
    qkv_sems = [got["w_qkv"][1:], got["w_qkv_more"]][: s.qkv_parts]
    w_qkv = [
        LineGather(s.dp, got["w_qkv"][0], True, *sems, part, s.qkv_parts)
        for part, sems in enumerate(qkv_sems)
    ]
    w_dense = LineGather(s.dp, got["w_dense"][0], True, *got["w_dense"][1:])
    w_up = LineGather(s.dp, got["w_up"][0], False, *got["w_up"][1:])
    w_down = LineGather(s.dp, got["w_down"][0], False, *got["w_down"][1:])
    g_qkv = LineReduce(s.dp, True, *got["g_qkv"])
    g_dense = LineReduce(s.dp, True, *got["g_dense"])
    g_up = LineReduce(s.dp, False, *got["g_up"])
    g_down = LineReduce(s.dp, False, *got["g_down"])
    w_dense = [] if s.dense_whole else [w_dense]
    w_up, w_down = [w_up], [w_down]
    halves = up_halves if s.split_up else wu_ref
    up_swap = remote(
        halves.at[1 - b], w_up[0].buf.at[block(d, s.up_rows)], got["up_swap"][0],
        got["up_swap"][1], d + 1 - 2 * b, t,
    )

    enter(s.dp)
    w_qkv[0].place(wq_ref)
    for w in w_dense:
        w.place(wd_ref)
    w_down[0].place(wn_ref)
    if s.split_up:
        for k in range(2 * hidden // LANES):
            up_halves[k % 2, :, (k // 2) * LANES : (k // 2 + 1) * LANES] = wu_ref[
                :, k * LANES : (k + 1) * LANES
            ]
    vec_in[...] = jnp.zeros(vec_in.shape, F32)
    for i, ref in enumerate(vec_refs):
        vec_in[i : i + 1, 0 : ref.shape[1]] = ref[...].astype(F32)
    row = lax.broadcasted_iota(jnp.int32, (VECTOR_ROWS, D), 0)

    def turn(value, first, second, third):
        return jnp.where(
            row < 6,
            pltpu.roll(value, first, 1),
            jnp.where(row == 6, pltpu.roll(value, second, 1), pltpu.roll(value, third, 1)),
        )

    def up_place(device):
        return (device % 2) * hidden + (device // 2) * s.up_piece

    def spread(value, device):
        wide = jnp.concatenate([value, jnp.zeros((VECTOR_ROWS, D - LANES), F32)], axis=1)
        return turn(
            wide, (device * TENSOR + t) * s.piece, up_place(device), device * s.qv_piece
        )

    def back(at):
        return lax.rem(D - at, D)

    entered(s.dp)
    vsum.start(lambda device: vec_in[...])
    for w in w_qkv + w_dense:
        w.start()
    up_swap.start()
    own_row = t * rows + lax.broadcasted_iota(jnp.int32, (rows, D), 0)
    live = og_ref[...] * (own_row < fill_ref[0]).astype(F32)
    live_grad[...] = live
    w_up[0].buf[block(d, s.up_rows)] = halves[b]
    x_normed, x_inverse = normalize(x_ref[...])
    vsum.middle(spread)
    relay_range(w_qkv, 1, 2)
    vec = vsum.finish()
    gather_x.start((x_normed * vec[0:1] + vec[1:2]).astype(BF16))
    relay_range(w_qkv, 2, 3)
    up_swap.wait()
    for w in w_up:
        w.start()
    relay_range(w_dense, 1, 2)
    gather_x.forward()
    relay_range(w_qkv, 3, s.lines)
    gather_og.start(live_grad[...].astype(BF16))
    relay_range(w_dense, 2, 3)
    for w in w_down:
        w.start()
    gather_x.finish()
    attn_in_t[...] = attn_in[...].T
    for w in w_qkv:
        w.finish()

    wq, wd = w_qkv[0].buf, (wd_ref if s.dense_whole else w_dense[0].buf)
    zero_bias = jnp.zeros((1, HEAD), F32)
    pieces = []
    for h in range(s.heads):
        at = 2 * h * HEAD
        pieces += [vec[7:8, at : at + HEAD], zero_bias, vec[7:8, at + HEAD : at + 2 * HEAD]]
    qkv_bias = jnp.concatenate(pieces, axis=1)

    def project(i):
        tile = block(i, 256)
        value = dot_nn(attn_in[tile], wq[...]) + qkv_bias
        qkv_t[:, tile] = value.astype(BF16).T

    loop(group // 256, project)
    relay_range(w_dense, 3, s.lines)

    def part_of(ref, h, which):
        return ref.at[block(3 * h + which, HEAD)]

    def attend(h):
        query = part_of(qkv_t, h, 0)
        key = part_of(qkv_t, h, 1)[...].T
        value = part_of(qkv_t, h, 2)
        head = (t * s.heads + h + 1).astype(F32)
        m = jnp.exp2(jnp.full((1, 256), -8.0 / HEADS, F32) * head)
        for i in range(group // 256):
            n = (i + 1) * 256
            cols = pl.ds(i * 256, 256)
            score = dot_nn(key[:n], query[:, cols]) * (1.0 / math.sqrt(HEAD))
            at_key = lax.broadcasted_iota(jnp.int32, (n, 256), 0)
            at_query = lax.broadcasted_iota(jnp.int32, (n, 256), 1) + i * 256
            score = score + m * (at_key - at_query).astype(F32)
            seen = (at_key >= begin_ref[:, cols]) & (at_key <= at_query)
            score = jnp.where(seen, score, MASKED_SCORE)
            weight = jnp.exp(score - jnp.max(score, axis=0, keepdims=True))
            weight = weight * (1.0 / jnp.sum(weight, axis=0, keepdims=True))
            probs_t[h, 0:n, cols] = weight
            context = dot_nn(value[:, 0:n], weight.astype(BF16))
            context_t[block(h, HEAD), cols] = context.astype(BF16)

    relay_range(w_up, 1, 2)
    loop(s.heads, attend)
    gather_og.forward()
    for w in w_dense:
        w.finish()

    part_attn = scatter_attn.part

    def project_out(i):
        tile = block(i, 256)
        part_attn[tile] = dot_tn(context_t[:, tile], wd[...]).astype(BF16)

    own_half = t // 2
    project_out(1 - own_half)
    for c in scatter_attn.first:
        c.start()
    project_out(own_half)
    for c in scatter_attn.own:
        c.start()
    gather_og.relay()
    relay_range(w_up, 2, 3)
    scatter_attn.middle()
    relay_range(w_down, 1, 2)
    half = rows // 2
    for k in range(2):
        at = pl.ds(k * half, half)
        mid = x_ref[at] + vec[2:3] + scatter_attn.finish_half(k)
        middle[at] = mid
        normed = normalize(mid)[0]
        gather_mlp.start_half(k, (normed * vec[3:4] + vec[4:5]).astype(BF16))
    gather_og.finish()
    gather_mlp.forward()
    relay_range(w_up, 3, s.lines)

    up, down = w_up[0].buf, w_down[0].buf
    up_bias = jnp.where(b == 0, vec[6:7, 0:hidden], vec[6:7, hidden : 2 * hidden])
    cubic, scale = 0.044715, math.sqrt(2.0 / math.pi)

    def forward(i):
        tile = block(i, 256)
        u = dot_nn(mlp_in[tile], up[...]) + up_bias
        square = u * u
        bend = jnp.tanh(scale * (u + cubic * (square * u)))
        active[tile] = (0.5 * u * (1.0 + bend)).astype(BF16)
        slope[tile] = 0.5 * (1.0 + bend) + (0.5 * scale) * u * (1.0 - bend * bend) * (
            1.0 + (3.0 * cubic) * square
        )

    chip = {
        "own": b * 2 + own_half, "x": (1 - b) * 2 + own_half,
        "y": b * 2 + 1 - own_half, "d": (1 - b) * 2 + 1 - own_half,
    }
    gather_mlp.ready("own")
    forward(chip["own"])
    gather_mlp.relay()
    for which in ("x", "y", "d"):
        gather_mlp.ready(which)
        forward(chip[which])
    relay_range(w_down, 2, 3)

    def down_gradient(i):
        cols = block(i, LANES)
        g_down.grad[cols] = dot_tn(active[:, cols], out_low[...]).astype(BF16)

    relay_range(w_down, 3, s.lines)

    def backward(i):
        tile = block(i, 256)
        grad = dot_nt(out_low[tile], down[...]) * slope[tile]
        low = grad.astype(BF16)
        pre_grad[tile] = low
        scatter_mlp.part[tile] = dot_nt(low, up[...]).astype(BF16)

    backward(chip["d"])
    scatter_mlp.first[0].start()
    backward(chip["x"])
    scatter_mlp.first[1].start()
    scatter_mlp.send_diagonal()
    backward(chip["y"])
    scatter_mlp.first[2].start()
    scatter_mlp.send_x()
    backward(chip["own"])
    scatter_mlp.first[3].start()
    scatter_mlp.send_y()
    loop(hidden // LANES, down_gradient)
    g_down.free()

    def up_gradient(i):
        cols = block(i, 256)
        g_up.grad[cols] = dot_tn(mlp_in[:, cols], pre_grad[...]).astype(BF16)

    scatter_mlp.second()
    loop(D // 256, up_gradient)
    g_up.free()

    def forward_out(i):
        tile = block(i, 256)
        scatter_out.part[tile] = dot_nn(active[tile], down[...]).astype(BF16)

    mid_normed[...], mid_inverse = normalize(middle[...])
    for k in range(2):
        at = pl.ds(k * half, half)
        upstream = scatter_mlp.finish_half(k)
        mid_up[at] = upstream
        grad = live_grad[at] + norm_backward(
            upstream, vec[3:4], mid_normed[at], mid_inverse[k * half : (k + 1) * half]
        )
        middle_grad[at] = grad
        gather_low.start_half(k, grad.astype(BF16))
    loop(2 * group // 256, forward_out)
    scatter_out.start()
    gather_low.forward()
    up_bias_grad = column_sum(pre_grad[...].astype(F32))
    sums = put_rows(
        jnp.zeros((VECTOR_ROWS, D), F32),
        [
            (2, column_sum(middle_grad[...])),
            (3, column_sum(mid_up[...] * mid_normed[...])),
            (4, column_sum(mid_up[...])),
            (5, column_sum(live_grad[...])),
        ],
    )
    scatter_out.middle()
    g_down.run()
    gather_low.finish()

    def dense_back(i):
        tile = block(i, 256)
        context_grad_t[:, tile] = dot_nt(wd[...], middle_low[tile]).astype(BF16)

    loop(group // 256, dense_back)
    dense_grad = dot_nn(context_t[...], middle_low[...])
    if s.dense_whole:
        dense_out[...] = dense_grad
    else:
        g_dense.grad[...] = dense_grad.astype(BF16)
        g_dense.start()
    root = 1.0 / math.sqrt(HEAD)

    def attend_back(h):
        at = block(h, HEAD)
        grad_t = context_grad_t[at]
        delta = column_sum(grad_t.astype(F32) * context_t[at].astype(F32))
        query, key = part_of(qkv_t, h, 0)[...], part_of(qkv_t, h, 1)[...]
        value = part_of(qkv_t, h, 2)[...].T
        query_grad, key_grad, value_grad = [], None, None
        for i in range(group // 256):
            n = (i + 1) * 256
            cols = slice(i * 256, n)
            probs = probs_t[h, 0:n, cols]
            score = (probs * (dot_nn(value[:n], grad_t[:, cols]) - delta[:, cols])).astype(BF16)
            query_grad.append(dot_nn(key[:, :n], score))
            key_part = dot_nt(query[:, cols], score)
            value_part = dot_nt(grad_t[:, cols], probs.astype(BF16))
            if i == 0:
                key_grad, value_grad = key_part, value_part
            else:
                wide = lambda v: jnp.concatenate(
                    [v, jnp.zeros((HEAD, n - v.shape[1]), F32)], axis=1
                )
                key_grad, value_grad = wide(key_grad) + key_part, wide(value_grad) + value_part
        part_of(qkv_grad_t, h, 0)[...] = (jnp.concatenate(query_grad, axis=1) * root).astype(BF16)
        part_of(qkv_grad_t, h, 1)[...] = (key_grad * root).astype(BF16)
        part_of(qkv_grad_t, h, 2)[...] = value_grad.astype(BF16)

    loop(s.heads, attend_back)
    scatter_out.second()
    qkv_grad[...] = qkv_grad_t[...].T

    def input_part(i):
        tile = block(i, 256)
        scatter_in.part[tile] = dot_nt(qkv_grad[tile], wq[...]).astype(BF16)

    pair_rows = 2 * s.qkv_rows

    def qkv_gradient(i):
        near = lax.rem(g_qkv.line + s.lines - 1 - i, s.lines)
        far = lax.rem(g_qkv.line + 1 + i, s.lines)
        target = jnp.where(2 * g_qkv.line < s.lines, near, far)
        tile = block(target, pair_rows)
        g_qkv.grad[tile] = dot_nn(attn_in_t[tile], qkv_grad[...]).astype(BF16)
        g_qkv.xcopy(target).start()

    loop(s.lines, qkv_gradient)
    input_part(1 - own_half)
    for c in scatter_in.first:
        c.start()
    input_part(own_half)
    for c in scatter_in.own:
        c.start()
    g_up.run()
    scatter_in.middle()
    if not s.dense_whole:
        g_dense.run()
    qkv_sum = column_sum(qkv_grad[...].astype(F32))
    qv_parts = []
    for h in range(s.heads):
        at = 3 * h * HEAD
        qv_parts += [qkv_sum[:, at : at + HEAD], qkv_sum[:, at + 2 * HEAD : at + 3 * HEAD]]
    qv_parts.append(jnp.zeros((1, D - 2 * s.width), F32))
    qv_grad = jnp.concatenate(qv_parts, axis=1)
    up_grad_row = jnp.concatenate(
        [jnp.where(b == 0, up_bias_grad, 0.0), jnp.where(b == 1, up_bias_grad, 0.0)], axis=1
    )
    x_normed, x_inverse = normalize(x_ref[...])
    upstream = scatter_in.finish()
    sums = put_rows(
        sums,
        [
            (0, column_sum(upstream * x_normed)),
            (1, column_sum(upstream)),
            (6, up_grad_row),
            (7, qv_grad),
        ],
    )
    vsum_out.start(
        lambda device: turn(
            sums, back(device * TENSOR * s.piece), back(up_place(device)),
            back(device * s.qv_piece),
        )[:, :LANES]
    )
    g_qkv.run(0, 1)
    input_grad[...] = middle_grad[...] + norm_backward(upstream, vec[0:1], x_normed, x_inverse)
    g_qkv.run(1, 2)
    vsum_out.middle(lambda value, device: value)
    g_qkv.run(2)

    def keep(ref):
        def put(value):
            ref[...] = value

        def add(value):
            ref[...] += value

        return put, add

    swap_sum, swap_send, swap_recv, ssem, rsem = got["g_swap"]
    g_down.finish(*keep(down_out))
    g_up.finish(*keep(swap_sum))
    swap_send[...] = swap_sum[block(1 - b, s.up_rows)].astype(BF16)
    swap = remote(swap_send, swap_recv, ssem, rsem, d + 1 - 2 * b, t)
    swap.start()

    def put_up(parity, value):
        if s.split_up:
            for k in range(hidden // LANES):
                at = pl.multiple_of((2 * k + parity) * LANES, LANES)
                up_out[:, pl.ds(at, LANES)] = value[:, k * LANES : (k + 1) * LANES]
        else:
            up_out[parity] = value

    put_up(b, swap_sum[block(b, s.up_rows)])
    block_out[...] = middle[...] + scatter_out.finish() + vec[5:6]
    if not s.dense_whole:
        g_dense.finish(*keep(dense_out))
    g_qkv.finish(*keep(qkv_out))
    swap.wait()
    put_up(1 - b, swap_recv[...].astype(F32))
    total = vsum_out.finish()
    turned = pltpu.roll(total, lax.rem(LANES - t * s.piece, LANES), 1)
    vec_out[...] = jnp.where(row[:, :LANES] < 6, turned, total)
    for c in (gather_mlp, scatter_mlp, scatter_attn):
        c.drain()
    for w in w_qkv + w_dense + w_up + w_down:
        w.drain()
    g_down.drain()
    g_up.drain()
    if not s.dense_whole:
        g_dense.drain()
    g_qkv.drain()


def block_call(s, *args):
    shape = jax.ShapeDtypeStruct
    pool = Refs()
    scratch_of(s, pool)
    vmem = pl.BlockSpec(memory_space=pltpu.VMEM)
    smem = pl.BlockSpec(memory_space=pltpu.SMEM)
    dense = (s.width if s.dense_whole else s.dense_rows, D)
    up = (s.up_rows, 2 * s.hidden) if s.split_up else (2, s.up_rows, s.hidden)
    return pl.pallas_call(
        lambda *refs: block_kernel(s, refs),
        out_shape=[
            shape((s.rows, D), F32),
            shape((s.rows, D), F32),
            shape((s.qkv_rows, s.qkv_cols), F32),
            shape(dense, F32),
            shape(up, F32),
            shape((s.down_rows, D), F32),
            shape((VECTOR_ROWS, LANES), F32),
        ],
        in_specs=[smem] + [vmem] * (len(args) - 1),
        out_specs=[vmem] * 7,
        scratch_shapes=pool.shapes,
        compiler_params=pltpu.CompilerParams(
            collective_id=1, has_side_effects=True, vmem_limit_bytes=62 * 1024 * 1024
        ),
        name="block_both_ways",
    )(*args)


def hand_out(arrays, table, pieces):
    n, m = len(arrays), len(pieces)

    total = n + m

    def kernel(*refs):
        sources, targets = refs[: n + 1], refs[n + 1 : n + 1 + total]
        held = refs[n + 1 + total : 2 * n + 2 + total]
        small = refs[2 * n + 2 + total : -2]
        sem_in, sem_out = refs[-2], refs[-1]
        arrive = [
            pltpu.make_async_copy(a, h, sem_in.at[i]) for i, (a, h) in enumerate(zip(sources, held))
        ]
        leave = [
            pltpu.make_async_copy(h, o, sem_out.at[i])
            for i, (h, o) in enumerate(zip(held[:n] + small, targets))
        ]
        arrive[n].start()
        for c in arrive[:n]:
            c.start()
        arrive[n].wait()
        for i in range(m):
            small[i][...] = held[n][i : i + 1, 0 : pieces[i]]
            leave[n + i].start()
        for c, e in zip(arrive[:n], leave):
            c.wait()
            e.start()
        for e in leave:
            e.wait()

    shape = jax.ShapeDtypeStruct
    anywhere = pl.BlockSpec(memory_space=pl.ANY)
    outs = pl.pallas_call(
        kernel,
        out_shape=[shape(a.shape, F32) for a in arrays] + [shape((1, p), F32) for p in pieces],
        in_specs=[anywhere] * (n + 1),
        out_specs=[anywhere] * total,
        scratch_shapes=[pltpu.VMEM(a.shape, F32) for a in arrays]
        + [pltpu.VMEM(table.shape, F32)]
        + [pltpu.VMEM((1, p), F32) for p in pieces]
        + [DMA((n + 1,)), DMA((total,))],
        name="hand_out",
    )(*arrays, table)
    return outs[:n], [o.reshape(-1) for o in outs[n:]]


def per_device(
    dp_count,
    block_input,
    seq_begin,
    group_fill,
    attention_norm_gain,
    attention_norm_bias,
    qkv_weight,
    qv_bias,
    dense_weight,
    dense_bias,
    feedforward_norm_gain,
    feedforward_norm_bias,
    up_weight,
    up_bias,
    down_weight,
    down_bias,
    out_grad,
):
    vectors = [
        attention_norm_gain,
        attention_norm_bias,
        dense_bias,
        feedforward_norm_gain,
        feedforward_norm_bias,
        down_bias,
        up_bias,
        qv_bias,
    ]
    up_rows, up_cols = up_weight.shape
    lines, piece = dp_count // 2, up_bias.shape[0]
    in_place = piece % LANES == 0
    up_split = up_weight
    if not in_place:
        up_split = up_weight.reshape(up_rows, lines, 2, piece).transpose(2, 0, 1, 3)
        up_split = up_split.reshape(2, up_rows, up_cols // 2)
    whole = dense_weight.shape[0] % 16 != 0
    dense = lax.all_gather(dense_weight, "dp", axis=0, tiled=True) if whole else dense_weight
    s = Sizes(
        dp_count, block_input.shape[0], seq_begin.shape[0], qkv_weight.shape, dense.shape,
        up_split.shape, down_weight.shape,
    )
    *arrays, table = block_call(
        s, group_fill, seq_begin[None], block_input, out_grad, qkv_weight, dense, up_split,
        down_weight, *[v[None] for v in vectors],
    )
    arrays, small = hand_out(arrays, table, [v.shape[0] for v in vectors])
    block_out, input_grad, qkv_out, dense_out, up_out, down_out = arrays
    if whole:
        dense_out = lax.psum_scatter(dense_out, "dp", scatter_dimension=0, tiled=True)
    if not in_place:
        up_out = up_out.reshape(2, up_rows, lines, piece).transpose(1, 2, 0, 3)
        up_out = up_out.reshape(up_rows, up_cols)
    return (
        block_out,
        input_grad,
        small[0],
        small[1],
        qkv_out,
        small[7],
        dense_out,
        small[2],
        small[3],
        small[4],
        up_out,
        small[6],
        down_out,
        small[5],
    )


def solution(mesh):
    rows, line = P(("dp", "tensor"), None), P(("dp", "tensor"))
    inner, columns = P(("tensor", "dp")), P("dp", "tensor")
    inner_rows = P(("tensor", "dp"), None)
    return jax.shard_map(
        functools.partial(per_device, mesh.shape["dp"]),
        mesh=mesh,
        in_specs=(
            rows, P("dp"), P("dp"), line, line, columns, inner, inner_rows, line, line, line,
            columns, inner, inner_rows, line, rows,
        ),
        out_specs=(
            rows, rows, line, line, columns, inner, inner_rows, line, line, line, columns, inner,
            inner_rows, line,
        ),
        check_vma=False,
    )
```

```python
import functools
import math

import jax
import jax.numpy as jnp
from jax import lax
from jax.experimental import pallas as pl
from jax.experimental.pallas import tpu as pltpu
from jax.sharding import PartitionSpec as P

D = 1024
HEADS = 16
HEAD = D // HEADS
TENSOR = 4
EPSILON = 1e-05
MASKED_SCORE = -1e30
MESH = pl.DeviceIdType.MESH
VECTOR_ROWS = 8
LANES = 128
BF16 = jnp.bfloat16
F32 = jnp.float32
DMA = pltpu.SemaphoreType.DMA


def dot_nn(a, b):
    return lax.dot_general(a, b, (((1,), (0,)), ((), ())), preferred_element_type=F32)


def dot_nt(a, b):
    return lax.dot_general(a, b, (((1,), (1,)), ((), ())), preferred_element_type=F32)


def dot_tn(a, b):
    return lax.dot_general(a, b, (((0,), (0,)), ((), ())), preferred_element_type=F32)


def normalize(hidden):
    centred = hidden - jnp.mean(hidden, axis=-1, keepdims=True)
    inverse = lax.rsqrt(jnp.mean(centred * centred, axis=-1, keepdims=True) + EPSILON)
    return centred * inverse, inverse


def norm_backward(upstream, gain, normed, inverse):
    scaled = upstream * gain
    return inverse * (
        scaled
        - jnp.mean(scaled, axis=-1, keepdims=True)
        - normed * jnp.mean(scaled * normed, axis=-1, keepdims=True)
    )


def column_sum(value):
    return jnp.sum(value, axis=0, keepdims=True)


def put_rows(base, values):
    row = lax.broadcasted_iota(jnp.int32, base.shape, 0)
    for index, value in values:
        base = jnp.where(row == index, value, base)
    return base


def place():
    return lax.axis_index("dp"), lax.axis_index("tensor")


def tensor_peers(t):
    h, c = t // 2, t % 2
    core = h * 2 + (1 - c)
    across = (1 - h) * 2 + c
    diagonal = (1 - h) * 2 + (1 - c)
    return core, across, diagonal


def block(start, rows):
    return pl.ds(pl.multiple_of(start * rows, rows), rows)


def enter(dp_count):
    d, t = place()
    barrier = pltpu.get_barrier_semaphore()
    for j in range(1, 4):
        pl.semaphore_signal(
            barrier, inc=1, device_id=(d, lax.rem(t + j, 4)), device_id_type=MESH
        )

    def greet(j, carry):
        pl.semaphore_signal(
            barrier, inc=1, device_id=(lax.rem(d + j, dp_count), t), device_id_type=MESH
        )
        return carry

    lax.fori_loop(1, dp_count, greet, 0)


def entered(dp_count):
    pl.semaphore_wait(pltpu.get_barrier_semaphore(), 3 + dp_count - 1)


def remote(src, dst, send, recv, d, t):
    return pltpu.make_async_remote_copy(
        src_ref=src, dst_ref=dst, send_sem=send, recv_sem=recv, device_id=(d, t), device_id_type=MESH
    )


class VectorExchange:
    def __init__(self, dp_count, dout, din, tbuf, dsend, drecv, tsend, trecv):
        self.dp_count = dp_count
        self.dout, self.din, self.tbuf = dout, din, tbuf
        self.dsend, self.drecv, self.tsend, self.trecv = dsend, drecv, tsend, trecv

    @staticmethod
    def scratch(dp_count, outgoing, width):
        return [
            pltpu.VMEM((outgoing, VECTOR_ROWS, LANES), F32),
            pltpu.VMEM((dp_count, VECTOR_ROWS, LANES), F32),
            pltpu.VMEM((4, VECTOR_ROWS, width), F32),
            DMA((dp_count,)),
            DMA((dp_count,)),
            DMA((4,)),
            DMA((4,)),
        ]

    def peer(self, j):
        return lax.rem(place()[0] + j, self.dp_count)

    def source(self, j):
        return lax.rem(place()[0] + self.dp_count - j, self.dp_count)

    def dcopy(self, j):
        out = self.dout.at[j] if self.dout.shape[0] > 1 else self.dout.at[0]
        return remote(
            out, self.din.at[j], self.dsend.at[j], self.drecv.at[j], self.peer(j), place()[1]
        )

    def tcopy(self, j):
        d, t = place()
        return remote(
            self.tbuf.at[0], self.tbuf.at[j], self.tsend.at[j], self.trecv.at[j],
            d, lax.rem(t + j, 4),
        )

    def start(self, block_for):
        def go(j, carry):
            value = block_for(self.peer(j))
            if self.dout.shape[0] > 1:
                self.dout[j] = value
            self.dcopy(j).start()
            return carry

        self.din[0] = block_for(place()[0])
        if self.dout.shape[0] == 1:
            self.dout[0] = block_for(place()[0])
        lax.fori_loop(1, self.dp_count, go, 0)

    def middle(self, spread):
        def wait(j, carry):
            self.dcopy(j).wait()
            return carry

        lax.fori_loop(1, self.dp_count, wait, 0)

        def add(j, total):
            return total + spread(self.din[j], self.source(j))

        self.tbuf[0] = lax.fori_loop(0, self.dp_count, add, jnp.zeros(self.tbuf.shape[1:], F32))
        for j in range(1, 4):
            self.tcopy(j).start()

    def finish(self):
        for j in range(1, 4):
            self.tcopy(j).wait()
        own = self.tbuf[0]
        total = own + self.tbuf[1] + self.tbuf[2] + self.tbuf[3]
        row = lax.broadcasted_iota(jnp.int32, own.shape, 0)
        return jnp.where(row < 6, total, own)


class TensorGather:
    def __init__(self, buf, send, recv):
        self.buf, self.rows = buf, buf.shape[0] // 4
        d, t = place()
        core, across, _ = tensor_peers(t)
        half = self.rows // 2
        at = lambda s, k: buf.at[block(s * 2 + k, half)]
        self.to_across = [
            remote(at(t, k), at(t, k), send.at[k], recv.at[k], d, across) for k in range(2)
        ]
        self.to_core = [
            remote(at(t, k), at(t, k), send.at[2 + k], recv.at[2 + k], d, core) for k in range(2)
        ]
        self.relay = [
            remote(at(across, k), at(across, k), send.at[4 + k], recv.at[4 + k], d, core)
            for k in range(2)
        ]

    @staticmethod
    def scratch(rows):
        return [pltpu.VMEM((4 * rows, D), BF16), DMA((6,)), DMA((6,))]

    def start_half(self, k, value):
        _, t = place()
        self.buf[block(t * 2 + k, self.rows // 2)] = value
        self.to_across[k].start()
        self.to_core[k].start()

    def start(self, value):
        half = self.rows // 2
        for k in range(2):
            self.start_half(k, value[k * half : (k + 1) * half])

    def forward(self):
        for k in range(2):
            self.to_across[k].wait_recv()
            self.relay[k].start()

    def finish(self):
        for c in self.to_across:
            c.wait_send()
        for c in self.to_core + self.relay:
            c.wait()


class TensorScatter:
    def __init__(self, part, near, far, out, send, recv):
        self.part, self.near, self.far, self.out = part, near, far, out
        d, t = place()
        core, across, diagonal = tensor_peers(t)
        self.count = far.shape[0]
        half = self.count // 2
        self.half = half
        p = lambda s, k: part.at[block(s * 2 + k, half)]
        n = lambda s, k: near.at[pl.ds((s * 2 + k) * half, half)]
        r = [pl.ds(k * half, half) for k in range(2)]
        self.rows = r
        self.first = [
            remote(p(diagonal, k), n(1, k), send.at[k], recv.at[k], d, core) for k in range(2)
        ]
        self.own = [
            remote(p(core, k), n(0, k), send.at[2 + k], recv.at[2 + k], d, core) for k in range(2)
        ]
        self.second = [
            remote(out.at[r[k]], far.at[r[k]], send.at[4 + k], recv.at[4 + k], d, across)
            for k in range(2)
        ]

    @staticmethod
    def scratch(rows):
        return [
            pltpu.VMEM((4 * rows, D), BF16),
            pltpu.VMEM((2 * rows, D), BF16),
            pltpu.VMEM((rows, D), BF16),
            pltpu.VMEM((rows, D), BF16),
            DMA((6,)),
            DMA((6,)),
        ]

    def start(self):
        for c in self.first + self.own:
            c.start()

    def middle(self):
        _, t = place()
        _, across, _ = tensor_peers(t)
        for k in range(2):
            self.first[k].wait_recv()
            self.out[self.rows[k]] = (
                self.part[block(across * 2 + k, self.half)].astype(F32)
                + self.near[pl.ds((2 + k) * self.half, self.half)].astype(F32)
            ).astype(BF16)
            self.second[k].start()

    def finish_half(self, k):
        _, t = place()
        self.own[k].wait_recv()
        self.second[k].wait_recv()
        return (
            self.part[block(t * 2 + k, self.half)].astype(F32)
            + self.near[pl.ds(k * self.half, self.half)].astype(F32)
            + self.far[self.rows[k]].astype(F32)
        )

    def drain(self):
        for c in self.first + self.own + self.second:
            c.wait_send()

    def finish(self):
        value = jnp.concatenate([self.finish_half(k) for k in range(2)], axis=0)
        self.drain()
        return value


def pair_peers():
    d, t = place()
    b, h, c = d % 2, t // 2, t % 2
    dx = d + 1 - 2 * b
    slot = lambda bb, hh, cc: bb * 4 + hh * 2 + cc
    return d, t, b, h, c, dx, slot


class PairGather:
    def __init__(self, buf, send, recv):
        self.buf, self.rows = buf, buf.shape[0] // 8
        d, t, b, h, c, dx, slot = pair_peers()
        half = self.rows // 2
        core, across = h * 2 + 1 - c, (1 - h) * 2 + c
        own, sx = slot(b, h, c), slot(1 - b, h, c)
        sy, sd = slot(b, 1 - h, c), slot(1 - b, 1 - h, c)

        def copy(i, s, k, dd, tt):
            ref = buf.at[block(s * 2 + k, half)]
            return remote(ref, ref, send.at[i], recv.at[i], dd, tt)

        self.own = own
        self.to_x = [copy(k, own, k, dx, t) for k in range(2)]
        self.to_y = [copy(2 + k, own, k, d, across) for k in range(2)]
        self.to_core = [copy(4 + k, own, k, d, core) for k in range(2)]
        self.x_to_y = copy(6, sx, 0, d, across)
        self.y_to_x = copy(7, sy, 1, dx, t)
        self.x_core = [copy(8 + k, sx, k, d, core) for k in range(2)]
        self.y_core = [copy(10 + k, sy, k, d, core) for k in range(2)]
        self.d_core = [copy(12 + k, sd, k, d, core) for k in range(2)]

    @staticmethod
    def scratch(rows):
        return [pltpu.VMEM((8 * rows, D), BF16), DMA((14,)), DMA((14,))]

    def start_half(self, k, value):
        self.buf[block(self.own * 2 + k, self.rows // 2)] = value
        order = [self.to_x[k], self.to_y[k]]
        for c in (order if k == 0 else order[::-1]) + [self.to_core[k]]:
            c.start()

    def start(self, value):
        half = self.rows // 2
        for k in range(2):
            self.start_half(k, value[k * half : (k + 1) * half])

    def forward(self):
        self.to_x[0].wait_recv()
        self.x_to_y.start()
        self.to_y[1].wait_recv()
        self.y_to_x.start()
        self.x_core[0].start()
        self.y_core[1].start()

    def relay(self):
        self.to_x[1].wait_recv()
        self.x_core[1].start()
        self.to_y[0].wait_recv()
        self.y_core[0].start()
        self.x_to_y.wait_recv()
        self.d_core[0].start()
        self.y_to_x.wait_recv()
        self.d_core[1].start()

    def ready(self, which):
        for c in {"own": self.to_core, "x": self.x_core, "y": self.y_core, "d": self.d_core}[which]:
            c.wait_recv()

    def drain(self):
        for c in self.to_x + self.to_y + [self.x_to_y, self.y_to_x]:
            c.wait_send()
        for c in self.to_core + self.x_core + self.y_core + self.d_core:
            c.wait_send()

    def finish(self):
        for which in ("own", "x", "y", "d"):
            self.ready(which)
        self.drain()


class PairScatter:
    def __init__(self, part, near, diag, out, far, send, recv):
        self.part, self.near, self.diag, self.out, self.far = part, near, diag, out, far
        d, t, b, h, c, dx, slot = pair_peers()
        rows = part.shape[0] // 8
        half = rows // 2
        self.rows, self.half = rows, half
        core, across = h * 2 + 1 - c, (1 - h) * 2 + c
        where = [(1 - b, 1 - h), (1 - b, h), (b, 1 - h), (b, h)]
        self.mine = [slot(bb, hh, c) for bb, hh in where]
        theirs = [slot(bb, hh, 1 - c) for bb, hh in where]
        self.first = [
            remote(
                part.at[block(theirs[i], rows)], near.at[pl.ds(i * rows, rows)],
                send.at[i], recv.at[i], d, core,
            )
            for i in range(4)
        ]

        def at(ref, i, k):
            return ref.at[pl.ds((i * 2 + k) * half, half)]

        self.diag_x = remote(at(out, 0, 0), at(diag, 0, 0), send.at[4], recv.at[4], dx, t)
        self.diag_y = remote(at(out, 0, 1), at(diag, 0, 1), send.at[5], recv.at[5], d, across)
        self.to_x = [
            remote(at(out, 1, k), at(far, 0, k), send.at[6 + k], recv.at[6 + k], dx, t)
            for k in range(2)
        ]
        self.to_y = [
            remote(at(out, 2, k), at(far, 1, k), send.at[8 + k], recv.at[8 + k], d, across)
            for k in range(2)
        ]

    @staticmethod
    def scratch(rows):
        return [
            pltpu.VMEM((8 * rows, D), BF16),
            pltpu.VMEM((4 * rows, D), BF16),
            pltpu.VMEM((rows, D), BF16),
            pltpu.VMEM((3 * rows, D), BF16),
            pltpu.VMEM((2 * rows, D), BF16),
            DMA((10,)),
            DMA((10,)),
        ]

    def start(self):
        for c in self.first:
            c.start()

    def pair(self, i, k):
        return (
            self.part[block(self.mine[i] * 2 + k, self.half)].astype(F32)
            + self.near[pl.ds((i * 2 + k) * self.half, self.half)].astype(F32)
        )

    def put(self, i, k, value):
        self.out[pl.ds((i * 2 + k) * self.half, self.half)] = value.astype(BF16)

    def send_diagonal(self):
        self.first[0].wait_recv()
        self.put(0, 0, self.pair(0, 0))
        self.diag_x.start()
        self.put(0, 1, self.pair(0, 1))
        self.diag_y.start()

    def send_x(self):
        self.first[1].wait_recv()
        self.put(1, 0, self.pair(1, 0))
        self.to_x[0].start()

    def send_y(self):
        self.first[2].wait_recv()
        self.put(2, 1, self.pair(2, 1))
        self.to_y[1].start()

    def middle(self):
        self.send_diagonal()
        self.send_x()
        self.send_y()

    def second(self):
        half = self.half
        self.diag_x.wait_recv()
        self.put(2, 0, self.pair(2, 0) + self.diag[pl.ds(0, half)].astype(F32))
        self.to_y[0].start()
        self.diag_y.wait_recv()
        self.put(1, 1, self.pair(1, 1) + self.diag[pl.ds(half, half)].astype(F32))
        self.to_x[1].start()

    def finish_half(self, k):
        self.to_x[k].wait_recv()
        self.to_y[k].wait_recv()
        if k == 0:
            self.first[3].wait_recv()
        half = self.half
        return (
            self.pair(3, k)
            + self.far[pl.ds(k * half, half)].astype(F32)
            + self.far[pl.ds((2 + k) * half, half)].astype(F32)
        )

    def drain(self):
        for c in self.first + [self.diag_x, self.diag_y] + self.to_x + self.to_y:
            c.wait_send()

    def finish(self):
        value = jnp.concatenate([self.finish_half(k) for k in range(2)], axis=0)
        self.drain()
        return value


class LineGather:
    def __init__(self, dp_count, buf, with_x, zsend, zrecv, xsend, xrecv, part=0, parts=1):
        self.buf, self.with_x, self.line_count = buf, with_x, dp_count // 2
        self.rows = buf.shape[0] // (dp_count if with_x else dp_count // 2)
        self.part, self.parts = part, parts
        self.zsend, self.zrecv, self.xsend, self.xrecv = zsend, zrecv, xsend, xrecv
        self.d, self.t = place()
        self.line, self.b = self.d // 2, self.d % 2

    @staticmethod
    def semaphores(dp_count):
        n = dp_count // 2
        return [DMA((2, n)), DMA((n,)), DMA((n,)), DMA((n,))]

    @staticmethod
    def scratch(dp_count, shape):
        return [pltpu.VMEM(shape, BF16)] + LineGather.semaphores(dp_count)

    def at(self, blk, b):
        slot = blk * 2 + b if self.with_x else blk
        return self.buf.at[block(slot * self.parts + self.part, self.rows // self.parts)]

    def zcopy(self, way, step, blk):
        ref = self.at(blk, self.b)
        return remote(
            ref, ref, self.zsend.at[way, step], self.zrecv.at[blk],
            (self.line + (1 if way == 0 else -1)) * 2 + self.b, self.t,
        )

    def xcopy(self, blk, b):
        ref = self.at(blk, b)
        return remote(
            ref, ref, self.xsend.at[blk], self.xrecv.at[blk],
            self.line * 2 + (1 - self.b), self.t,
        )

    def more(self, way):
        return (self.line + 1 < self.line_count) if way == 0 else (self.line > 0)

    def place(self, own):
        slot = self.d if self.with_x else self.line
        self.buf[block(slot, self.rows)] = own[...]

    def start(self):
        for way in range(2):

            @pl.when(self.more(way))
            def _():
                self.zcopy(way, 0, self.line).start()

        if self.with_x:
            self.xcopy(self.line, self.b).start()

    def hop(self, step, act, sending=False):
        for way in range(2):
            blk = self.line - step if way == 0 else self.line + step
            valid = (blk >= 0) if way == 0 else (blk < self.line_count)
            if sending:
                valid = valid & self.more(way)

            @pl.when(valid)
            def _():
                act(way, step, blk)

    def relay(self, step):
        def act(way, step, blk):
            self.zcopy(way, step, blk).wait_recv()

            @pl.when(self.more(way))
            def _():
                self.zcopy(way, step, blk).start()

            if self.with_x:
                self.xcopy(blk, self.b).start()

        self.hop(step, act)

    def finish(self):
        if self.with_x:

            def pair(blk, carry):
                self.xcopy(blk, 1 - self.b).wait_recv()
                return carry

            lax.fori_loop(0, self.line_count, pair, 0)

    def drain(self):
        def act(way, step, blk):
            self.zcopy(way, step, blk).wait_send()

        def step(i, carry):
            self.hop(i, act, sending=True)
            if self.with_x:
                self.xcopy(i, self.b).wait_send()
            return carry

        lax.fori_loop(0, self.line_count, step, 0)


def relay_range(items, first, last):
    def body(step, carry):
        for item in items:
            item.relay(step)
        return carry

    if first < last:
        lax.fori_loop(first, last, body, 0)


class LineReduce:
    def __init__(self, dp_count, with_x, grad, below, above, held, xsend, xrecv, zsend, zrecv):
        self.grad, self.below, self.above, self.with_x = grad, below, above, with_x
        self.held = held if with_x else grad
        self.xsend, self.xrecv, self.zsend, self.zrecv = xsend, xrecv, zsend, zrecv
        self.line_count = dp_count // 2
        self.rows = grad.shape[0] // (dp_count if with_x else self.line_count)
        self.d, self.t = place()
        self.line, self.b = self.d // 2, self.d % 2

    @staticmethod
    def scratch(dp_count, with_x, shape):
        n = dp_count // 2
        half = (shape[0] // 2, shape[1]) if with_x else shape
        held = half if with_x else (16, LANES)
        return [
            pltpu.VMEM(shape, BF16), pltpu.VMEM(half, BF16), pltpu.VMEM(half, BF16),
            pltpu.VMEM(held, BF16), DMA((n,)), DMA((n,)), DMA((n,)), DMA((2, n)),
        ]

    def xcopy(self, target):
        return remote(
            self.grad.at[block(target * 2 + (1 - self.b), self.rows)],
            self.held.at[block(target, self.rows)],
            self.xsend.at[target], self.xrecv.at[target],
            self.line * 2 + (1 - self.b), self.t,
        )

    def zcopy(self, way, target):
        dst = self.below if way == 0 else self.above
        return remote(
            self.held.at[block(target, self.rows)], dst.at[block(target, self.rows)],
            self.zsend.at[target], self.zrecv.at[way, target],
            (self.line + (1 if way == 0 else -1)) * 2 + self.b, self.t,
        )

    def each_target(self, act, first=0, stop=None):
        last = self.line_count - 1
        stop = last if stop is None else min(stop, last)

        def step(i, carry):
            @pl.when(last - i > self.line)
            def _():
                act(0, last - i)

            @pl.when(i < self.line)
            def _():
                act(1, i)

            return carry

        if first < stop:
            lax.fori_loop(first, stop, step, 0)

    def start(self):
        if self.with_x:

            def send(way, target):
                self.xcopy(target).start()

            self.each_target(send)
            send(0, self.line)

    def has(self, way):
        return (self.line > 0) if way == 0 else (self.line + 1 < self.line_count)

    def free(self):
        def send(way, target):
            @pl.when(jnp.logical_not(self.has(way)))
            def _():
                self.zcopy(way, target).start()

        self.each_target(send)

    def run(self, first=0, stop=None):
        def reduce(way, target):
            at = block(target, self.rows)
            dst = self.below if way == 0 else self.above
            if self.with_x:
                self.xcopy(target).wait_recv()
                mine = self.grad[block(target * 2 + self.b, self.rows)].astype(F32)

            @pl.when(self.has(way))
            def _():
                self.zcopy(way, target).wait_recv()
                total = self.held[at].astype(F32) + dst[at].astype(F32)
                if self.with_x:
                    total = total + mine
                self.held[at] = total.astype(BF16)
                if not self.with_x:
                    self.zcopy(way, target).start()

            if self.with_x:

                @pl.when(jnp.logical_not(self.has(way)))
                def _():
                    self.held[at] = (mine + self.held[at].astype(F32)).astype(BF16)

                self.zcopy(way, target).start()

        self.each_target(reduce, first, stop)

    def finish(self, put, add):
        at = block(self.line, self.rows)
        if self.with_x:
            self.xcopy(self.line).wait_recv()
            own = self.grad[block(self.d, self.rows)].astype(F32)
            put(own + self.held[at].astype(F32))
        else:
            put(self.grad[at].astype(F32))
        for way in range(2):

            @pl.when(self.has(way))
            def _():
                self.zcopy(way, self.line).wait_recv()
                add((self.below if way == 0 else self.above)[at].astype(F32))

    def drain(self):
        def act(way, target):
            self.zcopy(way, target).wait_send()
            if self.with_x:
                self.xcopy(target).wait_send()

        self.each_target(act)
        if self.with_x:
            self.xcopy(self.line).wait_send()


class Refs:
    def __init__(self):
        self.shapes, self.refs, self.at = [], None, 0

    def bind(self, refs):
        self.refs, self.at = refs, 0

    def take(self, shapes):
        if self.refs is None:
            self.shapes += shapes
            return [None] * len(shapes)
        got = self.refs[self.at : self.at + len(shapes)]
        self.at += len(shapes)
        return got


class Sizes:
    def __init__(self, dp_count, rows, group, qkv, dense, up, down):
        self.dp, self.lines, self.rows, self.group = dp_count, dp_count // 2, rows, group
        self.qkv_cols, self.heads = qkv[1], qkv[1] // (3 * HEAD)
        self.width = self.heads * HEAD
        self.split_up = len(up) == 2
        self.hidden = up[-1] // 2 if self.split_up else up[-1]
        self.qkv_rows, self.dense_rows, self.up_rows, self.down_rows = qkv[0], dense[0], up[-2], down[0]
        self.qkv_parts = 2 if qkv[0] % 32 == 0 else 1
        self.dense_whole = dense[0] == self.width
        self.piece = D // (dp_count * TENSOR)
        self.up_piece = 2 * self.hidden // dp_count
        self.qv_piece = 2 * self.width // dp_count


def scratch_of(s, pool):
    take = pool.take
    out = {}
    out["vsum"] = take(VectorExchange.scratch(s.dp, 1, D))
    out["vsum_out"] = take(VectorExchange.scratch(s.dp, s.dp, LANES))
    out["gather_x"] = take(TensorGather.scratch(s.rows))
    out["gather_low"] = take(TensorGather.scratch(s.rows))
    out["scatter_attn"] = take(TensorScatter.scratch(s.rows))
    out["scatter_in"] = take(TensorScatter.scratch(s.rows))
    out["gather_mlp"] = take(PairGather.scratch(s.rows))
    out["gather_og"] = take(PairGather.scratch(s.rows))
    out["scatter_mlp"] = take(PairScatter.scratch(s.rows))
    out["scatter_out"] = take(PairScatter.scratch(s.rows))
    out["w_qkv"] = take(LineGather.scratch(s.dp, (D, s.qkv_cols)))
    out["w_qkv_more"] = take(LineGather.semaphores(s.dp))
    out["w_dense"] = take(LineGather.scratch(s.dp, (s.width, D)))
    out["w_up"] = take(LineGather.scratch(s.dp, (D, s.hidden)))
    out["w_down"] = take(LineGather.scratch(s.dp, (s.hidden, D)))
    out["up_swap"] = take([DMA, DMA])
    out["g_qkv"] = take(LineReduce.scratch(s.dp, True, (D, s.qkv_cols)))
    out["g_dense"] = take(LineReduce.scratch(s.dp, True, (s.width, D)))
    out["g_up"] = take(LineReduce.scratch(s.dp, False, (D, s.hidden)))
    out["g_down"] = take(LineReduce.scratch(s.dp, False, (s.hidden, D)))
    out["g_swap"] = take(
        [
            pltpu.VMEM((2 * s.up_rows, s.hidden), F32),
            pltpu.VMEM((s.up_rows, s.hidden), BF16),
            pltpu.VMEM((s.up_rows, s.hidden), BF16),
            DMA,
            DMA,
        ]
    )
    out["data"] = take(
        [
            pltpu.VMEM((D, s.group), BF16),
            pltpu.VMEM((s.qkv_cols, s.group), BF16),
            pltpu.VMEM((s.heads, s.group, s.group), F32),
            pltpu.VMEM((s.width, s.group), BF16),
            pltpu.VMEM((s.width, s.group), BF16),
            pltpu.VMEM((s.qkv_cols, s.group), BF16),
            pltpu.VMEM((s.group, s.qkv_cols), BF16),
            pltpu.VMEM((2 * s.group, s.hidden), BF16),
            pltpu.VMEM((2 * s.group, s.hidden), F32),
            pltpu.VMEM((2 * s.group, s.hidden), BF16),
            pltpu.VMEM((s.rows, D), F32),
            pltpu.VMEM((s.rows, D), F32),
            pltpu.VMEM((s.rows, D), F32),
            pltpu.VMEM((VECTOR_ROWS, LANES), F32),
            pltpu.VMEM((2, s.up_rows, s.hidden), BF16),
            pltpu.VMEM((s.rows, D), F32),
            pltpu.VMEM((s.rows, D), F32),
        ]
    )
    return out


def loop(count, body):
    def step(i, carry):
        body(i)
        return carry

    lax.fori_loop(0, count, step, 0)


def block_kernel(s, refs_in):
    pool = Refs()
    scratch_of(s, pool)
    names_in, names_out = 8 + VECTOR_ROWS, 7
    (fill_ref, begin_ref, x_ref, og_ref, wq_ref, wd_ref, wu_ref, wn_ref) = refs_in[:8]
    vec_refs = refs_in[8:names_in]
    (block_out, input_grad, qkv_out, dense_out, up_out, down_out, vec_out) = refs_in[
        names_in : names_in + names_out
    ]
    pool.bind(refs_in[names_in + names_out :])
    got = scratch_of(s, pool)
    d, t = place()
    b = d % 2
    rows, group, hidden = s.rows, s.group, s.hidden
    (attn_in_t, qkv_t, probs_t, context_t, context_grad_t, qkv_grad_t, qkv_grad,
     active, slope, pre_grad, live_grad, middle, middle_grad, vec_in, up_halves, mid_normed, mid_up) = got["data"]

    vsum = VectorExchange(s.dp, *got["vsum"])
    vsum_out = VectorExchange(s.dp, *got["vsum_out"])
    attn_in, gx_send, gx_recv = got["gather_x"]
    gather_x = TensorGather(attn_in, gx_send, gx_recv)
    middle_low, gl_send, gl_recv = got["gather_low"]
    gather_low = TensorGather(middle_low, gl_send, gl_recv)
    scatter_attn = TensorScatter(*got["scatter_attn"])
    scatter_in = TensorScatter(*got["scatter_in"])
    mlp_in, gm_send, gm_recv = got["gather_mlp"]
    gather_mlp = PairGather(mlp_in, gm_send, gm_recv)
    out_low, go_send, go_recv = got["gather_og"]
    gather_og = PairGather(out_low, go_send, go_recv)
    scatter_mlp = PairScatter(*got["scatter_mlp"])
    scatter_out = PairScatter(*got["scatter_out"])
    qkv_sems = [got["w_qkv"][1:], got["w_qkv_more"]][: s.qkv_parts]
    w_qkv = [
        LineGather(s.dp, got["w_qkv"][0], True, *sems, part, s.qkv_parts)
        for part, sems in enumerate(qkv_sems)
    ]
    w_dense = LineGather(s.dp, got["w_dense"][0], True, *got["w_dense"][1:])
    w_up = LineGather(s.dp, got["w_up"][0], False, *got["w_up"][1:])
    w_down = LineGather(s.dp, got["w_down"][0], False, *got["w_down"][1:])
    g_qkv = LineReduce(s.dp, True, *got["g_qkv"])
    g_dense = LineReduce(s.dp, True, *got["g_dense"])
    g_up = LineReduce(s.dp, False, *got["g_up"])
    g_down = LineReduce(s.dp, False, *got["g_down"])
    w_dense = [] if s.dense_whole else [w_dense]
    w_up, w_down = [w_up], [w_down]
    halves = up_halves if s.split_up else wu_ref
    up_swap = remote(
        halves.at[1 - b], w_up[0].buf.at[block(d, s.up_rows)], got["up_swap"][0],
        got["up_swap"][1], d + 1 - 2 * b, t,
    )

    enter(s.dp)
    w_qkv[0].place(wq_ref)
    for w in w_dense:
        w.place(wd_ref)
    w_down[0].place(wn_ref)
    if s.split_up:
        for k in range(2 * hidden // LANES):
            up_halves[k % 2, :, (k // 2) * LANES : (k // 2 + 1) * LANES] = wu_ref[
                :, k * LANES : (k + 1) * LANES
            ]
    vec_in[...] = jnp.zeros(vec_in.shape, F32)
    for i, ref in enumerate(vec_refs):
        vec_in[i : i + 1, 0 : ref.shape[1]] = ref[...].astype(F32)
    row = lax.broadcasted_iota(jnp.int32, (VECTOR_ROWS, D), 0)

    def turn(value, first, second, third):
        return jnp.where(
            row < 6,
            pltpu.roll(value, first, 1),
            jnp.where(row == 6, pltpu.roll(value, second, 1), pltpu.roll(value, third, 1)),
        )

    def up_place(device):
        return (device % 2) * hidden + (device // 2) * s.up_piece

    def spread(value, device):
        wide = jnp.concatenate([value, jnp.zeros((VECTOR_ROWS, D - LANES), F32)], axis=1)
        return turn(
            wide, (device * TENSOR + t) * s.piece, up_place(device), device * s.qv_piece
        )

    def back(at):
        return lax.rem(D - at, D)

    entered(s.dp)
    vsum.start(lambda device: vec_in[...])
    for w in w_qkv + w_dense:
        w.start()
    up_swap.start()
    own_row = t * rows + lax.broadcasted_iota(jnp.int32, (rows, D), 0)
    live = og_ref[...] * (own_row < fill_ref[0]).astype(F32)
    live_grad[...] = live
    w_up[0].buf[block(d, s.up_rows)] = halves[b]
    x_normed, x_inverse = normalize(x_ref[...])
    vsum.middle(spread)
    relay_range(w_qkv, 1, 2)
    vec = vsum.finish()
    gather_x.start((x_normed * vec[0:1] + vec[1:2]).astype(BF16))
    relay_range(w_qkv, 2, 3)
    up_swap.wait()
    for w in w_up:
        w.start()
    relay_range(w_dense, 1, 2)
    gather_x.forward()
    relay_range(w_qkv, 3, s.lines)
    relay_range(w_dense, 2, 3)
    for w in w_down:
        w.start()
    gather_x.finish()
    attn_in_t[...] = attn_in[...].T
    for w in w_qkv:
        w.finish()

    wq, wd = w_qkv[0].buf, (wd_ref if s.dense_whole else w_dense[0].buf)
    zero_bias = jnp.zeros((1, HEAD), F32)
    pieces = []
    for h in range(s.heads):
        at = 2 * h * HEAD
        pieces += [vec[7:8, at : at + HEAD], zero_bias, vec[7:8, at + HEAD : at + 2 * HEAD]]
    qkv_bias = jnp.concatenate(pieces, axis=1)

    def project(i):
        tile = block(i, 256)
        value = dot_nn(attn_in[tile], wq[...]) + qkv_bias
        qkv_t[:, tile] = value.astype(BF16).T

    loop(group // 256, project)
    relay_range(w_dense, 3, s.lines)
    gather_og.start(live_grad[...].astype(BF16))

    def part_of(ref, h, which):
        return ref.at[block(3 * h + which, HEAD)]

    def attend(h):
        query = part_of(qkv_t, h, 0)
        key = part_of(qkv_t, h, 1)[...].T
        value = part_of(qkv_t, h, 2)
        head = (t * s.heads + h + 1).astype(F32)
        m = jnp.exp2(jnp.full((1, 256), -8.0 / HEADS, F32) * head)
        for i in range(group // 256):
            n = (i + 1) * 256
            cols = pl.ds(i * 256, 256)
            score = dot_nn(key[:n], query[:, cols]) * (1.0 / math.sqrt(HEAD))
            at_key = lax.broadcasted_iota(jnp.int32, (n, 256), 0)
            at_query = lax.broadcasted_iota(jnp.int32, (n, 256), 1) + i * 256
            score = score + m * (at_key - at_query).astype(F32)
            seen = (at_key >= begin_ref[:, cols]) & (at_key <= at_query)
            score = jnp.where(seen, score, MASKED_SCORE)
            weight = jnp.exp(score - jnp.max(score, axis=0, keepdims=True))
            weight = weight * (1.0 / jnp.sum(weight, axis=0, keepdims=True))
            probs_t[h, 0:n, cols] = weight
            context = dot_nn(value[:, 0:n], weight.astype(BF16))
            context_t[block(h, HEAD), cols] = context.astype(BF16)

    relay_range(w_up, 1, 2)
    loop(s.heads, attend)
    gather_og.forward()
    for w in w_dense:
        w.finish()

    part_attn = scatter_attn.part

    def project_out(i):
        tile = block(i, 256)
        part_attn[tile] = dot_tn(context_t[:, tile], wd[...]).astype(BF16)

    own_half = t // 2
    project_out(1 - own_half)
    for c in scatter_attn.first:
        c.start()
    project_out(own_half)
    for c in scatter_attn.own:
        c.start()
    gather_og.relay()
    relay_range(w_up, 2, 3)
    scatter_attn.middle()
    relay_range(w_down, 1, 2)
    half = rows // 2
    for k in range(2):
        at = pl.ds(k * half, half)
        mid = x_ref[at] + vec[2:3] + scatter_attn.finish_half(k)
        middle[at] = mid
        normed = normalize(mid)[0]
        gather_mlp.start_half(k, (normed * vec[3:4] + vec[4:5]).astype(BF16))
    gather_og.finish()
    gather_mlp.forward()
    relay_range(w_up, 3, s.lines)

    up, down = w_up[0].buf, w_down[0].buf
    up_bias = jnp.where(b == 0, vec[6:7, 0:hidden], vec[6:7, hidden : 2 * hidden])
    cubic, scale = 0.044715, math.sqrt(2.0 / math.pi)

    def forward(i):
        tile = block(i, 256)
        u = dot_nn(mlp_in[tile], up[...]) + up_bias
        square = u * u
        bend = jnp.tanh(scale * (u + cubic * (square * u)))
        active[tile] = (0.5 * u * (1.0 + bend)).astype(BF16)
        slope[tile] = 0.5 * (1.0 + bend) + (0.5 * scale) * u * (1.0 - bend * bend) * (
            1.0 + (3.0 * cubic) * square
        )

    chip = {
        "own": b * 2 + own_half, "x": (1 - b) * 2 + own_half,
        "y": b * 2 + 1 - own_half, "d": (1 - b) * 2 + 1 - own_half,
    }
    gather_mlp.ready("own")
    forward(chip["own"])
    gather_mlp.relay()
    for which in ("x", "y", "d"):
        gather_mlp.ready(which)
        forward(chip[which])
    relay_range(w_down, 2, 3)

    def down_gradient(i):
        cols = block(i, LANES)
        g_down.grad[cols] = dot_tn(active[:, cols], out_low[...]).astype(BF16)

    relay_range(w_down, 3, s.lines)

    def backward(i):
        tile = block(i, 256)
        grad = dot_nt(out_low[tile], down[...]) * slope[tile]
        low = grad.astype(BF16)
        pre_grad[tile] = low
        scatter_mlp.part[tile] = dot_nt(low, up[...]).astype(BF16)

    backward(chip["d"])
    scatter_mlp.first[0].start()
    backward(chip["x"])
    scatter_mlp.first[1].start()
    scatter_mlp.send_diagonal()
    backward(chip["y"])
    scatter_mlp.first[2].start()
    scatter_mlp.send_x()
    backward(chip["own"])
    scatter_mlp.first[3].start()
    scatter_mlp.send_y()
    loop(hidden // LANES, down_gradient)
    g_down.free()

    def up_gradient(i):
        cols = block(i, 256)
        g_up.grad[cols] = dot_tn(mlp_in[:, cols], pre_grad[...]).astype(BF16)

    scatter_mlp.second()
    loop(D // 256, up_gradient)
    g_up.free()

    def forward_out(i):
        tile = block(i, 256)
        scatter_out.part[tile] = dot_nn(active[tile], down[...]).astype(BF16)

    mid_normed[...], mid_inverse = normalize(middle[...])
    for k in range(2):
        at = pl.ds(k * half, half)
        upstream = scatter_mlp.finish_half(k)
        mid_up[at] = upstream
        grad = live_grad[at] + norm_backward(
            upstream, vec[3:4], mid_normed[at], mid_inverse[k * half : (k + 1) * half]
        )
        middle_grad[at] = grad
        gather_low.start_half(k, grad.astype(BF16))
    loop(2 * group // 256, forward_out)
    scatter_out.start()
    gather_low.forward()
    up_bias_grad = column_sum(pre_grad[...].astype(F32))
    sums = put_rows(
        jnp.zeros((VECTOR_ROWS, D), F32),
        [
            (2, column_sum(middle_grad[...])),
            (3, column_sum(mid_up[...] * mid_normed[...])),
            (4, column_sum(mid_up[...])),
            (5, column_sum(live_grad[...])),
        ],
    )
    scatter_out.middle()
    g_down.run()
    gather_low.finish()

    def dense_back(i):
        tile = block(i, 256)
        context_grad_t[:, tile] = dot_nt(wd[...], middle_low[tile]).astype(BF16)

    loop(group // 256, dense_back)
    dense_grad = dot_nn(context_t[...], middle_low[...])
    if s.dense_whole:
        dense_out[...] = dense_grad
    else:
        g_dense.grad[...] = dense_grad.astype(BF16)
        g_dense.start()
    root = 1.0 / math.sqrt(HEAD)

    def attend_back(h):
        at = block(h, HEAD)
        grad_t = context_grad_t[at]
        delta = column_sum(grad_t.astype(F32) * context_t[at].astype(F32))
        query, key = part_of(qkv_t, h, 0)[...], part_of(qkv_t, h, 1)[...]
        value = part_of(qkv_t, h, 2)[...].T
        query_grad, key_grad, value_grad = [], None, None
        for i in range(group // 256):
            n = (i + 1) * 256
            cols = slice(i * 256, n)
            probs = probs_t[h, 0:n, cols]
            score = (probs * (dot_nn(value[:n], grad_t[:, cols]) - delta[:, cols])).astype(BF16)
            query_grad.append(dot_nn(key[:, :n], score))
            key_part = dot_nt(query[:, cols], score)
            value_part = dot_nt(grad_t[:, cols], probs.astype(BF16))
            if i == 0:
                key_grad, value_grad = key_part, value_part
            else:
                wide = lambda v: jnp.concatenate(
                    [v, jnp.zeros((HEAD, n - v.shape[1]), F32)], axis=1
                )
                key_grad, value_grad = wide(key_grad) + key_part, wide(value_grad) + value_part
        part_of(qkv_grad_t, h, 0)[...] = (jnp.concatenate(query_grad, axis=1) * root).astype(BF16)
        part_of(qkv_grad_t, h, 1)[...] = (key_grad * root).astype(BF16)
        part_of(qkv_grad_t, h, 2)[...] = value_grad.astype(BF16)

    loop(s.heads, attend_back)
    scatter_out.second()
    qkv_grad[...] = qkv_grad_t[...].T

    def input_part(i):
        tile = block(i, 256)
        scatter_in.part[tile] = dot_nt(qkv_grad[tile], wq[...]).astype(BF16)

    pair_rows = 2 * s.qkv_rows

    def qkv_gradient(i):
        near = lax.rem(g_qkv.line + s.lines - 1 - i, s.lines)
        far = lax.rem(g_qkv.line + 1 + i, s.lines)
        target = jnp.where(2 * g_qkv.line < s.lines, near, far)
        tile = block(target, pair_rows)
        g_qkv.grad[tile] = dot_nn(attn_in_t[tile], qkv_grad[...]).astype(BF16)
        g_qkv.xcopy(target).start()

    loop(s.lines, qkv_gradient)
    input_part(1 - own_half)
    for c in scatter_in.first:
        c.start()
    input_part(own_half)
    for c in scatter_in.own:
        c.start()
    g_up.run()
    scatter_in.middle()
    if not s.dense_whole:
        g_dense.run()
    qkv_sum = column_sum(qkv_grad[...].astype(F32))
    qv_parts = []
    for h in range(s.heads):
        at = 3 * h * HEAD
        qv_parts += [qkv_sum[:, at : at + HEAD], qkv_sum[:, at + 2 * HEAD : at + 3 * HEAD]]
    qv_parts.append(jnp.zeros((1, D - 2 * s.width), F32))
    qv_grad = jnp.concatenate(qv_parts, axis=1)
    up_grad_row = jnp.concatenate(
        [jnp.where(b == 0, up_bias_grad, 0.0), jnp.where(b == 1, up_bias_grad, 0.0)], axis=1
    )
    x_normed, x_inverse = normalize(x_ref[...])
    upstream = scatter_in.finish()
    sums = put_rows(
        sums,
        [
            (0, column_sum(upstream * x_normed)),
            (1, column_sum(upstream)),
            (6, up_grad_row),
            (7, qv_grad),
        ],
    )
    vsum_out.start(
        lambda device: turn(
            sums, back(device * TENSOR * s.piece), back(up_place(device)),
            back(device * s.qv_piece),
        )[:, :LANES]
    )
    g_qkv.run(0, 1)
    input_grad[...] = middle_grad[...] + norm_backward(upstream, vec[0:1], x_normed, x_inverse)
    g_qkv.run(1, 2)
    vsum_out.middle(lambda value, device: value)
    g_qkv.run(2)

    def keep(ref):
        def put(value):
            ref[...] = value

        def add(value):
            ref[...] += value

        return put, add

    swap_sum, swap_send, swap_recv, ssem, rsem = got["g_swap"]
    g_down.finish(*keep(down_out))
    g_up.finish(*keep(swap_sum))
    swap_send[...] = swap_sum[block(1 - b, s.up_rows)].astype(BF16)
    swap = remote(swap_send, swap_recv, ssem, rsem, d + 1 - 2 * b, t)
    swap.start()

    def put_up(parity, value):
        if s.split_up:
            for k in range(hidden // LANES):
                at = pl.multiple_of((2 * k + parity) * LANES, LANES)
                up_out[:, pl.ds(at, LANES)] = value[:, k * LANES : (k + 1) * LANES]
        else:
            up_out[parity] = value

    put_up(b, swap_sum[block(b, s.up_rows)])
    block_out[...] = middle[...] + scatter_out.finish() + vec[5:6]
    if not s.dense_whole:
        g_dense.finish(*keep(dense_out))
    g_qkv.finish(*keep(qkv_out))
    swap.wait()
    put_up(1 - b, swap_recv[...].astype(F32))
    total = vsum_out.finish()
    turned = pltpu.roll(total, lax.rem(LANES - t * s.piece, LANES), 1)
    vec_out[...] = jnp.where(row[:, :LANES] < 6, turned, total)
    for c in (gather_mlp, scatter_mlp, scatter_attn):
        c.drain()
    for w in w_qkv + w_dense + w_up + w_down:
        w.drain()
    g_down.drain()
    g_up.drain()
    if not s.dense_whole:
        g_dense.drain()
    g_qkv.drain()


def block_call(s, *args):
    shape = jax.ShapeDtypeStruct
    pool = Refs()
    scratch_of(s, pool)
    vmem = pl.BlockSpec(memory_space=pltpu.VMEM)
    smem = pl.BlockSpec(memory_space=pltpu.SMEM)
    dense = (s.width if s.dense_whole else s.dense_rows, D)
    up = (s.up_rows, 2 * s.hidden) if s.split_up else (2, s.up_rows, s.hidden)
    return pl.pallas_call(
        lambda *refs: block_kernel(s, refs),
        out_shape=[
            shape((s.rows, D), F32),
            shape((s.rows, D), F32),
            shape((s.qkv_rows, s.qkv_cols), F32),
            shape(dense, F32),
            shape(up, F32),
            shape((s.down_rows, D), F32),
            shape((VECTOR_ROWS, LANES), F32),
        ],
        in_specs=[smem] + [vmem] * (len(args) - 1),
        out_specs=[vmem] * 7,
        scratch_shapes=pool.shapes,
        compiler_params=pltpu.CompilerParams(
            collective_id=1, has_side_effects=True, vmem_limit_bytes=62 * 1024 * 1024
        ),
        name="block_both_ways",
    )(*args)


def hand_out(arrays, table, pieces):
    n, m = len(arrays), len(pieces)

    total = n + m

    def kernel(*refs):
        sources, targets = refs[: n + 1], refs[n + 1 : n + 1 + total]
        held = refs[n + 1 + total : 2 * n + 2 + total]
        small = refs[2 * n + 2 + total : -2]
        sem_in, sem_out = refs[-2], refs[-1]
        arrive = [
            pltpu.make_async_copy(a, h, sem_in.at[i]) for i, (a, h) in enumerate(zip(sources, held))
        ]
        leave = [
            pltpu.make_async_copy(h, o, sem_out.at[i])
            for i, (h, o) in enumerate(zip(held[:n] + small, targets))
        ]
        arrive[n].start()
        for c in arrive[:n]:
            c.start()
        arrive[n].wait()
        for i in range(m):
            small[i][...] = held[n][i : i + 1, 0 : pieces[i]]
            leave[n + i].start()
        for c, e in zip(arrive[:n], leave):
            c.wait()
            e.start()
        for e in leave:
            e.wait()

    shape = jax.ShapeDtypeStruct
    anywhere = pl.BlockSpec(memory_space=pl.ANY)
    outs = pl.pallas_call(
        kernel,
        out_shape=[shape(a.shape, F32) for a in arrays] + [shape((1, p), F32) for p in pieces],
        in_specs=[anywhere] * (n + 1),
        out_specs=[anywhere] * total,
        scratch_shapes=[pltpu.VMEM(a.shape, F32) for a in arrays]
        + [pltpu.VMEM(table.shape, F32)]
        + [pltpu.VMEM((1, p), F32) for p in pieces]
        + [DMA((n + 1,)), DMA((total,))],
        name="hand_out",
    )(*arrays, table)
    return outs[:n], [o.reshape(-1) for o in outs[n:]]


def per_device(
    dp_count,
    block_input,
    seq_begin,
    group_fill,
    attention_norm_gain,
    attention_norm_bias,
    qkv_weight,
    qv_bias,
    dense_weight,
    dense_bias,
    feedforward_norm_gain,
    feedforward_norm_bias,
    up_weight,
    up_bias,
    down_weight,
    down_bias,
    out_grad,
):
    vectors = [
        attention_norm_gain,
        attention_norm_bias,
        dense_bias,
        feedforward_norm_gain,
        feedforward_norm_bias,
        down_bias,
        up_bias,
        qv_bias,
    ]
    up_rows, up_cols = up_weight.shape
    lines, piece = dp_count // 2, up_bias.shape[0]
    in_place = piece % LANES == 0
    up_split = up_weight
    if not in_place:
        up_split = up_weight.reshape(up_rows, lines, 2, piece).transpose(2, 0, 1, 3)
        up_split = up_split.reshape(2, up_rows, up_cols // 2)
    whole = dense_weight.shape[0] % 16 != 0
    dense = lax.all_gather(dense_weight, "dp", axis=0, tiled=True) if whole else dense_weight
    s = Sizes(
        dp_count, block_input.shape[0], seq_begin.shape[0], qkv_weight.shape, dense.shape,
        up_split.shape, down_weight.shape,
    )
    *arrays, table = block_call(
        s, group_fill, seq_begin[None], block_input, out_grad, qkv_weight, dense, up_split,
        down_weight, *[v[None] for v in vectors],
    )
    arrays, small = hand_out(arrays, table, [v.shape[0] for v in vectors])
    block_out, input_grad, qkv_out, dense_out, up_out, down_out = arrays
    if whole:
        dense_out = lax.psum_scatter(dense_out, "dp", scatter_dimension=0, tiled=True)
    if not in_place:
        up_out = up_out.reshape(2, up_rows, lines, piece).transpose(1, 2, 0, 3)
        up_out = up_out.reshape(up_rows, up_cols)
    return (
        block_out,
        input_grad,
        small[0],
        small[1],
        qkv_out,
        small[7],
        dense_out,
        small[2],
        small[3],
        small[4],
        up_out,
        small[6],
        down_out,
        small[5],
    )


def solution(mesh):
    rows, line = P(("dp", "tensor"), None), P(("dp", "tensor"))
    inner, columns = P(("tensor", "dp")), P("dp", "tensor")
    inner_rows = P(("tensor", "dp"), None)
    return jax.shard_map(
        functools.partial(per_device, mesh.shape["dp"]),
        mesh=mesh,
        in_specs=(
            rows, P("dp"), P("dp"), line, line, columns, inner, inner_rows, line, line, line,
            columns, inner, inner_rows, line, rows,
        ),
        out_specs=(
            rows, rows, line, line, columns, inner, inner_rows, line, line, line, columns, inner,
            inner_rows, line,
        ),
        check_vma=False,
    )
```
